32 devices in a mesh: beam: 2 (over x), tm: 8 (over z, y), sub: 2 (over core).
Axes of the slice: x: 2, y: 2, z: 4, core: 2. Of those that a mesh axis runs over, the one named last changes fastest.
Arguments:
- channels: bfloat16 [2, 1024, 4096], P(None, ('beam', 'tm'), 'sub'), parts along dimension 1, may hold values from -6 to 6
- synth_taps: float32 [4, 2, 2048], P(None, 'sub'), may hold values from 0.2 to 1
- chirp_phase: float32 [512, 4096], P('tm', 'sub'), may hold values from -3.140625 to 3.140625
Outputs:
- dedispersed: float32 [2, 1024, 2, 2048], P(None, ('beam', 'tm'), 'sub'), parts along dimension 1
The draws below stay inside these ranges and needn't reach their ends.
There are 2 independent parts, one for each index of `beam`. The reference program is written for one: setup_inputs(seed, part) draws one part's arguments, and reference() takes and returns one part's arrays. A program takes and returns all parts, laid end to end along the dimension named above; an argument that names none is the same for every part. Nothing has to cross between parts.
All inputs are finite; a program needn't handle non-finite values.
Results may differ from the reference program's by a relative error of at most 0.0003.
Values may be sent and summed in bfloat16 or wider, within the bound.
No kernel may reach another device: no remote copies, remote signals or barrier semaphores. Data moves between devices by JAX's collectives and lax.ppermute only.
A program may use at most 64 MiB of HBM per device.

```python
import math
import jax
import jax.numpy as jnp

C = 4096
P_SIZE = 4
FRAMES = 512


def steps_of(stream_key, dims, shards, low, high):
    factor_of, own = 1.0, jax.random.fold_in(stream_key, 6)
    for position, blocks in shards:
        draws = jnp.exp(jax.random.uniform(jax.random.fold_in(own, position), (blocks,), jnp.float32, low / len(shards), high / len(shards)))
        factor_of = factor_of * jnp.repeat(draws, dims[position] // blocks).reshape([-1 if axis == position else 1 for axis in range(len(dims))])
    return factor_of


def bell_draw(key, extent, spread, bound, split=(), kind=jnp.bfloat16):
    loudness = steps_of(key, extent, split, -0.22, 0.18) if split else 1.0
    values = jax.random.normal(key, extent, jnp.float32) * spread * loudness
    return jnp.minimum(jnp.maximum(values, -bound), bound).astype(kind)


def setup_inputs(seed: int = 0, part: int = 0) -> dict:
    splits = jax.random.split(jax.random.key(seed), 4)
    part_keys = jax.random.split(jax.random.fold_in(splits[3], part), 4)
    return {
        "channels": bell_draw(part_keys[0], (2, FRAMES, C), 1.0, 6.0, ((1, 8), (2, 2))),
        "synth_taps": jnp.clip(0.2 + 0.8 * jax.random.uniform(splits[1], (P_SIZE, 2, C // 2), jnp.float32) ** steps_of(splits[1], (P_SIZE, 2, C // 2), ((1, 2),), -0.2, 0.2), 0.2, 1.0),
        "chirp_phase": jnp.clip(jax.random.uniform(splits[2], (FRAMES, C), jnp.float32, -3.140625, 3.140625), -3.140625, 3.140625),
    }


def reference(channels, synth_taps, chirp_phase):
    frame_count = channels.shape[1]
    width = channels.shape[2]
    spectrum = channels[0].astype(jnp.float32) + 1j * channels[1].astype(jnp.float32)
    voltage = jnp.fft.ifft(spectrum, axis=1) * math.sqrt(width)
    full_taps = jnp.transpose(synth_taps, (0, 2, 1)).reshape(P_SIZE, width)
    synthesized = full_taps[0] * voltage
    for offset in range(1, P_SIZE):
        delayed = jnp.concatenate([jnp.zeros((offset, width), voltage.dtype), voltage[:frame_count - offset]], axis=0)
        synthesized = synthesized + full_taps[offset] * delayed
    series = synthesized.reshape(-1)
    response = jnp.exp(1j * jnp.transpose(chirp_phase).reshape(-1))
    filtered = jnp.fft.ifft(jnp.fft.fft(series) * response).reshape(frame_count, width // 2, 2)
    filtered = jnp.transpose(filtered, (0, 2, 1))
    return jnp.stack([jnp.real(filtered), jnp.imag(filtered)]).astype(jnp.float32)
```

```python
import math

import jax
import jax.numpy as jnp
import ml_dtypes
import numpy as np
from jax import lax
from jax.experimental import pallas as pl
from jax.experimental.pallas import tpu as pltpu
from jax.sharding import PartitionSpec as P

highest = lax.Precision.HIGHEST
inv_root2 = 1.0 / math.sqrt(2.0)


def partner(x, axis, distance):
    return lax.ppermute(x, axis, [(i, i ^ 1 << distance) for i in range(lax.axis_size(axis))])


def shifted(block, axis, distance):
    devices = range(lax.axis_size(axis))
    route = [(i - distance, i) for i in devices if i - distance in devices]
    return lax.ppermute(block, axis, route)


def roots_table(row_count, col_count, length, direction):
    product = (
        jnp.arange(row_count, dtype=jnp.int32)[:, None]
        * jnp.arange(col_count, dtype=jnp.int32)[None, :]
        % length
    )
    angles = direction * 2.0 * math.pi / length * product.astype(jnp.float32)
    return (jnp.cos(angles), jnp.sin(angles))


def global_roots(left_index, right_index, length, direction):
    product = left_index * right_index % length
    angles = direction * 2.0 * math.pi / length * product.astype(jnp.float32)
    return (jnp.cos(angles), jnp.sin(angles))


def parity_roots(parity_f, half, direction):
    angles = direction * math.pi / half * parity_f * jnp.arange(half, dtype=jnp.float32)
    return (jnp.cos(angles), jnp.sin(angles))


def complex_times(left_re, left_im, right_re, right_im):
    return (left_re * right_re - left_im * right_im, left_re * right_im + left_im * right_re)


def complex_einsum(form, left_re, left_im, right_re, right_im):

    def contract(former, latter):
        return jnp.einsum(form, former, latter, precision=highest)

    return (
        contract(left_re, right_re) - contract(left_im, right_im),
        contract(left_re, right_im) + contract(left_im, right_re),
    )


def dft_last(re_part, im_part, direction):
    length = re_part.shape[-1]
    outer_len = math.gcd(length, 32)
    inner_len = length // outer_len
    leading = re_part.shape[:-1]
    re_part = re_part.reshape(leading + (outer_len, inner_len))
    im_part = im_part.reshape(leading + (outer_len, inner_len))
    table_re, table_im = roots_table(outer_len, outer_len, outer_len, direction)
    re_part, im_part = complex_einsum("...uw,ur->...rw", re_part, im_part, table_re, table_im)
    twist_re, twist_im = roots_table(outer_len, inner_len, length, direction)
    re_part, im_part = complex_times(re_part, im_part, twist_re, twist_im)
    table_re, table_im = roots_table(inner_len, inner_len, inner_len, direction)
    re_part, im_part = complex_einsum("...rw,wt->...tr", re_part, im_part, table_re, table_im)
    factor = 1.0 / math.sqrt(length)
    return (
        re_part.reshape(leading + (length,)) * factor,
        im_part.reshape(leading + (length,)) * factor,
    )


def half_swap(re_part, im_part, sign_own):
    other_re, other_im = partner((re_part, im_part), "sub", 0)
    return (
        (other_re + sign_own * re_part) * inv_root2,
        (other_im + sign_own * im_part) * inv_root2,
    )


def to_columns(re_part, im_part):
    time_count = lax.axis_size("tm")
    time_index = lax.axis_index("tm")
    parity = lax.axis_index("sub")
    half = re_part.shape[1]
    got_re, got_im = (
        lax.all_to_all(re_part.T, "tm", split_axis=0, concat_axis=1, tiled=True),
        lax.all_to_all(im_part.T, "tm", split_axis=0, concat_axis=1, tiled=True),
    )
    col_width = half // time_count
    sample_index = 2 * (time_index * col_width + jnp.arange(col_width, dtype=jnp.int32)) + parity
    return (got_re, got_im, sample_index)


def to_rows(re_part, im_part):
    got_re, got_im = (
        lax.all_to_all(re_part, "tm", split_axis=1, concat_axis=0, tiled=True),
        lax.all_to_all(im_part, "tm", split_axis=1, concat_axis=0, tiled=True),
    )
    return (got_re.T, got_im.T)


def general_body(channels, synth_taps, chirp_phase):
    frames_dev = channels.shape[1]
    half = channels.shape[2]
    tap_count = synth_taps.shape[0]
    time_index = lax.axis_index("tm")
    time_count = lax.axis_size("tm")
    parity = lax.axis_index("sub")
    parity_f = parity.astype(jnp.float32)
    sign_own = 1.0 - 2.0 * parity_f
    total_frames = frames_dev * time_count
    series_len = total_frames * 2 * half
    partner_re, partner_im = partner((channels[0], channels[1]), "sub", 0)
    mixed_re = (
        partner_re.astype(jnp.float32) + sign_own * channels[0].astype(jnp.float32)
    ) * inv_root2
    mixed_im = (
        partner_im.astype(jnp.float32) + sign_own * channels[1].astype(jnp.float32)
    ) * inv_root2
    turn_re, turn_im = parity_roots(parity_f, half, 1.0)
    mixed_re, mixed_im = complex_times(mixed_re, mixed_im, turn_re, turn_im)
    volt_re, volt_im = dft_last(mixed_re, mixed_im, 1.0)
    keep_from = frames_dev - tap_count + 1
    tail_re, tail_im = shifted((volt_re[keep_from:], volt_im[keep_from:]), "tm", 1)
    long_re = jnp.concatenate([tail_re, volt_re], axis=0)
    long_im = jnp.concatenate([tail_im, volt_im], axis=0)
    synth_re = jnp.zeros_like(volt_re)
    synth_im = jnp.zeros_like(volt_im)
    for offset in range(tap_count):
        begin = tap_count - 1 - offset
        synth_re = synth_re + synth_taps[offset, 0] * long_re[begin : begin + frames_dev]
        synth_im = synth_im + synth_taps[offset, 0] * long_im[begin : begin + frames_dev]
    col_re, col_im, sample_index = to_columns(synth_re, synth_im)
    col_re, col_im = dft_last(col_re, col_im, -1.0)
    bin_index = jnp.arange(total_frames, dtype=jnp.int32)
    twist_re, twist_im = global_roots(sample_index[:, None], bin_index[None, :], series_len, -1.0)
    col_re, col_im = complex_times(col_re, col_im, twist_re, twist_im)
    row_re, row_im = to_rows(col_re, col_im)
    row_re, row_im = dft_last(row_re, row_im, -1.0)
    turn_re, turn_im = parity_roots(parity_f, half, -1.0)
    row_re, row_im = complex_times(row_re, row_im, turn_re, turn_im)
    row_re, row_im = half_swap(row_re, row_im, sign_own)
    row_re, row_im = complex_times(row_re, row_im, jnp.cos(chirp_phase), jnp.sin(chirp_phase))
    row_re, row_im = half_swap(row_re, row_im, sign_own)
    turn_re, turn_im = parity_roots(parity_f, half, 1.0)
    row_re, row_im = complex_times(row_re, row_im, turn_re, turn_im)
    row_re, row_im = dft_last(row_re, row_im, 1.0)
    own_bins = time_index * frames_dev + jnp.arange(frames_dev, dtype=jnp.int32)
    own_samples = 2 * jnp.arange(half, dtype=jnp.int32) + parity
    twist_re, twist_im = global_roots(own_bins[:, None], own_samples[None, :], series_len, 1.0)
    row_re, row_im = complex_times(row_re, row_im, twist_re, twist_im)
    col_re, col_im, ignored = to_columns(row_re, row_im)
    col_re, col_im = dft_last(col_re, col_im, 1.0)
    out_re, out_im = to_rows(col_re, col_im)
    return jnp.stack([out_re, out_im])[:, :, None, :]


LANES = 128
CEILING = 224.0
OFFSET = 2.0**-7.75


def expanded(x):
    grown = jnp.abs(x) + OFFSET
    for _ in range(4):
        grown = grown * grown
    return jnp.where(x < 0.0, -grown, grown).astype(jnp.bfloat16)


def restored(code):
    grown = code.astype(jnp.float32)
    size = jnp.abs(grown)
    for _ in range(4):
        size = lax.rsqrt(size)
    size = size - OFFSET
    return jnp.where(grown < 0.0, -size, size)


def times_root(pair, numerator, length):
    re, im = pair
    eighth = numerator * 8 % (8 * length)
    if eighth == 0:
        return re, im
    if eighth == 4 * length:
        return -re, -im
    if eighth == 2 * length:
        return -im, re
    if eighth == 6 * length:
        return im, -re
    angle = 2.0 * math.pi * numerator / length
    c, s = math.cos(angle), math.sin(angle)
    if eighth % (2 * length) == length:
        root = abs(c)
        if c * s > 0:
            plus, minus = (re - im) * root, (re + im) * root
            return (plus, minus) if c > 0 else (-plus, -minus)
        plus, minus = (re + im) * root, (im - re) * root
        return (plus, minus) if c > 0 else (-plus, -minus)
    return re * c - im * s, re * s + im * c


def fft_list(values, direction):
    count = len(values)
    if count == 1:
        return values
    even = fft_list(values[0::2], direction)
    odd = fft_list(values[1::2], direction)
    low, high = [], []
    for k in range(count // 2):
        t_re, t_im = times_root(odd[k], direction * k % count, count)
        e_re, e_im = even[k]
        low.append((e_re + t_re, e_im + t_im))
        high.append((e_re - t_re, e_im - t_im))
    return low + high


def split_parts(x):
    high = x.astype(jnp.bfloat16)
    return high, (x - high.astype(jnp.float32)).astype(jnp.bfloat16)


def np_split(table):
    high = table.astype(ml_dtypes.bfloat16)
    low = (table - high.astype(np.float64)).astype(ml_dtypes.bfloat16)
    return high, low


def real_form(table):
    return np.stack(
        [np.stack([table.real, -table.imag], -1), np.stack([table.imag, table.real], -1)], -2
    )


def frame_tables(time_count, fd, groups, forward):
    frames = time_count * fd
    per = fd // groups
    g = np.arange(fd)
    tables = []
    for p in range(time_count // 2):
        kd = 2 * p + np.arange(2)
        k1 = kd[:, None] + time_count * np.arange(fd)[None, :]
        sign = -1.0 if forward else 1.0
        phase = np.exp(sign * 2j * np.pi * (k1[:, :, None] * g % frames) / frames)
        form = real_form(phase / math.sqrt(frames))
        full = np.zeros((groups, 2, 2, per, 2, 2, fd))
        for j in range(2):
            block = form[j].reshape(groups, per, fd, 2, 2)
            if forward:
                full[:, :, j, :, j, :, :] = block.transpose(0, 3, 1, 4, 2)
            else:
                full[:, :, j, :, j, :, :] = block.transpose(0, 4, 1, 3, 2)
        size = 4 * fd
        full = full.reshape(size, size)
        if not forward:
            full = full.T
        tables.append(np.concatenate(np_split(full), axis=1))
    return np.stack(tables)


def lane_table(width, direction):
    index = np.arange(LANES)
    roots = np.exp(direction * 2j * np.pi * np.outer(index, index) / LANES) / math.sqrt(width)
    form = real_form(roots)
    table = form.transpose(3, 0, 2, 1).reshape(2 * LANES, 2 * LANES)
    return np.concatenate(np_split(table), axis=0)


def twist_table(width):
    blocks = width // LANES
    phase = 2.0 * np.pi * np.outer(np.arange(blocks), np.arange(LANES)) / width
    return np.stack([np.cos(phase), np.sin(phase)], 1).astype(np.float32)


def dot32(a, b):
    return jnp.dot(a, b, preferred_element_type=jnp.float32)


def left_product(table, high, low):
    return dot32(table, jnp.concatenate([high, high], axis=0)) + dot32(
        table[:, : high.shape[0]], low
    )


def right_product(x, table):
    high, low = split_parts(x)
    return dot32(jnp.concatenate([high, high], axis=1), table) + dot32(low, table[: x.shape[1]])


def frames_kernel(x_ref, table_ref, out_ref, high_ref, low_ref):
    time_count, _, fd, width = x_ref.shape
    groups = out_ref.shape[0]
    halves = width // LANES
    pairs = time_count // 2
    tails = 3
    power = jnp.zeros((16, LANES), jnp.float32)
    for g in range(0, fd, 16):
        for h in range(halves):
            lanes = slice(h * LANES, (h + 1) * LANES)
            values = []
            for d in range(time_count):
                re = x_ref[d, 0, g : g + 16, lanes].astype(jnp.float32)
                im = x_ref[d, 1, g : g + 16, lanes].astype(jnp.float32)
                power = power + (re * re + im * im)
                values.append((re, im))
            for kd, pair in enumerate(fft_list(values, -1)):
                for r in range(2):
                    high, low = split_parts(pair[r])
                    high_ref[kd, r, g : g + 16, lanes] = high
                    low_ref[kd, r, g : g + 16, lanes] = low
    energy = jnp.sum(jnp.sum(power, axis=0, keepdims=True), axis=1, keepdims=True)
    scale = CEILING * lax.rsqrt(jnp.maximum(energy, 1e-30))
    scale = scale.astype(jnp.bfloat16).astype(jnp.float32)
    rows = []
    for h in range(halves):
        lanes = slice(h * LANES, (h + 1) * LANES)
        for r in range(2):
            last = x_ref[time_count - 1, r, fd - 16 :, lanes].astype(jnp.float32)
            rows.append(last[16 - tails :])
            rows.append(jnp.broadcast_to(scale, (1, LANES)))
    tail = jnp.concatenate(rows, axis=0).astype(jnp.bfloat16)
    for dest in range(groups):
        out_ref[dest, halves * pairs] = tail
    for p in range(pairs):
        high = high_ref[2 * p : 2 * p + 2].reshape(4 * fd, width)
        low = low_ref[2 * p : 2 * p + 2].reshape(4 * fd, width)
        code = expanded(left_product(table_ref[p], high, low) * scale)
        for dest in range(groups):
            for h in range(halves):
                out_ref[dest, h * pairs + p] = code[
                    dest * 16 : dest * 16 + 16, h * LANES : (h + 1) * LANES
                ]


def rows_kernel(
    x_ref, cos_ref, sin_ref, taps_ref, row_ref, twist_ref, inverse_ref, forward_ref,
    out_ref, scale_ref, buf, wrap,
):
    groups, slots = x_ref.shape[0], x_ref.shape[1]
    blocks = twist_ref.shape[0]
    halves = blocks // groups
    pairs = (slots - 1) // halves
    lanes = LANES
    unitary = 1.0 / math.sqrt(groups * row_ref.shape[1])

    def block_of(source, h):
        return (source % 2) * (blocks // 2) + (source // 2) * halves + h

    def twist(n1, pair, direction):
        c, s = twist_ref[n1, 0:1, :], twist_ref[n1, 1:2, :]
        if direction < 0:
            s = -s
        return complex_times(pair[0], pair[1], c, s)

    def put(n1, pair):
        buf[n1 * 8 : n1 * 8 + 8, :lanes] = pair[0]
        buf[n1 * 8 : n1 * 8 + 8, lanes:] = pair[1]

    def take(n1):
        return buf[n1 * 8 : n1 * 8 + 8, :lanes], buf[n1 * 8 : n1 * 8 + 8, lanes:]

    def to_samples(values):
        for n1, pair in enumerate(fft_list(values, 1)):
            put(n1, twist(n1, pair, 1))
        buf[...] = right_product(buf[...], inverse_ref[...])

    energy = jnp.zeros((1, lanes), jnp.float32)
    steps = []
    for source in range(groups):
        step = 1.0 / x_ref[source, halves * pairs].astype(jnp.float32)[3:4]
        steps.append(step)
        reach = CEILING * step
        energy = energy + reach * reach
    gain = jnp.max(jnp.sum(taps_ref[...], axis=1), axis=0, keepdims=True)
    gain = jnp.max(gain, axis=1, keepdims=True)
    scale = CEILING * lax.rsqrt(energy) / gain
    scale_ref[...] = jnp.broadcast_to(scale, scale_ref.shape)

    values = [None] * blocks
    for source in range(groups):
        tile = x_ref[source, halves * pairs].astype(jnp.float32) * unitary
        for h in range(halves):
            part = tile[h * 8 : h * 8 + 8]
            values[block_of(source, h)] = (part, jnp.concatenate([part[4:], part[:4]], axis=0))
    to_samples(values)
    for n1 in range(blocks):
        parts = take(n1)
        t1, t2, t3 = [taps_ref[n1, q : q + 1, :] for q in range(1, 4)]
        rows = []
        for part in parts:
            v0, v1, v2 = part[0:1], part[1:2], part[2:3]
            rows += [t1 * v2 + t2 * v1 + t3 * v0, t2 * v2 + t3 * v1, t3 * v2, v0]
        wrap[n1] = jnp.concatenate(rows, axis=0)

    def one_pair(p, carry):
        first = pl.multiple_of(p * 8, 8)

        def row_table(index):
            return row_ref[2 * index, pl.ds(first, 8), :], row_ref[2 * index + 1, pl.ds(first, 8), :]

        values = [None] * blocks
        for source in range(groups):
            for h in range(halves):
                tile = restored(x_ref[source, h * pairs + p]) * steps[source]
                values[block_of(source, h)] = (tile[:8], tile[8:])
        to_samples(values)
        w1, w2, w3 = row_table(0), row_table(1), row_table(2)
        unit = row_table(3)
        turn = row_table(4)
        for n1 in range(blocks):
            re, im = take(n1)
            t = [taps_ref[n1, q : q + 1, :] for q in range(4)]
            gain_re = t[0] + w1[0] * t[1] + w2[0] * t[2] + w3[0] * t[3]
            gain_im = w1[1] * t[1] + w2[1] * t[2] + w3[1] * t[3]
            u = [wrap[n1, q : q + 1, :] for q in range(7)]
            back_re = u[0] + (w1[0] * u[1] - w1[1] * u[5]) + (w2[0] * u[2] - w2[1] * u[6])
            back_im = u[4] + (w1[0] * u[5] + w1[1] * u[1]) + (w2[0] * u[6] + w2[1] * u[2])
            re, im = complex_times(re, im, gain_re, gain_im)
            put(n1, complex_times(re - back_re, im - back_im, *turn))
            turn = complex_times(*turn, *unit)
        buf[...] = right_product(buf[...], forward_ref[...])
        values = [twist(n1, take(n1), -1) for n1 in range(blocks)]
        bins = []
        for k, pair in enumerate(fft_list(values, -1)):
            c = cos_ref[pl.ds(first, 8), k * lanes : (k + 1) * lanes]
            s = sin_ref[pl.ds(first, 8), k * lanes : (k + 1) * lanes]
            bins.append(complex_times(*pair, c, s))
        to_samples(bins)
        turn = row_table(4)
        turn = turn[0] * scale, turn[1] * scale
        for n1 in range(blocks):
            re, im = take(n1)
            back = re * turn[0] + im * turn[1], im * turn[0] - re * turn[1]
            dest = n1 // 2 % (groups // 2) * 2 + n1 % 2
            h = n1 // groups
            out_ref[dest, h * pairs + p] = expanded(jnp.concatenate(back, axis=0))
            turn = complex_times(*turn, *unit)
        return carry

    lax.fori_loop(0, pairs, one_pair, 0)


def columns_kernel(x_ref, table_ref, out_ref, high_ref, low_ref, mid_ref):
    groups, slots = x_ref.shape[0], x_ref.shape[1]
    time_count, halves, _, fd, _ = out_ref.shape
    pairs = slots // halves
    width = halves * LANES
    for p in range(pairs):
        for source in range(groups):
            for h in range(halves):
                high, low = split_parts(restored(x_ref[source, h * pairs + p]))
                rows = slice(source * 16, source * 16 + 16)
                cols = slice(h * LANES, (h + 1) * LANES)
                high_ref[rows, cols] = high
                low_ref[rows, cols] = low
        mid_ref[2 * p : 2 * p + 2] = left_product(
            table_ref[p], high_ref[...], low_ref[...]
        ).reshape(2, 2 * fd, width)
    for g in range(0, fd, 16):
        for h in range(halves):
            cols = slice(h * LANES, (h + 1) * LANES)
            values = [
                (mid_ref[kd, g : g + 16, cols], mid_ref[kd, fd + g : fd + g + 16, cols])
                for kd in range(time_count)
            ]
            for d, pair in enumerate(fft_list(values, 1)):
                for r in range(2):
                    out_ref[d, h, r, g : g + 16, :] = expanded(pair[r])


def output_kernel(x_ref, scale_ref, out_ref, mixed):
    time_count, halves, _, fd, _ = x_ref.shape
    lots = time_count * halves
    step = 1.0 / scale_ref[0:1, :]
    for h in range(halves):
        for e in range(time_count):
            tile = restored(x_ref[e, h].reshape(2 * fd, LANES)) * step
            mixed[pl.ds(e + time_count * h, LANES, stride=lots), :] = tile.T
    for block in range(lots):
        tile = mixed[block * LANES : (block + 1) * LANES, :].T
        for r in range(2):
            out_ref[r, :, block * LANES : (block + 1) * LANES] = tile[r * fd : (r + 1) * fd]


def call(kernel, outs, scratch, *args):
    return pl.pallas_call(
        kernel,
        out_shape=outs,
        in_specs=[pl.BlockSpec(memory_space=pltpu.VMEM)] * len(args),
        out_specs=jax.tree.map(lambda _: pl.BlockSpec(memory_space=pltpu.VMEM), outs),
        scratch_shapes=scratch,
    )(*args)


def swap_all(x, axes):
    return lax.all_to_all(x, axes, split_axis=0, concat_axis=0, tiled=True)


def row_tables(k1, frames, width):
    series_len = frames * width
    shifts = [1 * k1 % frames, 2 * k1 % frames, 3 * k1 % frames]
    parts = [jnp.broadcast_to(s[:, None] * width, (k1.shape[0], LANES)) for s in shifts]
    parts.append(jnp.broadcast_to(k1[:, None], (k1.shape[0], LANES)))
    blocks = width // LANES
    parts.append(k1[:, None] * (blocks * jnp.arange(LANES, dtype=jnp.int32))[None, :] % series_len)
    angles = jnp.stack(parts).astype(jnp.float32) * (-2.0 * math.pi / series_len)
    return jnp.stack([jnp.cos(angles), jnp.sin(angles)], 1).reshape(10, k1.shape[0], LANES)


def fast_body(channels, synth_taps, chirp_phase):
    _, fd, half = channels.shape
    time_count = lax.axis_size("tm")
    subs = lax.axis_size("sub")
    groups = time_count * subs
    width = half * subs
    frames = fd * time_count
    col_width = half // time_count
    halves = col_width // LANES
    pairs = time_count // 2
    blocks = width // LANES
    per = fd // groups
    own = fd // subs
    time_index = lax.axis_index("tm")
    parity = lax.axis_index("sub")
    f32, bf16 = jnp.float32, jnp.bfloat16
    shape = jax.ShapeDtypeStruct

    sent = channels.reshape(2, fd, time_count, col_width).transpose(2, 0, 1, 3)
    got = swap_all(sent, "tm")

    mine = lax.dynamic_slice_in_dim(chirp_phase, parity * own, own, 0)
    theirs = lax.dynamic_slice_in_dim(chirp_phase, (1 - parity) * own, own, 0)
    theirs = partner(theirs, "sub", 0)
    other_taps = partner(synth_taps[:, 0], "sub", 0)

    def both(a, b):
        return jnp.where(parity == 0, a, b), jnp.where(parity == 0, b, a)

    phase = jnp.concatenate(both(mine, theirs), axis=1)
    phase = phase.reshape(per, pairs, 2, width).transpose(1, 2, 0, 3).reshape(own, width)
    cos_part, sin_part = jnp.cos(phase), jnp.sin(phase)
    taps = jnp.stack(both(synth_taps[:, 0], other_taps), axis=-1)
    taps = taps.reshape(-1, LANES, blocks).transpose(2, 0, 1)
    row = jnp.arange(own, dtype=jnp.int32)
    k1 = row // per % 2 + 2 * (row // (2 * per))
    k1 = k1 + time_count * (time_index * (fd // time_count) + parity * per + row % per)
    rows = row_tables(k1, frames, width)

    slots = halves * pairs + 1
    coded = call(
        frames_kernel,
        shape((groups, slots, 16, LANES), bf16),
        [pltpu.VMEM((time_count, 2, fd, col_width), bf16)] * 2,
        got,
        jnp.asarray(frame_tables(time_count, fd, groups, True)),
    )
    coded = swap_all(coded, ("tm", "sub"))
    coded, scale = call(
        rows_kernel,
        (shape((groups, slots - 1, 16, LANES), bf16), shape((8, LANES), f32)),
        [pltpu.VMEM((blocks * 8, 2 * LANES), f32), pltpu.VMEM((blocks, 8, LANES), f32)],
        coded,
        cos_part,
        sin_part,
        taps,
        rows,
        jnp.asarray(twist_table(width)),
        jnp.asarray(lane_table(width, 1)),
        jnp.asarray(lane_table(width, -1)),
    )
    coded = swap_all(coded, ("tm", "sub"))
    coded = call(
        columns_kernel,
        shape((time_count, halves, 2, fd, LANES), bf16),
        [pltpu.VMEM((4 * fd, col_width), bf16)] * 2
        + [pltpu.VMEM((time_count, 2 * fd, col_width), f32)],
        coded,
        jnp.asarray(frame_tables(time_count, fd, groups, False)),
    )
    coded = swap_all(coded, "tm")
    out = call(
        output_kernel,
        shape((2, fd, half), f32),
        [pltpu.VMEM((half, LANES), f32)],
        coded,
        scale,
    )
    return out[:, :, None, :]


def body(channels, synth_taps, chirp_phase):
    _, fd, half = channels.shape
    time_count, subs = lax.axis_size("tm"), lax.axis_size("sub")
    groups = time_count * subs
    fits = (
        subs == 2
        and synth_taps.shape[0] == 4
        and half == time_count * 2 * LANES
        and fd == 4 * groups
        and time_count % 2 == 0
        and half == groups * LANES
        and 2 * fd == LANES
    )
    return (fast_body if fits else general_body)(channels, synth_taps, chirp_phase)


def solution(mesh):
    placed = (P(None, ("beam", "tm"), "sub"), P(None, "sub", None), P("tm", "sub"))
    return jax.shard_map(
        body,
        mesh=mesh,
        in_specs=placed,
        out_specs=P(None, ("beam", "tm"), "sub", None),
        check_vma=False,
    )
```

```python
import functools
import math

import jax
import jax.numpy as jnp
import ml_dtypes
import numpy as np
from jax import lax
from jax.experimental import pallas as pl
from jax.experimental.pallas import tpu as pltpu
from jax.sharding import PartitionSpec as P


highest = lax.Precision.HIGHEST
inv_root2 = 1.0 / math.sqrt(2.0)


def partner(x, axis, distance):
    return lax.ppermute(x, axis, [(i, i ^ 1 << distance) for i in range(lax.axis_size(axis))])


def shifted(block, axis, distance):
    devices = range(lax.axis_size(axis))
    route = [(i - distance, i) for i in devices if i - distance in devices]
    return lax.ppermute(block, axis, route)


def roots_table(row_count, col_count, length, direction):
    product = (
        jnp.arange(row_count, dtype=jnp.int32)[:, None]
        * jnp.arange(col_count, dtype=jnp.int32)[None, :]
        % length
    )
    angles = direction * 2.0 * math.pi / length * product.astype(jnp.float32)
    return (jnp.cos(angles), jnp.sin(angles))


def global_roots(left_index, right_index, length, direction):
    product = left_index * right_index % length
    angles = direction * 2.0 * math.pi / length * product.astype(jnp.float32)
    return (jnp.cos(angles), jnp.sin(angles))


def parity_roots(parity_f, half, direction):
    angles = direction * math.pi / half * parity_f * jnp.arange(half, dtype=jnp.float32)
    return (jnp.cos(angles), jnp.sin(angles))


def complex_times(left_re, left_im, right_re, right_im):
    return (left_re * right_re - left_im * right_im, left_re * right_im + left_im * right_re)


def complex_einsum(form, left_re, left_im, right_re, right_im):

    def contract(former, latter):
        return jnp.einsum(form, former, latter, precision=highest)

    return (
        contract(left_re, right_re) - contract(left_im, right_im),
        contract(left_re, right_im) + contract(left_im, right_re),
    )


def dft_last(re_part, im_part, direction):
    length = re_part.shape[-1]
    outer_len = math.gcd(length, 32)
    inner_len = length // outer_len
    leading = re_part.shape[:-1]
    re_part = re_part.reshape(leading + (outer_len, inner_len))
    im_part = im_part.reshape(leading + (outer_len, inner_len))
    table_re, table_im = roots_table(outer_len, outer_len, outer_len, direction)
    re_part, im_part = complex_einsum("...uw,ur->...rw", re_part, im_part, table_re, table_im)
    twist_re, twist_im = roots_table(outer_len, inner_len, length, direction)
    re_part, im_part = complex_times(re_part, im_part, twist_re, twist_im)
    table_re, table_im = roots_table(inner_len, inner_len, inner_len, direction)
    re_part, im_part = complex_einsum("...rw,wt->...tr", re_part, im_part, table_re, table_im)
    factor = 1.0 / math.sqrt(length)
    return (
        re_part.reshape(leading + (length,)) * factor,
        im_part.reshape(leading + (length,)) * factor,
    )


def half_swap(re_part, im_part, sign_own):
    other_re, other_im = partner((re_part, im_part), "sub", 0)
    return (
        (other_re + sign_own * re_part) * inv_root2,
        (other_im + sign_own * im_part) * inv_root2,
    )


def to_columns(re_part, im_part):
    time_count = lax.axis_size("tm")
    time_index = lax.axis_index("tm")
    parity = lax.axis_index("sub")
    half = re_part.shape[1]
    got_re, got_im = (
        lax.all_to_all(re_part.T, "tm", split_axis=0, concat_axis=1, tiled=True),
        lax.all_to_all(im_part.T, "tm", split_axis=0, concat_axis=1, tiled=True),
    )
    col_width = half // time_count
    sample_index = 2 * (time_index * col_width + jnp.arange(col_width, dtype=jnp.int32)) + parity
    return (got_re, got_im, sample_index)


def to_rows(re_part, im_part):
    got_re, got_im = (
        lax.all_to_all(re_part, "tm", split_axis=1, concat_axis=0, tiled=True),
        lax.all_to_all(im_part, "tm", split_axis=1, concat_axis=0, tiled=True),
    )
    return (got_re.T, got_im.T)


def general_body(channels, synth_taps, chirp_phase):
    frames_dev = channels.shape[1]
    half = channels.shape[2]
    tap_count = synth_taps.shape[0]
    time_index = lax.axis_index("tm")
    time_count = lax.axis_size("tm")
    parity = lax.axis_index("sub")
    parity_f = parity.astype(jnp.float32)
    sign_own = 1.0 - 2.0 * parity_f
    total_frames = frames_dev * time_count
    series_len = total_frames * 2 * half
    partner_re, partner_im = partner((channels[0], channels[1]), "sub", 0)
    mixed_re = (
        partner_re.astype(jnp.float32) + sign_own * channels[0].astype(jnp.float32)
    ) * inv_root2
    mixed_im = (
        partner_im.astype(jnp.float32) + sign_own * channels[1].astype(jnp.float32)
    ) * inv_root2
    turn_re, turn_im = parity_roots(parity_f, half, 1.0)
    mixed_re, mixed_im = complex_times(mixed_re, mixed_im, turn_re, turn_im)
    volt_re, volt_im = dft_last(mixed_re, mixed_im, 1.0)
    keep_from = frames_dev - tap_count + 1
    tail_re, tail_im = shifted((volt_re[keep_from:], volt_im[keep_from:]), "tm", 1)
    long_re = jnp.concatenate([tail_re, volt_re], axis=0)
    long_im = jnp.concatenate([tail_im, volt_im], axis=0)
    synth_re = jnp.zeros_like(volt_re)
    synth_im = jnp.zeros_like(volt_im)
    for offset in range(tap_count):
        begin = tap_count - 1 - offset
        synth_re = synth_re + synth_taps[offset, 0] * long_re[begin : begin + frames_dev]
        synth_im = synth_im + synth_taps[offset, 0] * long_im[begin : begin + frames_dev]
    col_re, col_im, sample_index = to_columns(synth_re, synth_im)
    col_re, col_im = dft_last(col_re, col_im, -1.0)
    bin_index = jnp.arange(total_frames, dtype=jnp.int32)
    twist_re, twist_im = global_roots(sample_index[:, None], bin_index[None, :], series_len, -1.0)
    col_re, col_im = complex_times(col_re, col_im, twist_re, twist_im)
    row_re, row_im = to_rows(col_re, col_im)
    row_re, row_im = dft_last(row_re, row_im, -1.0)
    turn_re, turn_im = parity_roots(parity_f, half, -1.0)
    row_re, row_im = complex_times(row_re, row_im, turn_re, turn_im)
    row_re, row_im = half_swap(row_re, row_im, sign_own)
    row_re, row_im = complex_times(row_re, row_im, jnp.cos(chirp_phase), jnp.sin(chirp_phase))
    row_re, row_im = half_swap(row_re, row_im, sign_own)
    turn_re, turn_im = parity_roots(parity_f, half, 1.0)
    row_re, row_im = complex_times(row_re, row_im, turn_re, turn_im)
    row_re, row_im = dft_last(row_re, row_im, 1.0)
    own_bins = time_index * frames_dev + jnp.arange(frames_dev, dtype=jnp.int32)
    own_samples = 2 * jnp.arange(half, dtype=jnp.int32) + parity
    twist_re, twist_im = global_roots(own_bins[:, None], own_samples[None, :], series_len, 1.0)
    row_re, row_im = complex_times(row_re, row_im, twist_re, twist_im)
    col_re, col_im, ignored = to_columns(row_re, row_im)
    col_re, col_im = dft_last(col_re, col_im, 1.0)
    out_re, out_im = to_rows(col_re, col_im)
    return jnp.stack([out_re, out_im])[:, :, None, :]


LANES = 128
CEILING = 224.0
OFFSET = 2.0**-7.75


def expanded(x):
    grown = jnp.abs(x) + OFFSET
    for _ in range(4):
        grown = grown * grown
    return jnp.where(x < 0.0, -grown, grown).astype(jnp.bfloat16)


def restored(code):
    grown = code.astype(jnp.float32)
    size = jnp.abs(grown)
    for _ in range(4):
        size = lax.rsqrt(size)
    size = size - OFFSET
    return jnp.where(grown < 0.0, -size, size)


def times_root(pair, numerator, length):
    re, im = pair
    eighth = numerator * 8 % (8 * length)
    if eighth == 0:
        return re, im
    if eighth == 4 * length:
        return -re, -im
    if eighth == 2 * length:
        return -im, re
    if eighth == 6 * length:
        return im, -re
    angle = 2.0 * math.pi * numerator / length
    c, s = math.cos(angle), math.sin(angle)
    if eighth % (2 * length) == length:
        root = abs(c)
        if c * s > 0:
            plus, minus = (re - im) * root, (re + im) * root
            return (plus, minus) if c > 0 else (-plus, -minus)
        plus, minus = (re + im) * root, (im - re) * root
        return (plus, minus) if c > 0 else (-plus, -minus)
    return re * c - im * s, re * s + im * c


def fft_list(values, direction):
    count = len(values)
    if count == 1:
        return values
    even = fft_list(values[0::2], direction)
    odd = fft_list(values[1::2], direction)
    low, high = [], []
    for k in range(count // 2):
        t_re, t_im = times_root(odd[k], direction * k % count, count)
        e_re, e_im = even[k]
        low.append((e_re + t_re, e_im + t_im))
        high.append((e_re - t_re, e_im - t_im))
    return low + high


def split_parts(x):
    high = x.astype(jnp.bfloat16)
    return high, (x - high.astype(jnp.float32)).astype(jnp.bfloat16)


def np_split(table):
    high = table.astype(ml_dtypes.bfloat16)
    low = (table - high.astype(np.float64)).astype(ml_dtypes.bfloat16)
    return high, low


def real_form(table):
    return np.stack(
        [np.stack([table.real, -table.imag], -1), np.stack([table.imag, table.real], -1)], -2
    )


def frame_tables(time_count, fd, groups, forward):
    frames = time_count * fd
    per = fd // groups
    g = np.arange(fd)
    tables = []
    for p in range(time_count // 2):
        kd = 2 * p + np.arange(2)
        k1 = kd[:, None] + time_count * np.arange(fd)[None, :]
        sign = -1.0 if forward else 1.0
        phase = np.exp(sign * 2j * np.pi * (k1[:, :, None] * g % frames) / frames)
        form = real_form(phase / math.sqrt(frames))
        full = np.zeros((groups, 2, 2, per, 2, 2, fd))
        for j in range(2):
            block = form[j].reshape(groups, per, fd, 2, 2)
            if forward:
                full[:, :, j, :, j, :, :] = block.transpose(0, 3, 1, 4, 2)
            else:
                full[:, :, j, :, j, :, :] = block.transpose(0, 4, 1, 3, 2)
        size = 4 * fd
        full = full.reshape(size, size)
        if not forward:
            full = full.T
        tables.append(np.concatenate(np_split(full), axis=1))
    return np.stack(tables)


def lane_table(width, direction):
    index = np.arange(LANES)
    roots = np.exp(direction * 2j * np.pi * np.outer(index, index) / LANES) / math.sqrt(width)
    form = real_form(roots)
    table = form.transpose(3, 0, 2, 1).reshape(2 * LANES, 2 * LANES)
    return np.concatenate(np_split(table), axis=0)


def twist_table(width):
    blocks = width // LANES
    phase = 2.0 * np.pi * np.outer(np.arange(blocks), np.arange(LANES)) / width
    return np.stack([np.cos(phase), np.sin(phase)], 1).astype(np.float32)


def dot32(a, b):
    return jnp.dot(a, b, preferred_element_type=jnp.float32)


def left_product(table, high, low):
    return dot32(table, jnp.concatenate([high, high], axis=0)) + dot32(
        table[:, : high.shape[0]], low
    )


def right_product(x, table):
    high, low = split_parts(x)
    return dot32(jnp.concatenate([high, high], axis=1), table) + dot32(low, table[: x.shape[1]])


def columns_apart_kernel(count, x_ref, *refs):
    outs, sems = refs[:count], refs[count]
    me = lax.axis_index("tm")
    width = outs[0].shape[2]
    copies = []
    for k in range(count):
        first = pl.multiple_of((me ^ k) * width, LANES)
        copies.append(
            pltpu.make_async_copy(x_ref.at[:, :, pl.ds(first, width)], outs[k], sems.at[k])
        )
    for copy in copies:
        copy.start()
    for copy in copies:
        copy.wait()


def phase_kernel(groups, own_ref, other_ref, out_ref):
    half = own_ref.shape[1]
    own = out_ref.shape[0]
    parity = lax.axis_index("sub")
    for ref, side in ((own_ref, parity), (other_ref, 1 - parity)):
        cols = pl.ds(pl.multiple_of(side * half, LANES), half)
        for low in range(own // 8):
            rows = ref[pl.ds(pl.multiple_of(parity * own + low * 8, 8), 8), :]
            for kd in range(8):
                place = kd // 2 * 8 + kd % 2 * 4 + low
                out_ref[place : place + 1, cols] = rows[kd : kd + 1]


def frames_kernel(count, *refs):
    parts, (table_ref, out_ref, x_ref, high_ref, low_ref) = refs[:count], refs[count:]
    time_count, _, fd, width = x_ref.shape
    me = lax.axis_index("tm")
    for k in range(count):
        x_ref[me ^ k] = parts[k][...]
    groups = out_ref.shape[0]
    halves = width // LANES
    pairs = time_count // 2
    tails = 3
    power = jnp.zeros((16, LANES), jnp.float32)
    for g in range(0, fd, 16):
        for h in range(halves):
            lanes = slice(h * LANES, (h + 1) * LANES)
            values = []
            for d in range(time_count):
                re = x_ref[d, 0, g : g + 16, lanes].astype(jnp.float32)
                im = x_ref[d, 1, g : g + 16, lanes].astype(jnp.float32)
                power = power + (re * re + im * im)
                values.append((re, im))
            for kd, pair in enumerate(fft_list(values, -1)):
                for r in range(2):
                    high, low = split_parts(pair[r])
                    high_ref[kd, r, g : g + 16, lanes] = high
                    low_ref[kd, r, g : g + 16, lanes] = low
    energy = jnp.sum(jnp.sum(power, axis=0, keepdims=True), axis=1, keepdims=True)
    scale = CEILING * lax.rsqrt(jnp.maximum(energy, 1e-30))
    scale = scale.astype(jnp.bfloat16).astype(jnp.float32)
    rows = []
    for h in range(halves):
        lanes = slice(h * LANES, (h + 1) * LANES)
        for r in range(2):
            last = x_ref[time_count - 1, r, fd - 16 :, lanes].astype(jnp.float32)
            rows.append(last[16 - tails :])
            rows.append(jnp.broadcast_to(scale, (1, LANES)))
    tail = jnp.concatenate(rows, axis=0).astype(jnp.bfloat16)
    for dest in range(groups):
        out_ref[dest, halves * pairs] = tail
    for p in range(pairs):
        high = high_ref[2 * p : 2 * p + 2].reshape(4 * fd, width)
        low = low_ref[2 * p : 2 * p + 2].reshape(4 * fd, width)
        code = expanded(left_product(table_ref[p], high, low) * scale)
        for dest in range(groups):
            for h in range(halves):
                out_ref[dest, h * pairs + p] = code[
                    dest * 16 : dest * 16 + 16, h * LANES : (h + 1) * LANES
                ]


def rows_kernel(
    x_ref, cos_ref, sin_ref, taps_ref, row_ref, twist_ref, inverse_ref, forward_ref,
    next_table_ref, out_ref, scale_ref, buf, wrap,
):
    groups, slots = x_ref.shape[0], x_ref.shape[1]
    blocks = twist_ref.shape[0]
    halves = blocks // groups
    pairs = (slots - 1) // halves
    lanes = LANES
    def tap(n1, q):
        row = n1 % 2 * 4 + q
        return taps_ref[n1 // 2, row : row + 1, :]

    unitary = 1.0 / math.sqrt(groups * row_ref.shape[1])

    def block_of(source, h):
        return (source % 2) * (blocks // 2) + (source // 2) * halves + h

    def twist(n1, pair, direction):
        c, s = twist_ref[n1, 0:1, :], twist_ref[n1, 1:2, :]
        if direction < 0:
            s = -s
        return complex_times(pair[0], pair[1], c, s)

    def put(n1, pair):
        buf[n1 * 8 : n1 * 8 + 8, :lanes] = pair[0]
        buf[n1 * 8 : n1 * 8 + 8, lanes:] = pair[1]

    def take(n1):
        return buf[n1 * 8 : n1 * 8 + 8, :lanes], buf[n1 * 8 : n1 * 8 + 8, lanes:]

    def to_samples(values):
        for n1, pair in enumerate(fft_list(values, 1)):
            put(n1, twist(n1, pair, 1))
        buf[...] = right_product(buf[...], inverse_ref[...])

    energy = jnp.zeros((1, lanes), jnp.float32)
    steps = []
    for source in range(groups):
        step = 1.0 / x_ref[source, halves * pairs].astype(jnp.float32)[3:4]
        steps.append(step)
        reach = CEILING * step
        energy = energy + reach * reach
    gain = jnp.max(taps_ref[...], axis=0)
    gain = jnp.maximum(
        jnp.sum(gain[:4], axis=0, keepdims=True), jnp.sum(gain[4:], axis=0, keepdims=True)
    )
    gain = jnp.max(gain, axis=1, keepdims=True)
    scale = CEILING * lax.rsqrt(energy) / gain
    scale_ref[...] = jnp.broadcast_to(scale, scale_ref.shape)

    values = [None] * blocks
    for source in range(groups):
        tile = x_ref[source, halves * pairs].astype(jnp.float32) * unitary
        for h in range(halves):
            part = tile[h * 8 : h * 8 + 8]
            values[block_of(source, h)] = (part, jnp.concatenate([part[4:], part[:4]], axis=0))
    to_samples(values)
    for n1 in range(blocks):
        parts = take(n1)
        t1, t2, t3 = [tap(n1, q) for q in range(1, 4)]
        rows = []
        for part in parts:
            v0, v1, v2 = part[0:1], part[1:2], part[2:3]
            rows += [t1 * v2 + t2 * v1 + t3 * v0, t2 * v2 + t3 * v1, t3 * v2, v0]
        wrap[n1] = jnp.concatenate(rows, axis=0)

    def one_pair(p, carry):
        first = pl.multiple_of(p * 8, 8)

        def row_table(index):
            return row_ref[2 * index, pl.ds(first, 8), :], row_ref[2 * index + 1, pl.ds(first, 8), :]

        values = [None] * blocks
        for source in range(groups):
            for h in range(halves):
                tile = restored(x_ref[source, h * pairs + p]) * steps[source]
                values[block_of(source, h)] = (tile[:8], tile[8:])
        to_samples(values)
        w1, w2, w3 = row_table(0), row_table(1), row_table(2)
        unit = row_table(3)
        turn = row_table(4)
        for n1 in range(blocks):
            re, im = take(n1)
            t = [tap(n1, q) for q in range(4)]
            gain_re = t[0] + w1[0] * t[1] + w2[0] * t[2] + w3[0] * t[3]
            gain_im = w1[1] * t[1] + w2[1] * t[2] + w3[1] * t[3]
            u = [wrap[n1, q : q + 1, :] for q in range(7)]
            back_re = u[0] + (w1[0] * u[1] - w1[1] * u[5]) + (w2[0] * u[2] - w2[1] * u[6])
            back_im = u[4] + (w1[0] * u[5] + w1[1] * u[1]) + (w2[0] * u[6] + w2[1] * u[2])
            re, im = complex_times(re, im, gain_re, gain_im)
            put(n1, complex_times(re - back_re, im - back_im, *turn))
            turn = complex_times(*turn, *unit)
        buf[...] = right_product(buf[...], forward_ref[...])
        values = [twist(n1, take(n1), -1) for n1 in range(blocks)]
        bins = []
        for k, pair in enumerate(fft_list(values, -1)):
            c = cos_ref[pl.ds(first, 8), k * lanes : (k + 1) * lanes]
            s = sin_ref[pl.ds(first, 8), k * lanes : (k + 1) * lanes]
            bins.append(complex_times(*pair, c, s))
        to_samples(bins)
        turn = row_table(4)
        turn = turn[0] * scale, turn[1] * scale
        for n1 in range(blocks):
            re, im = take(n1)
            back = re * turn[0] + im * turn[1], im * turn[0] - re * turn[1]
            dest = n1 // 2 % (groups // 2) * 2 + n1 % 2
            h = n1 // groups
            out_ref[dest, h * pairs + p] = expanded(jnp.concatenate(back, axis=0))
            turn = complex_times(*turn, *unit)
        return carry

    lax.fori_loop(0, pairs, one_pair, 0)


def columns_kernel(count, x_ref, table_ref, *refs):
    outs, (out_ref, high_ref, low_ref, mid_ref) = refs[:count], refs[count:]
    groups, slots = x_ref.shape[0], x_ref.shape[1]
    time_count, halves, _, fd, _ = out_ref.shape
    me = lax.axis_index("tm")
    pairs = slots // halves
    width = halves * LANES
    for p in range(pairs):
        for source in range(groups):
            for h in range(halves):
                high, low = split_parts(restored(x_ref[source, h * pairs + p]))
                rows = slice(source * 16, source * 16 + 16)
                cols = slice(h * LANES, (h + 1) * LANES)
                high_ref[rows, cols] = high
                low_ref[rows, cols] = low
        mid_ref[2 * p : 2 * p + 2] = left_product(
            table_ref[p], high_ref[...], low_ref[...]
        ).reshape(2, 2 * fd, width)
    for g in range(0, fd, 16):
        for h in range(halves):
            cols = slice(h * LANES, (h + 1) * LANES)
            values = [
                (mid_ref[kd, g : g + 16, cols], mid_ref[kd, fd + g : fd + g + 16, cols])
                for kd in range(time_count)
            ]
            for d, pair in enumerate(fft_list(values, 1)):
                for r in range(2):
                    out_ref[d, h, r, g : g + 16, :] = expanded(pair[r])
    for k in range(count):
        outs[k][...] = out_ref[me ^ k]


def output_kernel(count, *refs):
    parts, (scale_ref, out_ref, mixed) = refs[:count], refs[count:]
    halves, _, fd, _ = parts[0].shape
    lots = count * halves
    step = 1.0 / scale_ref[0:1, :]
    me = lax.axis_index("tm")
    for h in range(halves):
        for k in range(count):
            tile = restored(parts[k][h].reshape(2 * fd, LANES)) * step
            mixed[pl.ds((me ^ k) + count * h, LANES, stride=lots), :] = tile.T
    for block in range(lots):
        tile = mixed[block * LANES : (block + 1) * LANES, :].T
        for r in range(2):
            out_ref[r, :, 0, block * LANES : (block + 1) * LANES] = tile[r * fd : (r + 1) * fd]


def near(x):
    return pltpu.with_memory_space_constraint(x, pltpu.VMEM)


def call(kernel, outs, scratch, *args):
    return pl.pallas_call(
        kernel,
        out_shape=outs,
        in_specs=[pl.BlockSpec(memory_space=pltpu.VMEM)] * len(args),
        out_specs=jax.tree.map(lambda _: pl.BlockSpec(memory_space=pltpu.VMEM), outs),
        scratch_shapes=scratch,
        compiler_params=pltpu.CompilerParams(vmem_limit_bytes=24 << 20),
    )(*[near(x) for x in args])


def swap_parts(parts):
    count = len(parts)
    moved = {0: parts[0]}
    for k in range(count - 1, 0, -1):
        moved[k] = lax.ppermute(parts[k], "tm", [(i, i ^ k) for i in range(count)])
    return [moved[k] for k in range(count)]


def swap_all(x, axes):
    return lax.all_to_all(x, axes, split_axis=0, concat_axis=0, tiled=True)


def row_tables(k1, frames, width):
    series_len = frames * width
    shifts = [1 * k1 % frames, 2 * k1 % frames, 3 * k1 % frames]
    parts = [jnp.broadcast_to(s[:, None] * width, (k1.shape[0], LANES)) for s in shifts]
    parts.append(jnp.broadcast_to(k1[:, None], (k1.shape[0], LANES)))
    blocks = width // LANES
    parts.append(k1[:, None] * (blocks * jnp.arange(LANES, dtype=jnp.int32))[None, :] % series_len)
    angles = jnp.stack(parts).astype(jnp.float32) * (-2.0 * math.pi / series_len)
    return jnp.stack([jnp.cos(angles), jnp.sin(angles)], 1).reshape(10, k1.shape[0], LANES)


def fast_body(channels, synth_taps, chirp_phase):
    _, fd, half = channels.shape
    time_count = lax.axis_size("tm")
    subs = lax.axis_size("sub")
    groups = time_count * subs
    width = half * subs
    frames = fd * time_count
    col_width = half // time_count
    halves = col_width // LANES
    pairs = time_count // 2
    blocks = width // LANES
    per = fd // groups
    own = fd // subs
    time_index = lax.axis_index("tm")
    parity = lax.axis_index("sub")
    f32, bf16 = jnp.float32, jnp.bfloat16
    shape = pltpu.VMEM

    sent = pl.pallas_call(
        functools.partial(columns_apart_kernel, time_count),
        out_shape=[shape((2, fd, col_width), bf16)] * time_count,
        in_specs=[pl.BlockSpec(memory_space=pl.ANY)],
        out_specs=[pl.BlockSpec(memory_space=pltpu.VMEM)] * time_count,
        scratch_shapes=[pltpu.SemaphoreType.DMA((time_count,))],
        compiler_params=pltpu.CompilerParams(vmem_limit_bytes=24 << 20),
    )(channels)
    got = swap_parts(sent)

    theirs = partner(chirp_phase, "sub", 0)
    other_taps = partner(synth_taps, "sub", 0)[:, 0]

    def both(a, b):
        return jnp.where(parity == 0, a, b), jnp.where(parity == 0, b, a)

    phase = call(
        functools.partial(phase_kernel, groups), shape((own, width), f32), [], chirp_phase, theirs
    )
    cos_part, sin_part = jnp.cos(phase), jnp.sin(phase)
    taps = jnp.concatenate(both(synth_taps[:, 0], other_taps), axis=0)
    taps = taps.reshape(-1, LANES, blocks // 2).transpose(2, 0, 1)
    row = jnp.arange(own, dtype=jnp.int32)
    k1 = row // per % 2 + 2 * (row // (2 * per))
    k1 = k1 + time_count * (time_index * (fd // time_count) + parity * per + row % per)
    rows = row_tables(k1, frames, width)

    slots = halves * pairs + 1
    coded = call(
        functools.partial(frames_kernel, time_count),
        shape((groups, slots, 16, LANES), bf16),
        [pltpu.VMEM((time_count, 2, fd, col_width), bf16)] * 3,
        *got,
        jnp.asarray(frame_tables(time_count, fd, groups, True)),
    )
    coded = swap_all(coded, ("tm", "sub"))
    back_table = jnp.asarray(frame_tables(time_count, fd, groups, False))
    coded, scale = call(
        rows_kernel,
        (shape((groups, slots - 1, 16, LANES), bf16), shape((8, LANES), f32)),
        [pltpu.VMEM((blocks * 8, 2 * LANES), f32), pltpu.VMEM((blocks, 8, LANES), f32)],
        coded,
        cos_part,
        sin_part,
        taps,
        rows,
        jnp.asarray(twist_table(width)),
        jnp.asarray(lane_table(width, 1)),
        jnp.asarray(lane_table(width, -1)),
        back_table,
    )
    coded = swap_all(coded, ("tm", "sub"))
    sent = call(
        functools.partial(columns_kernel, time_count),
        [shape((halves, 2, fd, LANES), bf16)] * time_count,
        [pltpu.VMEM((time_count, halves, 2, fd, LANES), bf16)]
        + [pltpu.VMEM((4 * fd, col_width), bf16)] * 2
        + [pltpu.VMEM((time_count, 2 * fd, col_width), f32)],
        coded,
        back_table,
    )
    return call(
        functools.partial(output_kernel, time_count),
        jax.ShapeDtypeStruct((2, fd, 1, half), f32),
        [pltpu.VMEM((half, LANES), f32)],
        *swap_parts(sent),
        scale,
    )


def body(channels, synth_taps, chirp_phase):
    _, fd, half = channels.shape
    time_count, subs = lax.axis_size("tm"), lax.axis_size("sub")
    groups = time_count * subs
    fits = (
        subs == 2
        and synth_taps.shape[0] == 4
        and half == time_count * 2 * LANES
        and fd == 4 * groups
        and time_count & (time_count - 1) == 0
        and half == groups * LANES
        and 2 * fd == LANES
    )
    return (fast_body if fits else general_body)(channels, synth_taps, chirp_phase)


def solution(mesh):
    placed = (P(None, ("beam", "tm"), "sub"), P(None, "sub", None), P("tm", "sub"))
    return jax.shard_map(
        body,
        mesh=mesh,
        in_specs=placed,
        out_specs=P(None, ("beam", "tm"), "sub", None),
        check_vma=False,
    )
```

```python
import functools
import math

import jax
import jax.numpy as jnp
import ml_dtypes
import numpy as np
from jax import lax
from jax.experimental import pallas as pl
from jax.experimental.pallas import tpu as pltpu
from jax.sharding import PartitionSpec as P


highest = lax.Precision.HIGHEST
inv_root2 = 1.0 / math.sqrt(2.0)


def partner(x, axis, distance):
    return lax.ppermute(x, axis, [(i, i ^ 1 << distance) for i in range(lax.axis_size(axis))])


def shifted(block, axis, distance):
    devices = range(lax.axis_size(axis))
    route = [(i - distance, i) for i in devices if i - distance in devices]
    return lax.ppermute(block, axis, route)


def roots_table(row_count, col_count, length, direction):
    product = (
        jnp.arange(row_count, dtype=jnp.int32)[:, None]
        * jnp.arange(col_count, dtype=jnp.int32)[None, :]
        % length
    )
    angles = direction * 2.0 * math.pi / length * product.astype(jnp.float32)
    return (jnp.cos(angles), jnp.sin(angles))


def global_roots(left_index, right_index, length, direction):
    product = left_index * right_index % length
    angles = direction * 2.0 * math.pi / length * product.astype(jnp.float32)
    return (jnp.cos(angles), jnp.sin(angles))


def parity_roots(parity_f, half, direction):
    angles = direction * math.pi / half * parity_f * jnp.arange(half, dtype=jnp.float32)
    return (jnp.cos(angles), jnp.sin(angles))


def complex_times(left_re, left_im, right_re, right_im):
    return (left_re * right_re - left_im * right_im, left_re * right_im + left_im * right_re)


def complex_einsum(form, left_re, left_im, right_re, right_im):

    def contract(former, latter):
        return jnp.einsum(form, former, latter, precision=highest)

    return (
        contract(left_re, right_re) - contract(left_im, right_im),
        contract(left_re, right_im) + contract(left_im, right_re),
    )


def dft_last(re_part, im_part, direction):
    length = re_part.shape[-1]
    outer_len = math.gcd(length, 32)
    inner_len = length // outer_len
    leading = re_part.shape[:-1]
    re_part = re_part.reshape(leading + (outer_len, inner_len))
    im_part = im_part.reshape(leading + (outer_len, inner_len))
    table_re, table_im = roots_table(outer_len, outer_len, outer_len, direction)
    re_part, im_part = complex_einsum("...uw,ur->...rw", re_part, im_part, table_re, table_im)
    twist_re, twist_im = roots_table(outer_len, inner_len, length, direction)
    re_part, im_part = complex_times(re_part, im_part, twist_re, twist_im)
    table_re, table_im = roots_table(inner_len, inner_len, inner_len, direction)
    re_part, im_part = complex_einsum("...rw,wt->...tr", re_part, im_part, table_re, table_im)
    factor = 1.0 / math.sqrt(length)
    return (
        re_part.reshape(leading + (length,)) * factor,
        im_part.reshape(leading + (length,)) * factor,
    )


def half_swap(re_part, im_part, sign_own):
    other_re, other_im = partner((re_part, im_part), "sub", 0)
    return (
        (other_re + sign_own * re_part) * inv_root2,
        (other_im + sign_own * im_part) * inv_root2,
    )


def to_columns(re_part, im_part):
    time_count = lax.axis_size("tm")
    time_index = lax.axis_index("tm")
    parity = lax.axis_index("sub")
    half = re_part.shape[1]
    got_re, got_im = (
        lax.all_to_all(re_part.T, "tm", split_axis=0, concat_axis=1, tiled=True),
        lax.all_to_all(im_part.T, "tm", split_axis=0, concat_axis=1, tiled=True),
    )
    col_width = half // time_count
    sample_index = 2 * (time_index * col_width + jnp.arange(col_width, dtype=jnp.int32)) + parity
    return (got_re, got_im, sample_index)


def to_rows(re_part, im_part):
    got_re, got_im = (
        lax.all_to_all(re_part, "tm", split_axis=1, concat_axis=0, tiled=True),
        lax.all_to_all(im_part, "tm", split_axis=1, concat_axis=0, tiled=True),
    )
    return (got_re.T, got_im.T)


def general_body(channels, synth_taps, chirp_phase):
    frames_dev = channels.shape[1]
    half = channels.shape[2]
    tap_count = synth_taps.shape[0]
    time_index = lax.axis_index("tm")
    time_count = lax.axis_size("tm")
    parity = lax.axis_index("sub")
    parity_f = parity.astype(jnp.float32)
    sign_own = 1.0 - 2.0 * parity_f
    total_frames = frames_dev * time_count
    series_len = total_frames * 2 * half
    partner_re, partner_im = partner((channels[0], channels[1]), "sub", 0)
    mixed_re = (
        partner_re.astype(jnp.float32) + sign_own * channels[0].astype(jnp.float32)
    ) * inv_root2
    mixed_im = (
        partner_im.astype(jnp.float32) + sign_own * channels[1].astype(jnp.float32)
    ) * inv_root2
    turn_re, turn_im = parity_roots(parity_f, half, 1.0)
    mixed_re, mixed_im = complex_times(mixed_re, mixed_im, turn_re, turn_im)
    volt_re, volt_im = dft_last(mixed_re, mixed_im, 1.0)
    keep_from = frames_dev - tap_count + 1
    tail_re, tail_im = shifted((volt_re[keep_from:], volt_im[keep_from:]), "tm", 1)
    long_re = jnp.concatenate([tail_re, volt_re], axis=0)
    long_im = jnp.concatenate([tail_im, volt_im], axis=0)
    synth_re = jnp.zeros_like(volt_re)
    synth_im = jnp.zeros_like(volt_im)
    for offset in range(tap_count):
        begin = tap_count - 1 - offset
        synth_re = synth_re + synth_taps[offset, 0] * long_re[begin : begin + frames_dev]
        synth_im = synth_im + synth_taps[offset, 0] * long_im[begin : begin + frames_dev]
    col_re, col_im, sample_index = to_columns(synth_re, synth_im)
    col_re, col_im = dft_last(col_re, col_im, -1.0)
    bin_index = jnp.arange(total_frames, dtype=jnp.int32)
    twist_re, twist_im = global_roots(sample_index[:, None], bin_index[None, :], series_len, -1.0)
    col_re, col_im = complex_times(col_re, col_im, twist_re, twist_im)
    row_re, row_im = to_rows(col_re, col_im)
    row_re, row_im = dft_last(row_re, row_im, -1.0)
    turn_re, turn_im = parity_roots(parity_f, half, -1.0)
    row_re, row_im = complex_times(row_re, row_im, turn_re, turn_im)
    row_re, row_im = half_swap(row_re, row_im, sign_own)
    row_re, row_im = complex_times(row_re, row_im, jnp.cos(chirp_phase), jnp.sin(chirp_phase))
    row_re, row_im = half_swap(row_re, row_im, sign_own)
    turn_re, turn_im = parity_roots(parity_f, half, 1.0)
    row_re, row_im = complex_times(row_re, row_im, turn_re, turn_im)
    row_re, row_im = dft_last(row_re, row_im, 1.0)
    own_bins = time_index * frames_dev + jnp.arange(frames_dev, dtype=jnp.int32)
    own_samples = 2 * jnp.arange(half, dtype=jnp.int32) + parity
    twist_re, twist_im = global_roots(own_bins[:, None], own_samples[None, :], series_len, 1.0)
    row_re, row_im = complex_times(row_re, row_im, twist_re, twist_im)
    col_re, col_im, ignored = to_columns(row_re, row_im)
    col_re, col_im = dft_last(col_re, col_im, 1.0)
    out_re, out_im = to_rows(col_re, col_im)
    return jnp.stack([out_re, out_im])[:, :, None, :]


LANES = 128
CEILING = 224.0
STRIDE = 4
OFFSET = 2.0**-7.75


def expanded(x):
    grown = jnp.abs(x) + OFFSET
    for _ in range(4):
        grown = grown * grown
    return jnp.where(x < 0.0, -grown, grown).astype(jnp.bfloat16)


def restored(code):
    grown = code.astype(jnp.float32)
    size = jnp.abs(grown)
    for _ in range(4):
        size = lax.rsqrt(size)
    size = size - OFFSET
    return jnp.where(grown < 0.0, -size, size)


def times_root(pair, numerator, length):
    re, im = pair
    eighth = numerator * 8 % (8 * length)
    if eighth == 0:
        return re, im
    if eighth == 4 * length:
        return -re, -im
    if eighth == 2 * length:
        return -im, re
    if eighth == 6 * length:
        return im, -re
    angle = 2.0 * math.pi * numerator / length
    c, s = math.cos(angle), math.sin(angle)
    if eighth % (2 * length) == length:
        root = abs(c)
        if c * s > 0:
            plus, minus = (re - im) * root, (re + im) * root
            return (plus, minus) if c > 0 else (-plus, -minus)
        plus, minus = (re + im) * root, (im - re) * root
        return (plus, minus) if c > 0 else (-plus, -minus)
    return re * c - im * s, re * s + im * c


def fft_list(values, direction):
    count = len(values)
    if count == 1:
        return values
    even = fft_list(values[0::2], direction)
    odd = fft_list(values[1::2], direction)
    low, high = [], []
    for k in range(count // 2):
        t_re, t_im = times_root(odd[k], direction * k % count, count)
        e_re, e_im = even[k]
        low.append((e_re + t_re, e_im + t_im))
        high.append((e_re - t_re, e_im - t_im))
    return low + high


def split_parts(x):
    high = x.astype(jnp.bfloat16)
    return high, (x - high.astype(jnp.float32)).astype(jnp.bfloat16)


def np_split(table):
    high = table.astype(ml_dtypes.bfloat16)
    low = (table - high.astype(np.float64)).astype(ml_dtypes.bfloat16)
    return high, low


def real_form(table):
    return np.stack(
        [np.stack([table.real, -table.imag], -1), np.stack([table.imag, table.real], -1)], -2
    )


def frame_tables(time_count, fd, groups, forward):
    frames = time_count * fd
    per = fd // groups
    g = np.arange(fd)
    tables = []
    for p in range(time_count // 2):
        kd = 2 * p + np.arange(2)
        k1 = kd[:, None] + time_count * np.arange(fd)[None, :]
        sign = -1.0 if forward else 1.0
        phase = np.exp(sign * 2j * np.pi * (k1[:, :, None] * g % frames) / frames)
        form = real_form(phase / math.sqrt(frames))
        full = np.zeros((groups, 2, 2, per, 2, 2, fd))
        for j in range(2):
            block = form[j].reshape(groups, per, fd, 2, 2)
            if forward:
                full[:, :, j, :, j, :, :] = block.transpose(0, 3, 1, 4, 2)
            else:
                full[:, :, j, :, j, :, :] = block.transpose(0, 4, 1, 3, 2)
        size = 4 * fd
        full = full.reshape(size, size)
        if not forward:
            full = full.T
        tables.append(np.concatenate(np_split(full), axis=1))
    return np.stack(tables)


def lane_table(width, direction):
    index = np.arange(LANES)
    roots = np.exp(direction * 2j * np.pi * np.outer(index, index) / LANES) / math.sqrt(width)
    form = real_form(roots)
    table = form.transpose(3, 0, 2, 1).reshape(2 * LANES, 2 * LANES)
    return np.concatenate(np_split(table), axis=0)


def twist_table(width):
    blocks = width // LANES
    phase = 2.0 * np.pi * np.outer(np.arange(blocks), np.arange(LANES)) / width
    return np.stack([np.cos(phase), np.sin(phase)], 1).astype(np.float32)


def dot32(a, b):
    return jnp.dot(a, b, preferred_element_type=jnp.float32)


def left_product(table, high, low):
    return dot32(table, jnp.concatenate([high, high], axis=0)) + dot32(
        table[:, : high.shape[0]], low
    )


def right_product(x, table):
    high, low = split_parts(x)
    return dot32(jnp.concatenate([high, high], axis=1), table) + dot32(low, table[: x.shape[1]])


def columns_apart_kernel(count, x_ref, *refs):
    outs, sems = refs[:count], refs[count]
    me = lax.axis_index("tm")
    width = outs[0].shape[2]
    copies = []
    for k in range(count):
        first = pl.multiple_of((me ^ k) * width, LANES)
        copies.append(
            pltpu.make_async_copy(x_ref.at[:, :, pl.ds(first, width)], outs[k], sems.at[k])
        )
    for copy in copies:
        copy.start()
    for copy in copies:
        copy.wait()


def phase_kernel(groups, own_ref, other_ref, out_ref):
    half = own_ref.shape[1]
    own = out_ref.shape[0]
    parity = lax.axis_index("sub")
    for ref, side in ((own_ref, parity), (other_ref, 1 - parity)):
        cols = pl.ds(pl.multiple_of(side * half, LANES), half)
        for low in range(own // 8):
            rows = ref[pl.ds(pl.multiple_of(parity * own + low * 8, 8), 8), :]
            for kd in range(8):
                place = kd // 2 * 8 + kd % 2 * 4 + low
                out_ref[place : place + 1, cols] = rows[kd : kd + 1]


def frames_kernel(count, *refs):
    parts, (table_ref, out_ref, x_ref, high_ref, low_ref) = refs[:count], refs[count:]
    time_count, _, fd, width = x_ref.shape
    me = lax.axis_index("tm")
    for k in range(count):
        x_ref[me ^ k] = parts[k][...]
    groups = out_ref.shape[0]
    halves = width // LANES
    pairs = time_count // 2
    tails = 3
    power = jnp.zeros((16, LANES), jnp.float32)
    for g in range(0, fd, 16):
        for h in range(halves):
            lanes = slice(h * LANES, (h + 1) * LANES)
            values = []
            for d in range(time_count):
                re = x_ref[d, 0, g : g + 16, lanes].astype(jnp.float32)
                im = x_ref[d, 1, g : g + 16, lanes].astype(jnp.float32)
                power = power + (re * re + im * im)
                values.append((re, im))
            for kd, pair in enumerate(fft_list(values, -1)):
                for r in range(2):
                    high, low = split_parts(pair[r])
                    high_ref[kd, r, g : g + 16, lanes] = high
                    low_ref[kd, r, g : g + 16, lanes] = low
    energy = jnp.sum(jnp.sum(power, axis=0, keepdims=True), axis=1, keepdims=True)
    scale = CEILING * lax.rsqrt(jnp.maximum(energy, 1e-30))
    scale = scale.astype(jnp.bfloat16).astype(jnp.float32)
    rows = []
    for h in range(halves):
        lanes = slice(h * LANES, (h + 1) * LANES)
        for r in range(2):
            last = x_ref[time_count - 1, r, fd - 16 :, lanes].astype(jnp.float32)
            rows.append(last[16 - tails :])
            rows.append(jnp.broadcast_to(scale, (1, LANES)))
    tail = jnp.concatenate(rows, axis=0).astype(jnp.bfloat16)
    for dest in range(groups):
        out_ref[dest, halves * pairs] = tail
    for p in range(pairs):
        high = high_ref[2 * p : 2 * p + 2].reshape(4 * fd, width)
        low = low_ref[2 * p : 2 * p + 2].reshape(4 * fd, width)
        code = expanded(left_product(table_ref[p], high, low) * scale)
        for dest in range(groups):
            for h in range(halves):
                out_ref[dest, h * pairs + p] = code[
                    dest * 16 : dest * 16 + 16, h * LANES : (h + 1) * LANES
                ]


def rows_kernel(
    x_ref, cos_ref, sin_ref, taps_ref, row_ref, twist_ref, inverse_ref, forward_ref,
    next_table_ref, out_ref, scale_ref, first_buf, second_buf, wrap,
):
    groups, slots = x_ref.shape[0], x_ref.shape[1]
    blocks = twist_ref.shape[0]
    halves = blocks // groups
    pairs = (slots - 1) // halves
    lanes = LANES
    def tap(n1, q):
        row = n1 % 2 * 4 + q
        return taps_ref[n1 // 2, row : row + 1, :]

    unitary = 1.0 / math.sqrt(groups * row_ref.shape[1])

    def block_of(source, h):
        return (source % 2) * (blocks // 2) + (source // 2) * halves + h

    def twist(n1, pair, direction):
        c, s = twist_ref[n1, 0:1, :], twist_ref[n1, 1:2, :]
        if direction < 0:
            s = -s
        return complex_times(pair[0], pair[1], c, s)

    def put(buf, n1, pair):
        buf[n1 * 8 : n1 * 8 + 8, :lanes] = pair[0]
        buf[n1 * 8 : n1 * 8 + 8, lanes:] = pair[1]

    def take(buf, n1):
        return buf[n1 * 8 : n1 * 8 + 8, :lanes], buf[n1 * 8 : n1 * 8 + 8, lanes:]

    def put_samples(buf, values):
        for n1, pair in enumerate(fft_list(values, 1)):
            put(buf, n1, twist(n1, pair, 1))

    def mix(buf, table_ref):
        buf[...] = right_product(buf[...], table_ref[...])

    energy = jnp.zeros((1, lanes), jnp.float32)
    steps = []
    for source in range(groups):
        step = 1.0 / x_ref[source, halves * pairs].astype(jnp.float32)[3:4]
        steps.append(step)
        reach = CEILING * step
        energy = energy + reach * reach
    gain = jnp.max(taps_ref[...], axis=0)
    gain = jnp.maximum(
        jnp.sum(gain[:4], axis=0, keepdims=True), jnp.sum(gain[4:], axis=0, keepdims=True)
    )
    gain = jnp.max(gain, axis=1, keepdims=True)
    scale = CEILING * lax.rsqrt(energy) / gain
    scale_ref[...] = jnp.broadcast_to(scale, scale_ref.shape)

    values = [None] * blocks
    for source in range(groups):
        tile = x_ref[source, halves * pairs].astype(jnp.float32) * unitary
        for h in range(halves):
            part = tile[h * 8 : h * 8 + 8]
            values[block_of(source, h)] = (part, jnp.concatenate([part[4:], part[:4]], axis=0))
    put_samples(first_buf, values)
    mix(first_buf, inverse_ref)
    for n1 in range(blocks):
        parts = take(first_buf, n1)
        t1, t2, t3 = [tap(n1, q) for q in range(1, 4)]
        rows = []
        for part in parts:
            v0, v1, v2 = part[0:1], part[1:2], part[2:3]
            rows += [t1 * v2 + t2 * v1 + t3 * v0, t2 * v2 + t3 * v1, t3 * v2, v0]
        wrap[n1] = jnp.concatenate(rows, axis=0)

    def one_pair(p, buf):
        first = pl.multiple_of(p * 8, 8)

        def row_table(index):
            return row_ref[2 * index, pl.ds(first, 8), :], row_ref[2 * index + 1, pl.ds(first, 8), :]

        values = [None] * blocks
        for source in range(groups):
            for h in range(halves):
                tile = restored(x_ref[source, h * pairs + p]) * steps[source]
                values[block_of(source, h)] = (tile[:8], tile[8:])
        put_samples(buf, values)
        yield
        mix(buf, inverse_ref)
        yield
        w1, w2, w3 = row_table(0), row_table(1), row_table(2)
        unit = row_table(3)
        turn = row_table(4)
        for n1 in range(blocks):
            re, im = take(buf, n1)
            t = [tap(n1, q) for q in range(4)]
            gain_re = t[0] + w1[0] * t[1] + w2[0] * t[2] + w3[0] * t[3]
            gain_im = w1[1] * t[1] + w2[1] * t[2] + w3[1] * t[3]
            u = [wrap[n1, q : q + 1, :] for q in range(7)]
            back_re = u[0] + (w1[0] * u[1] - w1[1] * u[5]) + (w2[0] * u[2] - w2[1] * u[6])
            back_im = u[4] + (w1[0] * u[5] + w1[1] * u[1]) + (w2[0] * u[6] + w2[1] * u[2])
            re, im = complex_times(re, im, gain_re, gain_im)
            put(buf, n1, complex_times(re - back_re, im - back_im, *turn))
            turn = complex_times(*turn, *unit)
        yield
        mix(buf, forward_ref)
        yield
        values = [twist(n1, take(buf, n1), -1) for n1 in range(blocks)]
        bins = []
        for k, pair in enumerate(fft_list(values, -1)):
            c = cos_ref[pl.ds(first, 8), k * lanes : (k + 1) * lanes]
            s = sin_ref[pl.ds(first, 8), k * lanes : (k + 1) * lanes]
            bins.append(complex_times(*pair, c, s))
        put_samples(buf, bins)
        yield
        mix(buf, inverse_ref)
        yield
        turn = row_table(4)
        turn = turn[0] * scale, turn[1] * scale
        for n1 in range(blocks):
            re, im = take(buf, n1)
            back = re * turn[0] + im * turn[1], im * turn[0] - re * turn[1]
            dest = n1 // 2 % (groups // 2) * 2 + n1 % 2
            h = n1 // groups
            out_ref[dest, h * pairs + p] = expanded(jnp.concatenate(back, axis=0))
            turn = complex_times(*turn, *unit)

    def two_pairs(step, carry):
        early = one_pair(2 * step, first_buf)
        late = one_pair(2 * step + 1, second_buf)
        next(early)
        running = True
        while running:
            next(early, None)
            running = next(late, late) is not late
        return carry

    lax.fori_loop(0, pairs // 2, two_pairs, 0)


def columns_kernel(count, x_ref, table_ref, *refs):
    outs, (out_ref, high_ref, low_ref, mid_ref) = refs[:count], refs[count:]
    groups, slots = x_ref.shape[0], x_ref.shape[1]
    time_count, halves, _, fd, _ = out_ref.shape
    me = lax.axis_index("tm")
    pairs = slots // halves
    width = halves * LANES
    for p in range(pairs):
        for source in range(groups):
            for h in range(halves):
                high, low = split_parts(restored(x_ref[source, h * pairs + p]))
                rows = slice(source * 16, source * 16 + 16)
                cols = slice(h * LANES, (h + 1) * LANES)
                high_ref[rows, cols] = high
                low_ref[rows, cols] = low
        mid_ref[2 * p : 2 * p + 2] = left_product(
            table_ref[p], high_ref[...], low_ref[...]
        ).reshape(2, 2 * fd, width)
    for g in range(0, fd, 16):
        for h in range(halves):
            cols = slice(h * LANES, (h + 1) * LANES)
            values = [
                (mid_ref[kd, g : g + 16, cols], mid_ref[kd, fd + g : fd + g + 16, cols])
                for kd in range(time_count)
            ]
            for d, pair in enumerate(fft_list(values, 1)):
                for r in range(2):
                    out_ref[d, h, r, g : g + 16, :] = expanded(pair[r])
    for k in range(count):
        outs[k][...] = out_ref[me ^ k]


def output_kernel(count, *refs):
    parts, (scale_ref, out_ref, mixed, held, sems) = refs[:count], refs[count:]
    halves, _, fd, _ = parts[0].shape
    lots = count * halves
    step = 1.0 / scale_ref[0:1, :]
    me = lax.axis_index("tm")
    for h in range(halves):
        for k in range(count):
            tile = restored(parts[k][h].reshape(2 * fd, LANES)) * step
            mixed[pl.ds((me ^ k) + count * h, LANES, stride=lots), :] = tile.T
    copies = []
    for block in range(lots):
        tile = mixed[block * LANES : (block + 1) * LANES, :].T
        for r in range(2):
            held[r, :, 0, block * LANES : (block + 1) * LANES] = tile[r * fd : (r + 1) * fd]
        if block % STRIDE == STRIDE - 1:
            cols = pl.ds((block + 1 - STRIDE) * LANES, STRIDE * LANES)
            copies.append(
                pltpu.make_async_copy(
                    held.at[:, :, :, cols], out_ref.at[:, :, :, cols], sems.at[block // STRIDE]
                )
            )
            copies[-1].start()
    for copy in copies:
        copy.wait()


def near(x):
    return pltpu.with_memory_space_constraint(x, pltpu.VMEM)


def call(kernel, outs, scratch, *args):
    return pl.pallas_call(
        kernel,
        out_shape=outs,
        in_specs=[pl.BlockSpec(memory_space=pltpu.VMEM)] * len(args),
        out_specs=jax.tree.map(lambda _: pl.BlockSpec(memory_space=pltpu.VMEM), outs),
        scratch_shapes=scratch,
        compiler_params=pltpu.CompilerParams(vmem_limit_bytes=24 << 20),
    )(*[near(x) for x in args])


def swap_parts(parts):
    count = len(parts)
    moved = {0: parts[0]}
    for k in range(count - 1, 0, -1):
        moved[k] = lax.ppermute(parts[k], "tm", [(i, i ^ k) for i in range(count)])
    return [moved[k] for k in range(count)]


def swap_all(x, axes):
    return lax.all_to_all(x, axes, split_axis=0, concat_axis=0, tiled=True)


def row_tables(k1, frames, width):
    series_len = frames * width
    shifts = [1 * k1 % frames, 2 * k1 % frames, 3 * k1 % frames]
    parts = [jnp.broadcast_to(s[:, None] * width, (k1.shape[0], LANES)) for s in shifts]
    parts.append(jnp.broadcast_to(k1[:, None], (k1.shape[0], LANES)))
    blocks = width // LANES
    parts.append(k1[:, None] * (blocks * jnp.arange(LANES, dtype=jnp.int32))[None, :] % series_len)
    angles = jnp.stack(parts).astype(jnp.float32) * (-2.0 * math.pi / series_len)
    return jnp.stack([jnp.cos(angles), jnp.sin(angles)], 1).reshape(10, k1.shape[0], LANES)


def fast_body(channels, synth_taps, chirp_phase):
    _, fd, half = channels.shape
    time_count = lax.axis_size("tm")
    subs = lax.axis_size("sub")
    groups = time_count * subs
    width = half * subs
    frames = fd * time_count
    col_width = half // time_count
    halves = col_width // LANES
    pairs = time_count // 2
    blocks = width // LANES
    per = fd // groups
    own = fd // subs
    time_index = lax.axis_index("tm")
    parity = lax.axis_index("sub")
    f32, bf16 = jnp.float32, jnp.bfloat16
    shape = pltpu.VMEM

    sent = pl.pallas_call(
        functools.partial(columns_apart_kernel, time_count),
        out_shape=[shape((2, fd, col_width), bf16)] * time_count,
        in_specs=[pl.BlockSpec(memory_space=pl.ANY)],
        out_specs=[pl.BlockSpec(memory_space=pltpu.VMEM)] * time_count,
        scratch_shapes=[pltpu.SemaphoreType.DMA((time_count,))],
        compiler_params=pltpu.CompilerParams(vmem_limit_bytes=24 << 20),
    )(channels)
    got = swap_parts(sent)

    theirs = partner(chirp_phase, "sub", 0)
    other_taps = partner(synth_taps, "sub", 0)[:, 0]

    def both(a, b):
        return jnp.where(parity == 0, a, b), jnp.where(parity == 0, b, a)

    phase = call(
        functools.partial(phase_kernel, groups), shape((own, width), f32), [], chirp_phase, theirs
    )
    cos_part, sin_part = jnp.cos(phase), jnp.sin(phase)
    taps = jnp.concatenate(both(synth_taps[:, 0], other_taps), axis=0)
    taps = taps.reshape(-1, LANES, blocks // 2).transpose(2, 0, 1)
    row = jnp.arange(own, dtype=jnp.int32)
    k1 = row // per % 2 + 2 * (row // (2 * per))
    k1 = k1 + time_count * (time_index * (fd // time_count) + parity * per + row % per)
    rows = row_tables(k1, frames, width)

    slots = halves * pairs + 1
    coded = call(
        functools.partial(frames_kernel, time_count),
        shape((groups, slots, 16, LANES), bf16),
        [pltpu.VMEM((time_count, 2, fd, col_width), bf16)] * 3,
        *got,
        jnp.asarray(frame_tables(time_count, fd, groups, True)),
    )
    coded = swap_all(coded, ("tm", "sub"))
    back_table = jnp.asarray(frame_tables(time_count, fd, groups, False))
    coded, scale = call(
        rows_kernel,
        (shape((groups, slots - 1, 16, LANES), bf16), shape((8, LANES), f32)),
        [pltpu.VMEM((blocks * 8, 2 * LANES), f32)] * 2 + [pltpu.VMEM((blocks, 8, LANES), f32)],
        coded,
        cos_part,
        sin_part,
        taps,
        rows,
        jnp.asarray(twist_table(width)),
        jnp.asarray(lane_table(width, 1)),
        jnp.asarray(lane_table(width, -1)),
        back_table,
    )
    coded = swap_all(coded, ("tm", "sub"))
    sent = call(
        functools.partial(columns_kernel, time_count),
        [shape((halves, 2, fd, LANES), bf16)] * time_count,
        [pltpu.VMEM((time_count, halves, 2, fd, LANES), bf16)]
        + [pltpu.VMEM((4 * fd, col_width), bf16)] * 2
        + [pltpu.VMEM((time_count, 2 * fd, col_width), f32)],
        coded,
        back_table,
    )
    moved = swap_parts(sent)
    blocks_out = half // LANES
    return pl.pallas_call(
        functools.partial(output_kernel, time_count),
        out_shape=jax.ShapeDtypeStruct((2, fd, 1, half), f32),
        in_specs=[pl.BlockSpec(memory_space=pltpu.VMEM)] * (time_count + 1),
        out_specs=pl.BlockSpec(memory_space=pltpu.HBM),
        scratch_shapes=[
            pltpu.VMEM((half, LANES), f32),
            pltpu.VMEM((2, fd, 1, half), f32),
            pltpu.SemaphoreType.DMA((blocks_out // STRIDE,)),
        ],
        compiler_params=pltpu.CompilerParams(vmem_limit_bytes=24 << 20),
    )(*[near(x) for x in moved], near(scale))


def body(channels, synth_taps, chirp_phase):
    _, fd, half = channels.shape
    time_count, subs = lax.axis_size("tm"), lax.axis_size("sub")
    groups = time_count * subs
    fits = (
        subs == 2
        and synth_taps.shape[0] == 4
        and half == time_count * 2 * LANES
        and fd == 4 * groups
        and time_count & (time_count - 1) == 0
        and half == groups * LANES
        and 2 * fd == LANES
    )
    return (fast_body if fits else general_body)(channels, synth_taps, chirp_phase)


def solution(mesh):
    placed = (P(None, ("beam", "tm"), "sub"), P(None, "sub", None), P("tm", "sub"))
    return jax.shard_map(
        body,
        mesh=mesh,
        in_specs=placed,
        out_specs=P(None, ("beam", "tm"), "sub", None),
        check_vma=False,
    )
```

```python
import functools
import math

import jax
import jax.numpy as jnp
import ml_dtypes
import numpy as np
from jax import lax
from jax.experimental import pallas as pl
from jax.experimental.pallas import tpu as pltpu
from jax.sharding import PartitionSpec as P


highest = lax.Precision.HIGHEST
inv_root2 = 1.0 / math.sqrt(2.0)


def partner(x, axis, distance):
    return lax.ppermute(x, axis, [(i, i ^ 1 << distance) for i in range(lax.axis_size(axis))])


def shifted(block, axis, distance):
    devices = range(lax.axis_size(axis))
    route = [(i - distance, i) for i in devices if i - distance in devices]
    return lax.ppermute(block, axis, route)


def roots_table(row_count, col_count, length, direction):
    product = (
        jnp.arange(row_count, dtype=jnp.int32)[:, None]
        * jnp.arange(col_count, dtype=jnp.int32)[None, :]
        % length
    )
    angles = direction * 2.0 * math.pi / length * product.astype(jnp.float32)
    return (jnp.cos(angles), jnp.sin(angles))


def global_roots(left_index, right_index, length, direction):
    product = left_index * right_index % length
    angles = direction * 2.0 * math.pi / length * product.astype(jnp.float32)
    return (jnp.cos(angles), jnp.sin(angles))


def parity_roots(parity_f, half, direction):
    angles = direction * math.pi / half * parity_f * jnp.arange(half, dtype=jnp.float32)
    return (jnp.cos(angles), jnp.sin(angles))


def complex_times(left_re, left_im, right_re, right_im):
    return (left_re * right_re - left_im * right_im, left_re * right_im + left_im * right_re)


def complex_einsum(form, left_re, left_im, right_re, right_im):

    def contract(former, latter):
        return jnp.einsum(form, former, latter, precision=highest)

    return (
        contract(left_re, right_re) - contract(left_im, right_im),
        contract(left_re, right_im) + contract(left_im, right_re),
    )


def dft_last(re_part, im_part, direction):
    length = re_part.shape[-1]
    outer_len = math.gcd(length, 32)
    inner_len = length // outer_len
    leading = re_part.shape[:-1]
    re_part = re_part.reshape(leading + (outer_len, inner_len))
    im_part = im_part.reshape(leading + (outer_len, inner_len))
    table_re, table_im = roots_table(outer_len, outer_len, outer_len, direction)
    re_part, im_part = complex_einsum("...uw,ur->...rw", re_part, im_part, table_re, table_im)
    twist_re, twist_im = roots_table(outer_len, inner_len, length, direction)
    re_part, im_part = complex_times(re_part, im_part, twist_re, twist_im)
    table_re, table_im = roots_table(inner_len, inner_len, inner_len, direction)
    re_part, im_part = complex_einsum("...rw,wt->...tr", re_part, im_part, table_re, table_im)
    factor = 1.0 / math.sqrt(length)
    return (
        re_part.reshape(leading + (length,)) * factor,
        im_part.reshape(leading + (length,)) * factor,
    )


def half_swap(re_part, im_part, sign_own):
    other_re, other_im = partner((re_part, im_part), "sub", 0)
    return (
        (other_re + sign_own * re_part) * inv_root2,
        (other_im + sign_own * im_part) * inv_root2,
    )


def to_columns(re_part, im_part):
    time_count = lax.axis_size("tm")
    time_index = lax.axis_index("tm")
    parity = lax.axis_index("sub")
    half = re_part.shape[1]
    got_re, got_im = (
        lax.all_to_all(re_part.T, "tm", split_axis=0, concat_axis=1, tiled=True),
        lax.all_to_all(im_part.T, "tm", split_axis=0, concat_axis=1, tiled=True),
    )
    col_width = half // time_count
    sample_index = 2 * (time_index * col_width + jnp.arange(col_width, dtype=jnp.int32)) + parity
    return (got_re, got_im, sample_index)


def to_rows(re_part, im_part):
    got_re, got_im = (
        lax.all_to_all(re_part, "tm", split_axis=1, concat_axis=0, tiled=True),
        lax.all_to_all(im_part, "tm", split_axis=1, concat_axis=0, tiled=True),
    )
    return (got_re.T, got_im.T)


def general_body(channels, synth_taps, chirp_phase):
    frames_dev = channels.shape[1]
    half = channels.shape[2]
    tap_count = synth_taps.shape[0]
    time_index = lax.axis_index("tm")
    time_count = lax.axis_size("tm")
    parity = lax.axis_index("sub")
    parity_f = parity.astype(jnp.float32)
    sign_own = 1.0 - 2.0 * parity_f
    total_frames = frames_dev * time_count
    series_len = total_frames * 2 * half
    partner_re, partner_im = partner((channels[0], channels[1]), "sub", 0)
    mixed_re = (
        partner_re.astype(jnp.float32) + sign_own * channels[0].astype(jnp.float32)
    ) * inv_root2
    mixed_im = (
        partner_im.astype(jnp.float32) + sign_own * channels[1].astype(jnp.float32)
    ) * inv_root2
    turn_re, turn_im = parity_roots(parity_f, half, 1.0)
    mixed_re, mixed_im = complex_times(mixed_re, mixed_im, turn_re, turn_im)
    volt_re, volt_im = dft_last(mixed_re, mixed_im, 1.0)
    keep_from = frames_dev - tap_count + 1
    tail_re, tail_im = shifted((volt_re[keep_from:], volt_im[keep_from:]), "tm", 1)
    long_re = jnp.concatenate([tail_re, volt_re], axis=0)
    long_im = jnp.concatenate([tail_im, volt_im], axis=0)
    synth_re = jnp.zeros_like(volt_re)
    synth_im = jnp.zeros_like(volt_im)
    for offset in range(tap_count):
        begin = tap_count - 1 - offset
        synth_re = synth_re + synth_taps[offset, 0] * long_re[begin : begin + frames_dev]
        synth_im = synth_im + synth_taps[offset, 0] * long_im[begin : begin + frames_dev]
    col_re, col_im, sample_index = to_columns(synth_re, synth_im)
    col_re, col_im = dft_last(col_re, col_im, -1.0)
    bin_index = jnp.arange(total_frames, dtype=jnp.int32)
    twist_re, twist_im = global_roots(sample_index[:, None], bin_index[None, :], series_len, -1.0)
    col_re, col_im = complex_times(col_re, col_im, twist_re, twist_im)
    row_re, row_im = to_rows(col_re, col_im)
    row_re, row_im = dft_last(row_re, row_im, -1.0)
    turn_re, turn_im = parity_roots(parity_f, half, -1.0)
    row_re, row_im = complex_times(row_re, row_im, turn_re, turn_im)
    row_re, row_im = half_swap(row_re, row_im, sign_own)
    row_re, row_im = complex_times(row_re, row_im, jnp.cos(chirp_phase), jnp.sin(chirp_phase))
    row_re, row_im = half_swap(row_re, row_im, sign_own)
    turn_re, turn_im = parity_roots(parity_f, half, 1.0)
    row_re, row_im = complex_times(row_re, row_im, turn_re, turn_im)
    row_re, row_im = dft_last(row_re, row_im, 1.0)
    own_bins = time_index * frames_dev + jnp.arange(frames_dev, dtype=jnp.int32)
    own_samples = 2 * jnp.arange(half, dtype=jnp.int32) + parity
    twist_re, twist_im = global_roots(own_bins[:, None], own_samples[None, :], series_len, 1.0)
    row_re, row_im = complex_times(row_re, row_im, twist_re, twist_im)
    col_re, col_im, ignored = to_columns(row_re, row_im)
    col_re, col_im = dft_last(col_re, col_im, 1.0)
    out_re, out_im = to_rows(col_re, col_im)
    return jnp.stack([out_re, out_im])[:, :, None, :]


LANES = 128
CEILING = 224.0
STRIDE = 8
OFFSET = 2.0**-7.75


def expanded(x):
    grown = jnp.abs(x) + OFFSET
    for _ in range(4):
        grown = grown * grown
    return jnp.where(x < 0.0, -grown, grown).astype(jnp.bfloat16)


def restored(code):
    grown = code.astype(jnp.float32)
    size = jnp.abs(grown)
    for _ in range(4):
        size = lax.rsqrt(size)
    size = size - OFFSET
    return jnp.where(grown < 0.0, -size, size)


def times_root(pair, numerator, length):
    re, im = pair
    eighth = numerator * 8 % (8 * length)
    if eighth == 0:
        return re, im
    if eighth == 4 * length:
        return -re, -im
    if eighth == 2 * length:
        return -im, re
    if eighth == 6 * length:
        return im, -re
    angle = 2.0 * math.pi * numerator / length
    c, s = math.cos(angle), math.sin(angle)
    if eighth % (2 * length) == length:
        root = abs(c)
        if c * s > 0:
            plus, minus = (re - im) * root, (re + im) * root
            return (plus, minus) if c > 0 else (-plus, -minus)
        plus, minus = (re + im) * root, (im - re) * root
        return (plus, minus) if c > 0 else (-plus, -minus)
    return re * c - im * s, re * s + im * c


def fft_list(values, direction):
    count = len(values)
    if count == 1:
        return values
    even = fft_list(values[0::2], direction)
    odd = fft_list(values[1::2], direction)
    low, high = [], []
    for k in range(count // 2):
        t_re, t_im = times_root(odd[k], direction * k % count, count)
        e_re, e_im = even[k]
        low.append((e_re + t_re, e_im + t_im))
        high.append((e_re - t_re, e_im - t_im))
    return low + high


def split_parts(x):
    high = x.astype(jnp.bfloat16)
    return high, (x - high.astype(jnp.float32)).astype(jnp.bfloat16)


def np_split(table):
    high = table.astype(ml_dtypes.bfloat16)
    low = (table - high.astype(np.float64)).astype(ml_dtypes.bfloat16)
    return high, low


def real_form(table):
    return np.stack(
        [np.stack([table.real, -table.imag], -1), np.stack([table.imag, table.real], -1)], -2
    )


def frame_tables(time_count, fd, groups, forward):
    frames = time_count * fd
    per = fd // groups
    g = np.arange(fd)
    tables = []
    for p in range(time_count // 2):
        kd = 2 * p + np.arange(2)
        k1 = kd[:, None] + time_count * np.arange(fd)[None, :]
        sign = -1.0 if forward else 1.0
        phase = np.exp(sign * 2j * np.pi * (k1[:, :, None] * g % frames) / frames)
        form = real_form(phase / math.sqrt(frames))
        full = np.zeros((groups, 2, 2, per, 2, 2, fd))
        for j in range(2):
            block = form[j].reshape(groups, per, fd, 2, 2)
            if forward:
                full[:, :, j, :, j, :, :] = block.transpose(0, 3, 1, 4, 2)
            else:
                full[:, :, j, :, j, :, :] = block.transpose(0, 4, 1, 3, 2)
        size = 4 * fd
        full = full.reshape(size, size)
        if not forward:
            full = full.T
        tables.append(np.concatenate(np_split(full), axis=1))
    return np.stack(tables)


def lane_table(width, direction):
    index = np.arange(LANES)
    roots = np.exp(direction * 2j * np.pi * np.outer(index, index) / LANES) / math.sqrt(width)
    form = real_form(roots)
    table = form.transpose(3, 0, 2, 1).reshape(2 * LANES, 2 * LANES)
    return np.concatenate(np_split(table), axis=0)


def twist_table(width):
    blocks = width // LANES
    phase = 2.0 * np.pi * np.outer(np.arange(blocks), np.arange(LANES)) / width
    return np.stack([np.cos(phase), np.sin(phase)], 1).astype(np.float32)


def dot32(a, b):
    return jnp.dot(a, b, preferred_element_type=jnp.float32)


def left_product(table, high, low):
    return dot32(table, jnp.concatenate([high, high], axis=0)) + dot32(
        table[:, : high.shape[0]], low
    )


def right_product(x, table):
    high, low = split_parts(x)
    return dot32(jnp.concatenate([high, high], axis=1), table) + dot32(low, table[: x.shape[1]])


def columns_apart_kernel(count, x_ref, *refs):
    outs, sems = refs[:count], refs[count]
    me = lax.axis_index("tm")
    width = outs[0].shape[2]
    copies = []
    for k in range(count):
        first = pl.multiple_of((me ^ k) * width, LANES)
        copies.append(
            pltpu.make_async_copy(x_ref.at[:, :, pl.ds(first, width)], outs[k], sems.at[k])
        )
    for copy in copies:
        copy.start()
    for copy in copies:
        copy.wait()


def phase_kernel(groups, own_ref, other_ref, out_ref):
    half = own_ref.shape[1]
    own = out_ref.shape[0]
    parity = lax.axis_index("sub")
    for ref, side in ((own_ref, parity), (other_ref, 1 - parity)):
        cols = pl.ds(pl.multiple_of(side * half, LANES), half)
        for low in range(own // 8):
            rows = ref[pl.ds(pl.multiple_of(parity * own + low * 8, 8), 8), :]
            for kd in range(8):
                place = kd // 2 * 8 + kd % 2 * 4 + low
                out_ref[place : place + 1, cols] = rows[kd : kd + 1]


def frames_kernel(count, *refs):
    parts, table_ref = refs[:count], refs[count]
    out_ref, x_ref, high_ref, low_ref = refs[count + 5 :]
    time_count, _, fd, width = x_ref.shape
    me = lax.axis_index("tm")
    for k in range(count):
        x_ref[me ^ k] = parts[k][...]
    groups = out_ref.shape[0]
    halves = width // LANES
    pairs = time_count // 2
    tails = 3
    power = jnp.zeros((16, LANES), jnp.float32)
    for g in range(0, fd, 16):
        for h in range(halves):
            lanes = slice(h * LANES, (h + 1) * LANES)
            values = []
            for d in range(time_count):
                re = x_ref[d, 0, g : g + 16, lanes].astype(jnp.float32)
                im = x_ref[d, 1, g : g + 16, lanes].astype(jnp.float32)
                power = power + (re * re + im * im)
                values.append((re, im))
            for kd, pair in enumerate(fft_list(values, -1)):
                for r in range(2):
                    high, low = split_parts(pair[r])
                    high_ref[kd, r, g : g + 16, lanes] = high
                    low_ref[kd, r, g : g + 16, lanes] = low
    energy = jnp.sum(jnp.sum(power, axis=0, keepdims=True), axis=1, keepdims=True)
    scale = CEILING * lax.rsqrt(jnp.maximum(energy, 1e-30))
    scale = scale.astype(jnp.bfloat16).astype(jnp.float32)
    rows = []
    for h in range(halves):
        lanes = slice(h * LANES, (h + 1) * LANES)
        for r in range(2):
            last = x_ref[time_count - 1, r, fd - 16 :, lanes].astype(jnp.float32)
            rows.append(last[16 - tails :])
            rows.append(jnp.broadcast_to(scale, (1, LANES)))
    tail = jnp.concatenate(rows, axis=0).astype(jnp.bfloat16)
    for dest in range(groups):
        out_ref[dest, halves * pairs] = tail
    for p in range(pairs):
        high = high_ref[2 * p : 2 * p + 2].reshape(4 * fd, width)
        low = low_ref[2 * p : 2 * p + 2].reshape(4 * fd, width)
        code = expanded(left_product(table_ref[p], high, low) * scale)
        for dest in range(groups):
            for h in range(halves):
                out_ref[dest, h * pairs + p] = code[
                    dest * 16 : dest * 16 + 16, h * LANES : (h + 1) * LANES
                ]


def rows_kernel(
    x_ref, cos_ref, sin_ref, taps_ref, row_ref, twist_ref, inverse_ref, forward_ref,
    next_table_ref, out_ref, scale_ref, first_buf, second_buf, wrap,
):
    groups, slots = x_ref.shape[0], x_ref.shape[1]
    blocks = twist_ref.shape[0]
    halves = blocks // groups
    pairs = (slots - 1) // halves
    lanes = LANES
    def tap(n1, q):
        row = n1 % 2 * 4 + q
        return taps_ref[n1 // 2, row : row + 1, :]

    unitary = 1.0 / math.sqrt(groups * row_ref.shape[1])

    def block_of(source, h):
        return (source % 2) * (blocks // 2) + (source // 2) * halves + h

    def twist(n1, pair, direction):
        c, s = twist_ref[n1, 0:1, :], twist_ref[n1, 1:2, :]
        if direction < 0:
            s = -s
        return complex_times(pair[0], pair[1], c, s)

    def put(buf, n1, pair):
        buf[n1 * 8 : n1 * 8 + 8, :lanes] = pair[0]
        buf[n1 * 8 : n1 * 8 + 8, lanes:] = pair[1]

    def take(buf, n1):
        return buf[n1 * 8 : n1 * 8 + 8, :lanes], buf[n1 * 8 : n1 * 8 + 8, lanes:]

    def put_samples(buf, values):
        for n1, pair in enumerate(fft_list(values, 1)):
            put(buf, n1, twist(n1, pair, 1))

    def mix(buf, table_ref):
        buf[...] = right_product(buf[...], table_ref[...])

    energy = jnp.zeros((1, lanes), jnp.float32)
    steps = []
    for source in range(groups):
        step = 1.0 / x_ref[source, halves * pairs].astype(jnp.float32)[3:4]
        steps.append(step)
        reach = CEILING * step
        energy = energy + reach * reach
    gain = jnp.max(taps_ref[...], axis=0)
    gain = jnp.maximum(
        jnp.sum(gain[:4], axis=0, keepdims=True), jnp.sum(gain[4:], axis=0, keepdims=True)
    )
    gain = jnp.max(gain, axis=1, keepdims=True)
    scale = CEILING * lax.rsqrt(energy) / gain
    scale_ref[...] = jnp.broadcast_to(scale, scale_ref.shape)

    values = [None] * blocks
    for source in range(groups):
        tile = x_ref[source, halves * pairs].astype(jnp.float32) * unitary
        for h in range(halves):
            part = tile[h * 8 : h * 8 + 8]
            values[block_of(source, h)] = (part, jnp.concatenate([part[4:], part[:4]], axis=0))
    put_samples(first_buf, values)
    mix(first_buf, inverse_ref)
    for n1 in range(blocks):
        parts = take(first_buf, n1)
        t1, t2, t3 = [tap(n1, q) for q in range(1, 4)]
        rows = []
        for part in parts:
            v0, v1, v2 = part[0:1], part[1:2], part[2:3]
            rows += [t1 * v2 + t2 * v1 + t3 * v0, t2 * v2 + t3 * v1, t3 * v2, v0]
        wrap[n1] = jnp.concatenate(rows, axis=0)

    def one_pair(p, buf):
        first = pl.multiple_of(p * 8, 8)

        def row_table(index):
            return row_ref[2 * index, pl.ds(first, 8), :], row_ref[2 * index + 1, pl.ds(first, 8), :]

        values = [None] * blocks
        for source in range(groups):
            for h in range(halves):
                tile = restored(x_ref[source, h * pairs + p]) * steps[source]
                values[block_of(source, h)] = (tile[:8], tile[8:])
        put_samples(buf, values)
        yield
        mix(buf, inverse_ref)
        yield
        w1, w2, w3 = row_table(0), row_table(1), row_table(2)
        unit = row_table(3)
        turn = row_table(4)
        for n1 in range(blocks):
            re, im = take(buf, n1)
            t = [tap(n1, q) for q in range(4)]
            gain_re = t[0] + w1[0] * t[1] + w2[0] * t[2] + w3[0] * t[3]
            gain_im = w1[1] * t[1] + w2[1] * t[2] + w3[1] * t[3]
            u = [wrap[n1, q : q + 1, :] for q in range(7)]
            back_re = u[0] + (w1[0] * u[1] - w1[1] * u[5]) + (w2[0] * u[2] - w2[1] * u[6])
            back_im = u[4] + (w1[0] * u[5] + w1[1] * u[1]) + (w2[0] * u[6] + w2[1] * u[2])
            re, im = complex_times(re, im, gain_re, gain_im)
            put(buf, n1, complex_times(re - back_re, im - back_im, *turn))
            turn = complex_times(*turn, *unit)
        yield
        mix(buf, forward_ref)
        yield
        values = [twist(n1, take(buf, n1), -1) for n1 in range(blocks)]
        bins = []
        for k, pair in enumerate(fft_list(values, -1)):
            c = cos_ref[pl.ds(first, 8), k * lanes : (k + 1) * lanes]
            s = sin_ref[pl.ds(first, 8), k * lanes : (k + 1) * lanes]
            bins.append(complex_times(*pair, c, s))
        put_samples(buf, bins)
        yield
        mix(buf, inverse_ref)
        yield
        turn = row_table(4)
        turn = turn[0] * scale, turn[1] * scale
        for n1 in range(blocks):
            re, im = take(buf, n1)
            back = re * turn[0] + im * turn[1], im * turn[0] - re * turn[1]
            dest = n1 // 2 % (groups // 2) * 2 + n1 % 2
            h = n1 // groups
            out_ref[dest, h * pairs + p] = expanded(jnp.concatenate(back, axis=0))
            turn = complex_times(*turn, *unit)

    def two_pairs(step, carry):
        early = one_pair(2 * step, first_buf)
        late = one_pair(2 * step + 1, second_buf)
        next(early)
        running = True
        while running:
            next(early, None)
            running = next(late, late) is not late
        return carry

    lax.fori_loop(0, pairs // 2, two_pairs, 0)


def columns_kernel(count, x_ref, table_ref, *refs):
    outs, (out_ref, high_ref, low_ref, mid_ref) = refs[:count], refs[count:]
    groups, slots = x_ref.shape[0], x_ref.shape[1]
    time_count, halves, _, fd, _ = out_ref.shape
    me = lax.axis_index("tm")
    pairs = slots // halves
    width = halves * LANES
    for p in range(pairs):
        for source in range(groups):
            for h in range(halves):
                high, low = split_parts(restored(x_ref[source, h * pairs + p]))
                rows = slice(source * 16, source * 16 + 16)
                cols = slice(h * LANES, (h + 1) * LANES)
                high_ref[rows, cols] = high
                low_ref[rows, cols] = low
        mid_ref[2 * p : 2 * p + 2] = left_product(
            table_ref[p], high_ref[...], low_ref[...]
        ).reshape(2, 2 * fd, width)
    for g in range(0, fd, 16):
        for h in range(halves):
            cols = slice(h * LANES, (h + 1) * LANES)
            values = [
                (mid_ref[kd, g : g + 16, cols], mid_ref[kd, fd + g : fd + g + 16, cols])
                for kd in range(time_count)
            ]
            for d, pair in enumerate(fft_list(values, 1)):
                for r in range(2):
                    out_ref[d, h, r, g : g + 16, :] = expanded(pair[r])
    for k in range(count):
        outs[k][...] = out_ref[me ^ k]


def early_kernel(count, *refs):
    parts, out_ref = refs[:count], refs[count]
    halves, _, fd, _ = parts[0].shape
    for i, part in enumerate(parts):
        for h in range(halves):
            out_ref[i * halves + h] = restored(part[h].reshape(2 * fd, LANES)).T


def output_kernel(early, late, *refs):
    turned, parts = refs[0], refs[1 : 1 + len(late)]
    scale_ref, out_ref, mixed, held, sems = refs[1 + len(late) :]
    halves, _, fd, _ = parts[0].shape
    count = len(early) + len(late)
    lots = count * halves
    step = 1.0 / scale_ref[0:1, :]
    me = lax.axis_index("tm")
    for h in range(halves):
        for i, k in enumerate(early):
            rows = pl.ds((me ^ k) + count * h, LANES, stride=lots)
            mixed[rows, :] = turned[i * halves + h] * step
        for i, k in enumerate(late):
            rows = pl.ds((me ^ k) + count * h, LANES, stride=lots)
            mixed[rows, :] = (restored(parts[i][h].reshape(2 * fd, LANES)) * step).T
    wide = held.reshape(2 * fd, lots, LANES)
    copies = []
    for block in range(lots):
        tile = mixed[block * LANES : (block + 1) * LANES, :].T
        held[pl.ds(block, 2 * fd, stride=lots), :] = tile
        if block % STRIDE == STRIDE - 1:
            span = pl.ds(block + 1 - STRIDE, STRIDE)
            copies.append(
                pltpu.make_async_copy(
                    wide.at[:, span, :], out_ref.at[:, span, :], sems.at[block // STRIDE]
                )
            )
            copies[-1].start()
    for copy in copies:
        copy.wait()


def near(x):
    return pltpu.with_memory_space_constraint(x, pltpu.VMEM)


def call(kernel, outs, scratch, *args):
    return pl.pallas_call(
        kernel,
        out_shape=outs,
        in_specs=[pl.BlockSpec(memory_space=pltpu.VMEM)] * len(args),
        out_specs=jax.tree.map(lambda _: pl.BlockSpec(memory_space=pltpu.VMEM), outs),
        scratch_shapes=scratch,
        compiler_params=pltpu.CompilerParams(vmem_limit_bytes=24 << 20),
    )(*[near(x) for x in args])


def swap_parts(parts):
    count = len(parts)
    moved = {0: parts[0]}
    for k in range(count - 1, 0, -1):
        moved[k] = lax.ppermute(parts[k], "tm", [(i, i ^ k) for i in range(count)])
    return [moved[k] for k in range(count)]


def swap_all(x, axes):
    return lax.all_to_all(x, axes, split_axis=0, concat_axis=0, tiled=True)


def row_tables(k1, frames, width):
    series_len = frames * width
    shifts = [1 * k1 % frames, 2 * k1 % frames, 3 * k1 % frames]
    parts = [jnp.broadcast_to(s[:, None] * width, (k1.shape[0], LANES)) for s in shifts]
    parts.append(jnp.broadcast_to(k1[:, None], (k1.shape[0], LANES)))
    blocks = width // LANES
    parts.append(k1[:, None] * (blocks * jnp.arange(LANES, dtype=jnp.int32))[None, :] % series_len)
    angles = jnp.stack(parts).astype(jnp.float32) * (-2.0 * math.pi / series_len)
    return jnp.stack([jnp.cos(angles), jnp.sin(angles)], 1).reshape(10, k1.shape[0], LANES)


def fast_body(channels, synth_taps, chirp_phase):
    _, fd, half = channels.shape
    time_count = lax.axis_size("tm")
    subs = lax.axis_size("sub")
    groups = time_count * subs
    width = half * subs
    frames = fd * time_count
    col_width = half // time_count
    halves = col_width // LANES
    pairs = time_count // 2
    blocks = width // LANES
    per = fd // groups
    own = fd // subs
    time_index = lax.axis_index("tm")
    parity = lax.axis_index("sub")
    f32, bf16 = jnp.float32, jnp.bfloat16
    shape = pltpu.VMEM

    sent = pl.pallas_call(
        functools.partial(columns_apart_kernel, time_count),
        out_shape=[shape((2, fd, col_width), bf16)] * time_count,
        in_specs=[pl.BlockSpec(memory_space=pltpu.HBM)],
        out_specs=[pl.BlockSpec(memory_space=pltpu.VMEM)] * time_count,
        scratch_shapes=[pltpu.SemaphoreType.DMA((time_count,))],
        compiler_params=pltpu.CompilerParams(vmem_limit_bytes=24 << 20),
    )(pltpu.with_memory_space_constraint(channels, pltpu.HBM))
    got = swap_parts(sent)

    theirs = partner(chirp_phase, "sub", 0)
    other_taps = partner(synth_taps, "sub", 0)[:, 0]

    def both(a, b):
        return jnp.where(parity == 0, a, b), jnp.where(parity == 0, b, a)

    phase = call(
        functools.partial(phase_kernel, groups), shape((own, width), f32), [], chirp_phase, theirs
    )
    cos_part, sin_part = jnp.cos(phase), jnp.sin(phase)
    taps = jnp.concatenate(both(synth_taps[:, 0], other_taps), axis=0)
    taps = taps.reshape(-1, LANES, blocks // 2).transpose(2, 0, 1)
    row = jnp.arange(own, dtype=jnp.int32)
    k1 = row // per % 2 + 2 * (row // (2 * per))
    k1 = k1 + time_count * (time_index * (fd // time_count) + parity * per + row % per)
    rows = row_tables(k1, frames, width)

    slots = halves * pairs + 1
    coded = call(
        functools.partial(frames_kernel, time_count),
        shape((groups, slots, 16, LANES), bf16),
        [pltpu.VMEM((time_count, 2, fd, col_width), bf16)] * 3,
        *got,
        jnp.asarray(frame_tables(time_count, fd, groups, True)),
        cos_part,
        sin_part,
        taps,
        rows,
    )
    coded = swap_all(coded, ("tm", "sub"))
    back_table = jnp.asarray(frame_tables(time_count, fd, groups, False))
    coded, scale = call(
        rows_kernel,
        (shape((groups, slots - 1, 16, LANES), bf16), shape((8, LANES), f32)),
        [pltpu.VMEM((blocks * 8, 2 * LANES), f32)] * 2 + [pltpu.VMEM((blocks, 8, LANES), f32)],
        coded,
        cos_part,
        sin_part,
        taps,
        rows,
        jnp.asarray(twist_table(width)),
        jnp.asarray(lane_table(width, 1)),
        jnp.asarray(lane_table(width, -1)),
        back_table,
    )
    coded = swap_all(coded, ("tm", "sub"))
    sent = call(
        functools.partial(columns_kernel, time_count),
        [shape((halves, 2, fd, LANES), bf16)] * time_count,
        [pltpu.VMEM((time_count, halves, 2, fd, LANES), bf16)]
        + [pltpu.VMEM((4 * fd, col_width), bf16)] * 2
        + [pltpu.VMEM((time_count, 2 * fd, col_width), f32)],
        coded,
        back_table,
    )
    moved = swap_parts(sent)
    early = [0, *range(time_count - 1, time_count // 2, -1)]
    late = list(range(time_count // 2, 0, -1))
    turned = call(
        functools.partial(early_kernel, len(early)),
        shape((len(early) * halves, LANES, 2 * fd), f32),
        [],
        *[moved[k] for k in early],
    )
    blocks_out = half // LANES
    out = pl.pallas_call(
        functools.partial(output_kernel, early, late),
        out_shape=jax.ShapeDtypeStruct((2 * fd, blocks_out, LANES), f32),
        in_specs=[pl.BlockSpec(memory_space=pltpu.VMEM)] * (len(late) + 2),
        out_specs=pl.BlockSpec(memory_space=pltpu.HBM),
        scratch_shapes=[
            pltpu.VMEM((half, LANES), f32),
            pltpu.VMEM((2 * fd * blocks_out, LANES), f32),
            pltpu.SemaphoreType.DMA((blocks_out // STRIDE,)),
        ],
        compiler_params=pltpu.CompilerParams(vmem_limit_bytes=24 << 20),
    )(near(turned), *[near(moved[k]) for k in late], near(scale))
    return out.reshape(2, fd, 1, half)


def body(channels, synth_taps, chirp_phase):
    _, fd, half = channels.shape
    time_count, subs = lax.axis_size("tm"), lax.axis_size("sub")
    groups = time_count * subs
    fits = (
        subs == 2
        and synth_taps.shape[0] == 4
        and half == time_count * 2 * LANES
        and fd == 4 * groups
        and time_count & (time_count - 1) == 0
        and half == groups * LANES
        and 2 * fd == LANES
    )
    return (fast_body if fits else general_body)(channels, synth_taps, chirp_phase)


def solution(mesh):
    placed = (P(None, ("beam", "tm"), "sub"), P(None, "sub", None), P("tm", "sub"))
    return jax.shard_map(
        body,
        mesh=mesh,
        in_specs=placed,
        out_specs=P(None, ("beam", "tm"), "sub", None),
        check_vma=False,
    )
```

```python
import functools
import math

import jax
import jax.numpy as jnp
import ml_dtypes
import numpy as np
from jax import lax
from jax.experimental import pallas as pl
from jax.experimental.pallas import tpu as pltpu
from jax.sharding import PartitionSpec as P


highest = lax.Precision.HIGHEST
inv_root2 = 1.0 / math.sqrt(2.0)


def partner(x, axis, distance):
    return lax.ppermute(x, axis, [(i, i ^ 1 << distance) for i in range(lax.axis_size(axis))])


def shifted(block, axis, distance):
    devices = range(lax.axis_size(axis))
    route = [(i - distance, i) for i in devices if i - distance in devices]
    return lax.ppermute(block, axis, route)


def roots_table(row_count, col_count, length, direction):
    product = (
        jnp.arange(row_count, dtype=jnp.int32)[:, None]
        * jnp.arange(col_count, dtype=jnp.int32)[None, :]
        % length
    )
    angles = direction * 2.0 * math.pi / length * product.astype(jnp.float32)
    return (jnp.cos(angles), jnp.sin(angles))


def global_roots(left_index, right_index, length, direction):
    product = left_index * right_index % length
    angles = direction * 2.0 * math.pi / length * product.astype(jnp.float32)
    return (jnp.cos(angles), jnp.sin(angles))


def parity_roots(parity_f, half, direction):
    angles = direction * math.pi / half * parity_f * jnp.arange(half, dtype=jnp.float32)
    return (jnp.cos(angles), jnp.sin(angles))


def complex_times(left_re, left_im, right_re, right_im):
    return (left_re * right_re - left_im * right_im, left_re * right_im + left_im * right_re)


def complex_einsum(form, left_re, left_im, right_re, right_im):

    def contract(former, latter):
        return jnp.einsum(form, former, latter, precision=highest)

    return (
        contract(left_re, right_re) - contract(left_im, right_im),
        contract(left_re, right_im) + contract(left_im, right_re),
    )


def dft_last(re_part, im_part, direction):
    length = re_part.shape[-1]
    outer_len = math.gcd(length, 32)
    inner_len = length // outer_len
    leading = re_part.shape[:-1]
    re_part = re_part.reshape(leading + (outer_len, inner_len))
    im_part = im_part.reshape(leading + (outer_len, inner_len))
    table_re, table_im = roots_table(outer_len, outer_len, outer_len, direction)
    re_part, im_part = complex_einsum("...uw,ur->...rw", re_part, im_part, table_re, table_im)
    twist_re, twist_im = roots_table(outer_len, inner_len, length, direction)
    re_part, im_part = complex_times(re_part, im_part, twist_re, twist_im)
    table_re, table_im = roots_table(inner_len, inner_len, inner_len, direction)
    re_part, im_part = complex_einsum("...rw,wt->...tr", re_part, im_part, table_re, table_im)
    factor = 1.0 / math.sqrt(length)
    return (
        re_part.reshape(leading + (length,)) * factor,
        im_part.reshape(leading + (length,)) * factor,
    )


def half_swap(re_part, im_part, sign_own):
    other_re, other_im = partner((re_part, im_part), "sub", 0)
    return (
        (other_re + sign_own * re_part) * inv_root2,
        (other_im + sign_own * im_part) * inv_root2,
    )


def to_columns(re_part, im_part):
    time_count = lax.axis_size("tm")
    time_index = lax.axis_index("tm")
    parity = lax.axis_index("sub")
    half = re_part.shape[1]
    got_re, got_im = (
        lax.all_to_all(re_part.T, "tm", split_axis=0, concat_axis=1, tiled=True),
        lax.all_to_all(im_part.T, "tm", split_axis=0, concat_axis=1, tiled=True),
    )
    col_width = half // time_count
    sample_index = 2 * (time_index * col_width + jnp.arange(col_width, dtype=jnp.int32)) + parity
    return (got_re, got_im, sample_index)


def to_rows(re_part, im_part):
    got_re, got_im = (
        lax.all_to_all(re_part, "tm", split_axis=1, concat_axis=0, tiled=True),
        lax.all_to_all(im_part, "tm", split_axis=1, concat_axis=0, tiled=True),
    )
    return (got_re.T, got_im.T)


def general_body(channels, synth_taps, chirp_phase):
    frames_dev = channels.shape[1]
    half = channels.shape[2]
    tap_count = synth_taps.shape[0]
    time_index = lax.axis_index("tm")
    time_count = lax.axis_size("tm")
    parity = lax.axis_index("sub")
    parity_f = parity.astype(jnp.float32)
    sign_own = 1.0 - 2.0 * parity_f
    total_frames = frames_dev * time_count
    series_len = total_frames * 2 * half
    partner_re, partner_im = partner((channels[0], channels[1]), "sub", 0)
    mixed_re = (
        partner_re.astype(jnp.float32) + sign_own * channels[0].astype(jnp.float32)
    ) * inv_root2
    mixed_im = (
        partner_im.astype(jnp.float32) + sign_own * channels[1].astype(jnp.float32)
    ) * inv_root2
    turn_re, turn_im = parity_roots(parity_f, half, 1.0)
    mixed_re, mixed_im = complex_times(mixed_re, mixed_im, turn_re, turn_im)
    volt_re, volt_im = dft_last(mixed_re, mixed_im, 1.0)
    keep_from = frames_dev - tap_count + 1
    tail_re, tail_im = shifted((volt_re[keep_from:], volt_im[keep_from:]), "tm", 1)
    long_re = jnp.concatenate([tail_re, volt_re], axis=0)
    long_im = jnp.concatenate([tail_im, volt_im], axis=0)
    synth_re = jnp.zeros_like(volt_re)
    synth_im = jnp.zeros_like(volt_im)
    for offset in range(tap_count):
        begin = tap_count - 1 - offset
        synth_re = synth_re + synth_taps[offset, 0] * long_re[begin : begin + frames_dev]
        synth_im = synth_im + synth_taps[offset, 0] * long_im[begin : begin + frames_dev]
    col_re, col_im, sample_index = to_columns(synth_re, synth_im)
    col_re, col_im = dft_last(col_re, col_im, -1.0)
    bin_index = jnp.arange(total_frames, dtype=jnp.int32)
    twist_re, twist_im = global_roots(sample_index[:, None], bin_index[None, :], series_len, -1.0)
    col_re, col_im = complex_times(col_re, col_im, twist_re, twist_im)
    row_re, row_im = to_rows(col_re, col_im)
    row_re, row_im = dft_last(row_re, row_im, -1.0)
    turn_re, turn_im = parity_roots(parity_f, half, -1.0)
    row_re, row_im = complex_times(row_re, row_im, turn_re, turn_im)
    row_re, row_im = half_swap(row_re, row_im, sign_own)
    row_re, row_im = complex_times(row_re, row_im, jnp.cos(chirp_phase), jnp.sin(chirp_phase))
    row_re, row_im = half_swap(row_re, row_im, sign_own)
    turn_re, turn_im = parity_roots(parity_f, half, 1.0)
    row_re, row_im = complex_times(row_re, row_im, turn_re, turn_im)
    row_re, row_im = dft_last(row_re, row_im, 1.0)
    own_bins = time_index * frames_dev + jnp.arange(frames_dev, dtype=jnp.int32)
    own_samples = 2 * jnp.arange(half, dtype=jnp.int32) + parity
    twist_re, twist_im = global_roots(own_bins[:, None], own_samples[None, :], series_len, 1.0)
    row_re, row_im = complex_times(row_re, row_im, twist_re, twist_im)
    col_re, col_im, ignored = to_columns(row_re, row_im)
    col_re, col_im = dft_last(col_re, col_im, 1.0)
    out_re, out_im = to_rows(col_re, col_im)
    return jnp.stack([out_re, out_im])[:, :, None, :]


LANES = 128
CEILING = 224.0
STRIDE = 8
OFFSET = 2.0**-7.75


def expanded(x):
    grown = jnp.abs(x) + OFFSET
    for _ in range(4):
        grown = grown * grown
    return jnp.where(x < 0.0, -grown, grown).astype(jnp.bfloat16)


def restored(code):
    grown = code.astype(jnp.float32)
    size = jnp.abs(grown)
    for _ in range(4):
        size = lax.rsqrt(size)
    size = size - OFFSET
    return jnp.where(grown < 0.0, -size, size)


def times_root(pair, numerator, length):
    re, im = pair
    eighth = numerator * 8 % (8 * length)
    if eighth == 0:
        return re, im
    if eighth == 4 * length:
        return -re, -im
    if eighth == 2 * length:
        return -im, re
    if eighth == 6 * length:
        return im, -re
    angle = 2.0 * math.pi * numerator / length
    c, s = math.cos(angle), math.sin(angle)
    if eighth % (2 * length) == length:
        root = abs(c)
        if c * s > 0:
            plus, minus = (re - im) * root, (re + im) * root
            return (plus, minus) if c > 0 else (-plus, -minus)
        plus, minus = (re + im) * root, (im - re) * root
        return (plus, minus) if c > 0 else (-plus, -minus)
    return re * c - im * s, re * s + im * c


def fft_list(values, direction):
    count = len(values)
    if count == 1:
        return values
    even = fft_list(values[0::2], direction)
    odd = fft_list(values[1::2], direction)
    low, high = [], []
    for k in range(count // 2):
        t_re, t_im = times_root(odd[k], direction * k % count, count)
        e_re, e_im = even[k]
        low.append((e_re + t_re, e_im + t_im))
        high.append((e_re - t_re, e_im - t_im))
    return low + high


def split_parts(x):
    high = x.astype(jnp.bfloat16)
    return high, (x - high.astype(jnp.float32)).astype(jnp.bfloat16)


def np_split(table):
    high = table.astype(ml_dtypes.bfloat16)
    low = (table - high.astype(np.float64)).astype(ml_dtypes.bfloat16)
    return high, low


def real_form(table):
    return np.stack(
        [np.stack([table.real, -table.imag], -1), np.stack([table.imag, table.real], -1)], -2
    )


def frame_tables(time_count, fd, groups, forward):
    frames = time_count * fd
    per = fd // groups
    g = np.arange(fd)
    tables = []
    for p in range(time_count // 2):
        kd = 2 * p + np.arange(2)
        k1 = kd[:, None] + time_count * np.arange(fd)[None, :]
        sign = -1.0 if forward else 1.0
        phase = np.exp(sign * 2j * np.pi * (k1[:, :, None] * g % frames) / frames)
        form = real_form(phase / math.sqrt(frames))
        full = np.zeros((groups, 2, 2, per, 2, 2, fd))
        for j in range(2):
            block = form[j].reshape(groups, per, fd, 2, 2)
            if forward:
                full[:, :, j, :, j, :, :] = block.transpose(0, 3, 1, 4, 2)
            else:
                full[:, :, j, :, j, :, :] = block.transpose(0, 4, 1, 3, 2)
        size = 4 * fd
        full = full.reshape(size, size)
        if not forward:
            full = full.T
        tables.append(np.concatenate(np_split(full), axis=1))
    return np.stack(tables)


def lane_table(width, direction):
    index = np.arange(LANES)
    roots = np.exp(direction * 2j * np.pi * np.outer(index, index) / LANES) / math.sqrt(width)
    form = real_form(roots)
    table = form.transpose(3, 0, 2, 1).reshape(2 * LANES, 2 * LANES)
    return np.concatenate(np_split(table), axis=0)


def twist_table(width):
    blocks = width // LANES
    phase = 2.0 * np.pi * np.outer(np.arange(blocks), np.arange(LANES)) / width
    return np.stack([np.cos(phase), np.sin(phase)], 1).astype(np.float32)


def dot32(a, b):
    return jnp.dot(a, b, preferred_element_type=jnp.float32)


def left_product(table, high, low):
    return dot32(table, jnp.concatenate([high, high], axis=0)) + dot32(
        table[:, : high.shape[0]], low
    )


def right_product(x, table):
    high, low = split_parts(x)
    return dot32(jnp.concatenate([high, high], axis=1), table) + dot32(low, table[: x.shape[1]])


def columns_apart_kernel(count, x_ref, *refs):
    outs, sems = refs[:count], refs[count]
    me = lax.axis_index("tm")
    width = outs[0].shape[2]
    copies = []
    for k in range(count):
        first = pl.multiple_of((me ^ k) * width, LANES)
        copies.append(
            pltpu.make_async_copy(x_ref.at[:, :, pl.ds(first, width)], outs[k], sems.at[k])
        )
    for copy in copies:
        copy.start()
    for copy in copies:
        copy.wait()


def phase_kernel(groups, own_ref, other_ref, out_ref):
    half = own_ref.shape[1]
    own = out_ref.shape[0]
    parity = lax.axis_index("sub")
    for ref, side in ((own_ref, parity), (other_ref, 1 - parity)):
        cols = pl.ds(pl.multiple_of(side * half, LANES), half)
        for low in range(own // 8):
            rows = ref[pl.ds(pl.multiple_of(parity * own + low * 8, 8), 8), :]
            for kd in range(8):
                place = kd // 2 * 8 + kd % 2 * 4 + low
                out_ref[place : place + 1, cols] = rows[kd : kd + 1]


def frames_kernel(count, *refs):
    parts, table_ref = refs[:count], refs[count]
    out_ref, x_ref, high_ref, low_ref = refs[count + 5 :]
    time_count, _, fd, width = x_ref.shape
    me = lax.axis_index("tm")
    for k in range(count):
        x_ref[me ^ k] = parts[k][...]
    groups = out_ref.shape[0]
    halves = width // LANES
    pairs = time_count // 2
    tails = 3
    power = jnp.zeros((16, LANES), jnp.float32)
    for g in range(0, fd, 16):
        for h in range(halves):
            lanes = slice(h * LANES, (h + 1) * LANES)
            values = []
            for d in range(time_count):
                re = x_ref[d, 0, g : g + 16, lanes].astype(jnp.float32)
                im = x_ref[d, 1, g : g + 16, lanes].astype(jnp.float32)
                power = power + (re * re + im * im)
                values.append((re, im))
            for kd, pair in enumerate(fft_list(values, -1)):
                for r in range(2):
                    high, low = split_parts(pair[r])
                    high_ref[kd, r, g : g + 16, lanes] = high
                    low_ref[kd, r, g : g + 16, lanes] = low
    energy = jnp.sum(jnp.sum(power, axis=0, keepdims=True), axis=1, keepdims=True)
    scale = CEILING * lax.rsqrt(jnp.maximum(energy, 1e-30))
    scale = scale.astype(jnp.bfloat16).astype(jnp.float32)
    rows = []
    for h in range(halves):
        lanes = slice(h * LANES, (h + 1) * LANES)
        for r in range(2):
            last = x_ref[time_count - 1, r, fd - 16 :, lanes].astype(jnp.float32)
            rows.append(last[16 - tails :])
            rows.append(jnp.broadcast_to(scale, (1, LANES)))
    tail = jnp.concatenate(rows, axis=0).astype(jnp.bfloat16)
    for dest in range(groups):
        out_ref[dest, halves * pairs] = tail
    for p in range(pairs):
        high = high_ref[2 * p : 2 * p + 2].reshape(4 * fd, width)
        low = low_ref[2 * p : 2 * p + 2].reshape(4 * fd, width)
        code = expanded(left_product(table_ref[p], high, low) * scale)
        for dest in range(groups):
            for h in range(halves):
                out_ref[dest, h * pairs + p] = code[
                    dest * 16 : dest * 16 + 16, h * LANES : (h + 1) * LANES
                ]


def rows_kernel(
    x_ref, cos_ref, sin_ref, taps_ref, row_ref, twist_ref, inverse_ref, forward_ref,
    next_table_ref, out_ref, scale_ref, first_buf, second_buf, wrap,
):
    groups, slots = x_ref.shape[0], x_ref.shape[1]
    blocks = twist_ref.shape[0]
    halves = blocks // groups
    pairs = (slots - 1) // halves
    lanes = LANES
    def tap(n1, q):
        row = n1 % 2 * 4 + q
        return taps_ref[n1 // 2, row : row + 1, :]

    unitary = 1.0 / math.sqrt(groups * row_ref.shape[1])

    def block_of(source, h):
        return (source % 2) * (blocks // 2) + (source // 2) * halves + h

    def twist(n1, pair, direction):
        c, s = twist_ref[n1, 0:1, :], twist_ref[n1, 1:2, :]
        if direction < 0:
            s = -s
        return complex_times(pair[0], pair[1], c, s)

    def put(buf, n1, pair):
        buf[n1 * 8 : n1 * 8 + 8, :lanes] = pair[0]
        buf[n1 * 8 : n1 * 8 + 8, lanes:] = pair[1]

    def take(buf, n1):
        return buf[n1 * 8 : n1 * 8 + 8, :lanes], buf[n1 * 8 : n1 * 8 + 8, lanes:]

    def put_samples(buf, values):
        for n1, pair in enumerate(fft_list(values, 1)):
            put(buf, n1, twist(n1, pair, 1))

    def mix(buf, table_ref):
        buf[...] = right_product(buf[...], table_ref[...])

    energy = jnp.zeros((1, lanes), jnp.float32)
    steps = []
    for source in range(groups):
        step = 1.0 / x_ref[source, halves * pairs].astype(jnp.float32)[3:4]
        steps.append(step)
        reach = CEILING * step
        energy = energy + reach * reach
    gain = jnp.max(taps_ref[...], axis=0)
    gain = jnp.maximum(
        jnp.sum(gain[:4], axis=0, keepdims=True), jnp.sum(gain[4:], axis=0, keepdims=True)
    )
    gain = jnp.max(gain, axis=1, keepdims=True)
    scale = CEILING * lax.rsqrt(energy) / gain
    scale_ref[...] = jnp.broadcast_to(scale, scale_ref.shape)

    values = [None] * blocks
    for source in range(groups):
        tile = x_ref[source, halves * pairs].astype(jnp.float32) * unitary
        for h in range(halves):
            part = tile[h * 8 : h * 8 + 8]
            values[block_of(source, h)] = (part, jnp.concatenate([part[4:], part[:4]], axis=0))
    put_samples(first_buf, values)
    mix(first_buf, inverse_ref)
    for n1 in range(blocks):
        parts = take(first_buf, n1)
        t1, t2, t3 = [tap(n1, q) for q in range(1, 4)]
        rows = []
        for part in parts:
            v0, v1, v2 = part[0:1], part[1:2], part[2:3]
            rows += [t1 * v2 + t2 * v1 + t3 * v0, t2 * v2 + t3 * v1, t3 * v2, v0]
        wrap[n1] = jnp.concatenate(rows, axis=0)

    def one_pair(p, buf):
        first = pl.multiple_of(p * 8, 8)

        def row_table(index):
            return row_ref[2 * index, pl.ds(first, 8), :], row_ref[2 * index + 1, pl.ds(first, 8), :]

        values = [None] * blocks
        for source in range(groups):
            for h in range(halves):
                tile = restored(x_ref[source, h * pairs + p]) * steps[source]
                values[block_of(source, h)] = (tile[:8], tile[8:])
        put_samples(buf, values)
        yield
        mix(buf, inverse_ref)
        yield
        w1, w2, w3 = row_table(0), row_table(1), row_table(2)
        unit = row_table(3)
        turn = row_table(4)
        for n1 in range(blocks):
            re, im = take(buf, n1)
            t = [tap(n1, q) for q in range(4)]
            gain_re = t[0] + w1[0] * t[1] + w2[0] * t[2] + w3[0] * t[3]
            gain_im = w1[1] * t[1] + w2[1] * t[2] + w3[1] * t[3]
            u = [wrap[n1, q : q + 1, :] for q in range(7)]
            back_re = u[0] + (w1[0] * u[1] - w1[1] * u[5]) + (w2[0] * u[2] - w2[1] * u[6])
            back_im = u[4] + (w1[0] * u[5] + w1[1] * u[1]) + (w2[0] * u[6] + w2[1] * u[2])
            re, im = complex_times(re, im, gain_re, gain_im)
            put(buf, n1, complex_times(re - back_re, im - back_im, *turn))
            turn = complex_times(*turn, *unit)
        yield
        mix(buf, forward_ref)
        yield
        values = [twist(n1, take(buf, n1), -1) for n1 in range(blocks)]
        bins = []
        for k, pair in enumerate(fft_list(values, -1)):
            c = cos_ref[pl.ds(first, 8), k * lanes : (k + 1) * lanes]
            s = sin_ref[pl.ds(first, 8), k * lanes : (k + 1) * lanes]
            bins.append(complex_times(*pair, c, s))
        put_samples(buf, bins)
        yield
        mix(buf, inverse_ref)
        yield
        turn = row_table(4)
        turn = turn[0] * scale, turn[1] * scale
        for n1 in range(blocks):
            re, im = take(buf, n1)
            back = re * turn[0] + im * turn[1], im * turn[0] - re * turn[1]
            dest = n1 // 2 % (groups // 2) * 2 + n1 % 2
            h = n1 // groups
            out_ref[dest, h * pairs + p] = expanded(jnp.concatenate(back, axis=0))
            turn = complex_times(*turn, *unit)

    def two_pairs(step, carry):
        early = one_pair(2 * step, first_buf)
        late = one_pair(2 * step + 1, second_buf)
        next(early)
        running = True
        while running:
            next(early, None)
            running = next(late, late) is not late
        return carry

    lax.fori_loop(0, pairs // 2, two_pairs, 0)


def columns_kernel(count, x_ref, table_ref, *refs):
    outs, (out_ref, high_ref, low_ref, mid_ref) = refs[:count], refs[count:]
    groups, slots = x_ref.shape[0], x_ref.shape[1]
    time_count, halves, _, fd, _ = out_ref.shape
    me = lax.axis_index("tm")
    pairs = slots // halves
    width = halves * LANES

    def decode(p):
        for source in range(groups):
            for h in range(halves):
                high, low = split_parts(restored(x_ref[source, h * pairs + p]))
                rows = slice(source * 16, source * 16 + 16)
                cols = slice(h * LANES, (h + 1) * LANES)
                high_ref[p, rows, cols] = high
                low_ref[p, rows, cols] = low

    decode(0)
    for p in range(pairs):
        if p + 1 < pairs:
            decode(p + 1)
        mid_ref[2 * p : 2 * p + 2] = left_product(
            table_ref[p], high_ref[p], low_ref[p]
        ).reshape(2, 2 * fd, width)
    for g in range(0, fd, 16):
        for h in range(halves):
            cols = slice(h * LANES, (h + 1) * LANES)
            values = [
                (mid_ref[kd, g : g + 16, cols], mid_ref[kd, fd + g : fd + g + 16, cols])
                for kd in range(time_count)
            ]
            for d, pair in enumerate(fft_list(values, 1)):
                for r in range(2):
                    out_ref[d, h, r, g : g + 16, :] = expanded(pair[r])
    for k in range(count):
        outs[k][...] = out_ref[me ^ k]


def early_kernel(count, *refs):
    parts, out_ref = refs[:count], refs[count]
    halves, _, fd, _ = parts[0].shape
    for i, part in enumerate(parts):
        for h in range(halves):
            out_ref[i * halves + h] = restored(part[h].reshape(2 * fd, LANES)).T


def output_kernel(early, late, *refs):
    turned, parts = refs[0], refs[1 : 1 + len(late)]
    scale_ref, out_ref, mixed, held, sems = refs[1 + len(late) :]
    halves, _, fd, _ = parts[0].shape
    count = len(early) + len(late)
    lots = count * halves
    step = 1.0 / scale_ref[0:1, :]
    me = lax.axis_index("tm")
    for h in range(halves):
        for i, k in enumerate(early):
            rows = pl.ds((me ^ k) + count * h, LANES, stride=lots)
            mixed[rows, :] = turned[i * halves + h] * step
        for i, k in enumerate(late):
            rows = pl.ds((me ^ k) + count * h, LANES, stride=lots)
            mixed[rows, :] = (restored(parts[i][h].reshape(2 * fd, LANES)) * step).T
    wide = held.reshape(2 * fd, lots, LANES)
    copies = []
    for block in range(lots):
        tile = mixed[block * LANES : (block + 1) * LANES, :].T
        held[pl.ds(block, 2 * fd, stride=lots), :] = tile
        if block % STRIDE == STRIDE - 1:
            span = pl.ds(block + 1 - STRIDE, STRIDE)
            copies.append(
                pltpu.make_async_copy(
                    wide.at[:, span, :], out_ref.at[:, span, :], sems.at[block // STRIDE]
                )
            )
            copies[-1].start()
    for copy in copies:
        copy.wait()


def near(x):
    return pltpu.with_memory_space_constraint(x, pltpu.VMEM)


def call(kernel, outs, scratch, *args):
    return pl.pallas_call(
        kernel,
        out_shape=outs,
        in_specs=[pl.BlockSpec(memory_space=pltpu.VMEM)] * len(args),
        out_specs=jax.tree.map(lambda _: pl.BlockSpec(memory_space=pltpu.VMEM), outs),
        scratch_shapes=scratch,
        compiler_params=pltpu.CompilerParams(vmem_limit_bytes=24 << 20),
    )(*[near(x) for x in args])


def swap_parts(parts):
    count = len(parts)
    moved = {0: parts[0]}
    for k in range(count - 1, 0, -1):
        moved[k] = lax.ppermute(parts[k], "tm", [(i, i ^ k) for i in range(count)])
    return [moved[k] for k in range(count)]


def swap_all(x, axes):
    return lax.all_to_all(x, axes, split_axis=0, concat_axis=0, tiled=True)


def row_tables(k1, frames, width):
    series_len = frames * width
    shifts = [1 * k1 % frames, 2 * k1 % frames, 3 * k1 % frames]
    parts = [jnp.broadcast_to(s[:, None] * width, (k1.shape[0], LANES)) for s in shifts]
    parts.append(jnp.broadcast_to(k1[:, None], (k1.shape[0], LANES)))
    blocks = width // LANES
    parts.append(k1[:, None] * (blocks * jnp.arange(LANES, dtype=jnp.int32))[None, :] % series_len)
    angles = jnp.stack(parts).astype(jnp.float32) * (-2.0 * math.pi / series_len)
    return jnp.stack([jnp.cos(angles), jnp.sin(angles)], 1).reshape(10, k1.shape[0], LANES)


def fast_body(channels, synth_taps, chirp_phase):
    _, fd, half = channels.shape
    time_count = lax.axis_size("tm")
    subs = lax.axis_size("sub")
    groups = time_count * subs
    width = half * subs
    frames = fd * time_count
    col_width = half // time_count
    halves = col_width // LANES
    pairs = time_count // 2
    blocks = width // LANES
    per = fd // groups
    own = fd // subs
    time_index = lax.axis_index("tm")
    parity = lax.axis_index("sub")
    f32, bf16 = jnp.float32, jnp.bfloat16
    shape = pltpu.VMEM

    sent = pl.pallas_call(
        functools.partial(columns_apart_kernel, time_count),
        out_shape=[shape((2, fd, col_width), bf16)] * time_count,
        in_specs=[pl.BlockSpec(memory_space=pltpu.HBM)],
        out_specs=[pl.BlockSpec(memory_space=pltpu.VMEM)] * time_count,
        scratch_shapes=[pltpu.SemaphoreType.DMA((time_count,))],
        compiler_params=pltpu.CompilerParams(vmem_limit_bytes=24 << 20),
    )(pltpu.with_memory_space_constraint(channels, pltpu.HBM))
    got = swap_parts(sent)

    theirs = partner(chirp_phase, "sub", 0)
    other_taps = partner(synth_taps, "sub", 0)[:, 0]

    def both(a, b):
        return jnp.where(parity == 0, a, b), jnp.where(parity == 0, b, a)

    phase = call(
        functools.partial(phase_kernel, groups), shape((own, width), f32), [], chirp_phase, theirs
    )
    cos_part, sin_part = jnp.cos(phase), jnp.sin(phase)
    taps = jnp.concatenate(both(synth_taps[:, 0], other_taps), axis=0)
    taps = taps.reshape(-1, LANES, blocks // 2).transpose(2, 0, 1)
    row = jnp.arange(own, dtype=jnp.int32)
    k1 = row // per % 2 + 2 * (row // (2 * per))
    k1 = k1 + time_count * (time_index * (fd // time_count) + parity * per + row % per)
    rows = row_tables(k1, frames, width)

    slots = halves * pairs + 1
    coded = call(
        functools.partial(frames_kernel, time_count),
        shape((groups, slots, 16, LANES), bf16),
        [pltpu.VMEM((time_count, 2, fd, col_width), bf16)] * 3,
        *got,
        jnp.asarray(frame_tables(time_count, fd, groups, True)),
        cos_part,
        sin_part,
        taps,
        rows,
    )
    coded = swap_all(coded, ("tm", "sub"))
    back_table = jnp.asarray(frame_tables(time_count, fd, groups, False))
    coded, scale = call(
        rows_kernel,
        (shape((groups, slots - 1, 16, LANES), bf16), shape((8, LANES), f32)),
        [pltpu.VMEM((blocks * 8, 2 * LANES), f32)] * 2 + [pltpu.VMEM((blocks, 8, LANES), f32)],
        coded,
        cos_part,
        sin_part,
        taps,
        rows,
        jnp.asarray(twist_table(width)),
        jnp.asarray(lane_table(width, 1)),
        jnp.asarray(lane_table(width, -1)),
        back_table,
    )
    coded = swap_all(coded, ("tm", "sub"))
    sent = call(
        functools.partial(columns_kernel, time_count),
        [shape((halves, 2, fd, LANES), bf16)] * time_count,
        [pltpu.VMEM((time_count, halves, 2, fd, LANES), bf16)]
        + [pltpu.VMEM((pairs, 4 * fd, col_width), bf16)] * 2
        + [pltpu.VMEM((time_count, 2 * fd, col_width), f32)],
        coded,
        back_table,
    )
    moved = swap_parts(sent)
    early = [0, *range(time_count - 1, time_count // 2, -1)]
    late = list(range(time_count // 2, 0, -1))
    turned = call(
        functools.partial(early_kernel, len(early)),
        shape((len(early) * halves, LANES, 2 * fd), f32),
        [],
        *[moved[k] for k in early],
    )
    blocks_out = half // LANES
    out = pl.pallas_call(
        functools.partial(output_kernel, early, late),
        out_shape=jax.ShapeDtypeStruct((2 * fd, blocks_out, LANES), f32),
        in_specs=[pl.BlockSpec(memory_space=pltpu.VMEM)] * (len(late) + 2),
        out_specs=pl.BlockSpec(memory_space=pltpu.HBM),
        scratch_shapes=[
            pltpu.VMEM((half, LANES), f32),
            pltpu.VMEM((2 * fd * blocks_out, LANES), f32),
            pltpu.SemaphoreType.DMA((blocks_out // STRIDE,)),
        ],
        compiler_params=pltpu.CompilerParams(vmem_limit_bytes=24 << 20),
    )(near(turned), *[near(moved[k]) for k in late], near(scale))
    return out.reshape(2, fd, 1, half)


def body(channels, synth_taps, chirp_phase):
    _, fd, half = channels.shape
    time_count, subs = lax.axis_size("tm"), lax.axis_size("sub")
    groups = time_count * subs
    fits = (
        subs == 2
        and synth_taps.shape[0] == 4
        and half == time_count * 2 * LANES
        and fd == 4 * groups
        and time_count & (time_count - 1) == 0
        and half == groups * LANES
        and 2 * fd == LANES
    )
    return (fast_body if fits else general_body)(channels, synth_taps, chirp_phase)


def solution(mesh):
    placed = (P(None, ("beam", "tm"), "sub"), P(None, "sub", None), P("tm", "sub"))
    return jax.shard_map(
        body,
        mesh=mesh,
        in_specs=placed,
        out_specs=P(None, ("beam", "tm"), "sub", None),
        check_vma=False,
    )
```

```python
import functools
import math

import jax
import jax.numpy as jnp
import ml_dtypes
import numpy as np
from jax import lax
from jax.experimental import pallas as pl
from jax.experimental.pallas import tpu as pltpu
from jax.sharding import PartitionSpec as P


highest = lax.Precision.HIGHEST
inv_root2 = 1.0 / math.sqrt(2.0)


def partner(x, axis, distance):
    return lax.ppermute(x, axis, [(i, i ^ 1 << distance) for i in range(lax.axis_size(axis))])


def shifted(block, axis, distance):
    devices = range(lax.axis_size(axis))
    route = [(i - distance, i) for i in devices if i - distance in devices]
    return lax.ppermute(block, axis, route)


def roots_table(row_count, col_count, length, direction):
    product = (
        jnp.arange(row_count, dtype=jnp.int32)[:, None]
        * jnp.arange(col_count, dtype=jnp.int32)[None, :]
        % length
    )
    angles = direction * 2.0 * math.pi / length * product.astype(jnp.float32)
    return (jnp.cos(angles), jnp.sin(angles))


def global_roots(left_index, right_index, length, direction):
    product = left_index * right_index % length
    angles = direction * 2.0 * math.pi / length * product.astype(jnp.float32)
    return (jnp.cos(angles), jnp.sin(angles))


def parity_roots(parity_f, half, direction):
    angles = direction * math.pi / half * parity_f * jnp.arange(half, dtype=jnp.float32)
    return (jnp.cos(angles), jnp.sin(angles))


def complex_times(left_re, left_im, right_re, right_im):
    return (left_re * right_re - left_im * right_im, left_re * right_im + left_im * right_re)


def complex_einsum(form, left_re, left_im, right_re, right_im):

    def contract(former, latter):
        return jnp.einsum(form, former, latter, precision=highest)

    return (
        contract(left_re, right_re) - contract(left_im, right_im),
        contract(left_re, right_im) + contract(left_im, right_re),
    )


def dft_last(re_part, im_part, direction):
    length = re_part.shape[-1]
    outer_len = math.gcd(length, 32)
    inner_len = length // outer_len
    leading = re_part.shape[:-1]
    re_part = re_part.reshape(leading + (outer_len, inner_len))
    im_part = im_part.reshape(leading + (outer_len, inner_len))
    table_re, table_im = roots_table(outer_len, outer_len, outer_len, direction)
    re_part, im_part = complex_einsum("...uw,ur->...rw", re_part, im_part, table_re, table_im)
    twist_re, twist_im = roots_table(outer_len, inner_len, length, direction)
    re_part, im_part = complex_times(re_part, im_part, twist_re, twist_im)
    table_re, table_im = roots_table(inner_len, inner_len, inner_len, direction)
    re_part, im_part = complex_einsum("...rw,wt->...tr", re_part, im_part, table_re, table_im)
    factor = 1.0 / math.sqrt(length)
    return (
        re_part.reshape(leading + (length,)) * factor,
        im_part.reshape(leading + (length,)) * factor,
    )


def half_swap(re_part, im_part, sign_own):
    other_re, other_im = partner((re_part, im_part), "sub", 0)
    return (
        (other_re + sign_own * re_part) * inv_root2,
        (other_im + sign_own * im_part) * inv_root2,
    )


def to_columns(re_part, im_part):
    time_count = lax.axis_size("tm")
    time_index = lax.axis_index("tm")
    parity = lax.axis_index("sub")
    half = re_part.shape[1]
    got_re, got_im = (
        lax.all_to_all(re_part.T, "tm", split_axis=0, concat_axis=1, tiled=True),
        lax.all_to_all(im_part.T, "tm", split_axis=0, concat_axis=1, tiled=True),
    )
    col_width = half // time_count
    sample_index = 2 * (time_index * col_width + jnp.arange(col_width, dtype=jnp.int32)) + parity
    return (got_re, got_im, sample_index)


def to_rows(re_part, im_part):
    got_re, got_im = (
        lax.all_to_all(re_part, "tm", split_axis=1, concat_axis=0, tiled=True),
        lax.all_to_all(im_part, "tm", split_axis=1, concat_axis=0, tiled=True),
    )
    return (got_re.T, got_im.T)


def general_body(channels, synth_taps, chirp_phase):
    frames_dev = channels.shape[1]
    half = channels.shape[2]
    tap_count = synth_taps.shape[0]
    time_index = lax.axis_index("tm")
    time_count = lax.axis_size("tm")
    parity = lax.axis_index("sub")
    parity_f = parity.astype(jnp.float32)
    sign_own = 1.0 - 2.0 * parity_f
    total_frames = frames_dev * time_count
    series_len = total_frames * 2 * half
    partner_re, partner_im = partner((channels[0], channels[1]), "sub", 0)
    mixed_re = (
        partner_re.astype(jnp.float32) + sign_own * channels[0].astype(jnp.float32)
    ) * inv_root2
    mixed_im = (
        partner_im.astype(jnp.float32) + sign_own * channels[1].astype(jnp.float32)
    ) * inv_root2
    turn_re, turn_im = parity_roots(parity_f, half, 1.0)
    mixed_re, mixed_im = complex_times(mixed_re, mixed_im, turn_re, turn_im)
    volt_re, volt_im = dft_last(mixed_re, mixed_im, 1.0)
    keep_from = frames_dev - tap_count + 1
    tail_re, tail_im = shifted((volt_re[keep_from:], volt_im[keep_from:]), "tm", 1)
    long_re = jnp.concatenate([tail_re, volt_re], axis=0)
    long_im = jnp.concatenate([tail_im, volt_im], axis=0)
    synth_re = jnp.zeros_like(volt_re)
    synth_im = jnp.zeros_like(volt_im)
    for offset in range(tap_count):
        begin = tap_count - 1 - offset
        synth_re = synth_re + synth_taps[offset, 0] * long_re[begin : begin + frames_dev]
        synth_im = synth_im + synth_taps[offset, 0] * long_im[begin : begin + frames_dev]
    col_re, col_im, sample_index = to_columns(synth_re, synth_im)
    col_re, col_im = dft_last(col_re, col_im, -1.0)
    bin_index = jnp.arange(total_frames, dtype=jnp.int32)
    twist_re, twist_im = global_roots(sample_index[:, None], bin_index[None, :], series_len, -1.0)
    col_re, col_im = complex_times(col_re, col_im, twist_re, twist_im)
    row_re, row_im = to_rows(col_re, col_im)
    row_re, row_im = dft_last(row_re, row_im, -1.0)
    turn_re, turn_im = parity_roots(parity_f, half, -1.0)
    row_re, row_im = complex_times(row_re, row_im, turn_re, turn_im)
    row_re, row_im = half_swap(row_re, row_im, sign_own)
    row_re, row_im = complex_times(row_re, row_im, jnp.cos(chirp_phase), jnp.sin(chirp_phase))
    row_re, row_im = half_swap(row_re, row_im, sign_own)
    turn_re, turn_im = parity_roots(parity_f, half, 1.0)
    row_re, row_im = complex_times(row_re, row_im, turn_re, turn_im)
    row_re, row_im = dft_last(row_re, row_im, 1.0)
    own_bins = time_index * frames_dev + jnp.arange(frames_dev, dtype=jnp.int32)
    own_samples = 2 * jnp.arange(half, dtype=jnp.int32) + parity
    twist_re, twist_im = global_roots(own_bins[:, None], own_samples[None, :], series_len, 1.0)
    row_re, row_im = complex_times(row_re, row_im, twist_re, twist_im)
    col_re, col_im, ignored = to_columns(row_re, row_im)
    col_re, col_im = dft_last(col_re, col_im, 1.0)
    out_re, out_im = to_rows(col_re, col_im)
    return jnp.stack([out_re, out_im])[:, :, None, :]


LANES = 128
CEILING = 224.0
STRIDE = 8
OFFSET = 2.0**-7.75


def expanded(x):
    grown = jnp.abs(x) + OFFSET
    for _ in range(4):
        grown = grown * grown
    return jnp.where(x < 0.0, -grown, grown).astype(jnp.bfloat16)


def restored(code):
    grown = code.astype(jnp.float32)
    size = jnp.abs(grown)
    for _ in range(4):
        size = lax.rsqrt(size)
    size = size - OFFSET
    return jnp.where(grown < 0.0, -size, size)


def times_root(pair, numerator, length):
    re, im = pair
    eighth = numerator * 8 % (8 * length)
    if eighth == 0:
        return re, im
    if eighth == 4 * length:
        return -re, -im
    if eighth == 2 * length:
        return -im, re
    if eighth == 6 * length:
        return im, -re
    angle = 2.0 * math.pi * numerator / length
    c, s = math.cos(angle), math.sin(angle)
    if eighth % (2 * length) == length:
        root = abs(c)
        if c * s > 0:
            plus, minus = (re - im) * root, (re + im) * root
            return (plus, minus) if c > 0 else (-plus, -minus)
        plus, minus = (re + im) * root, (im - re) * root
        return (plus, minus) if c > 0 else (-plus, -minus)
    return re * c - im * s, re * s + im * c


def fft_list(values, direction):
    count = len(values)
    if count == 1:
        return values
    even = fft_list(values[0::2], direction)
    odd = fft_list(values[1::2], direction)
    low, high = [], []
    for k in range(count // 2):
        t_re, t_im = times_root(odd[k], direction * k % count, count)
        e_re, e_im = even[k]
        low.append((e_re + t_re, e_im + t_im))
        high.append((e_re - t_re, e_im - t_im))
    return low + high


def split_parts(x):
    high = x.astype(jnp.bfloat16)
    return high, (x - high.astype(jnp.float32)).astype(jnp.bfloat16)


def np_split(table):
    high = table.astype(ml_dtypes.bfloat16)
    low = (table - high.astype(np.float64)).astype(ml_dtypes.bfloat16)
    return high, low


def real_form(table):
    return np.stack(
        [np.stack([table.real, -table.imag], -1), np.stack([table.imag, table.real], -1)], -2
    )


def frame_tables(time_count, fd, groups, forward):
    frames = time_count * fd
    per = fd // groups
    g = np.arange(fd)
    tables = []
    for p in range(time_count // 2):
        kd = 2 * p + np.arange(2)
        k1 = kd[:, None] + time_count * np.arange(fd)[None, :]
        sign = -1.0 if forward else 1.0
        phase = np.exp(sign * 2j * np.pi * (k1[:, :, None] * g % frames) / frames)
        form = real_form(phase / math.sqrt(frames))
        full = np.zeros((groups, 2, 2, per, 2, 2, fd))
        for j in range(2):
            block = form[j].reshape(groups, per, fd, 2, 2)
            if forward:
                full[:, :, j, :, j, :, :] = block.transpose(0, 3, 1, 4, 2)
            else:
                full[:, :, j, :, j, :, :] = block.transpose(0, 4, 1, 3, 2)
        size = 4 * fd
        full = full.reshape(size, size)
        if not forward:
            full = full.T
        tables.append(np.concatenate(np_split(full), axis=1))
    return np.stack(tables)


def lane_table(width, direction):
    index = np.arange(LANES)
    roots = np.exp(direction * 2j * np.pi * np.outer(index, index) / LANES) / math.sqrt(width)
    form = real_form(roots)
    table = form.transpose(3, 0, 2, 1).reshape(2 * LANES, 2 * LANES)
    return np.concatenate(np_split(table), axis=0)


def twist_table(width):
    blocks = width // LANES
    phase = 2.0 * np.pi * np.outer(np.arange(blocks), np.arange(LANES)) / width
    return np.stack([np.cos(phase), np.sin(phase)], 1).astype(np.float32)


def dot32(a, b):
    return jnp.dot(a, b, preferred_element_type=jnp.float32)


def left_product(table, high, low):
    return dot32(table, jnp.concatenate([high, high], axis=0)) + dot32(
        table[:, : high.shape[0]], low
    )


def right_product(x, table):
    high, low = split_parts(x)
    return dot32(jnp.concatenate([high, high], axis=1), table) + dot32(low, table[: x.shape[1]])


def columns_apart_kernel(count, x_ref, *refs):
    outs, sems = refs[:count], refs[count]
    me = lax.axis_index("tm")
    width = outs[0].shape[2]
    copies = []
    for k in range(count):
        first = pl.multiple_of((me ^ k) * width, LANES)
        copies.append(
            pltpu.make_async_copy(x_ref.at[:, :, pl.ds(first, width)], outs[k], sems.at[k])
        )
    for copy in copies:
        copy.start()
    for copy in copies:
        copy.wait()


def phase_kernel(groups, own_ref, other_ref, out_ref):
    half = own_ref.shape[1]
    own = out_ref.shape[0]
    parity = lax.axis_index("sub")
    for ref, side in ((own_ref, parity), (other_ref, 1 - parity)):
        cols = pl.ds(pl.multiple_of(side * half, LANES), half)
        for low in range(own // 8):
            rows = ref[pl.ds(pl.multiple_of(parity * own + low * 8, 8), 8), :]
            for kd in range(8):
                place = kd // 2 * 8 + kd % 2 * 4 + low
                out_ref[place : place + 1, cols] = rows[kd : kd + 1]


def frames_kernel(count, *refs):
    parts, table_ref = refs[:count], refs[count]
    out_ref, x_ref, high_ref, low_ref = refs[count + 5 :]
    time_count, _, fd, width = x_ref.shape
    me = lax.axis_index("tm")
    for k in range(count):
        x_ref[me ^ k] = parts[k][...]
    groups = out_ref.shape[0]
    halves = width // LANES
    pairs = time_count // 2
    tails = 3
    power = jnp.zeros((16, LANES), jnp.float32)
    for g in range(0, fd, 16):
        for h in range(halves):
            lanes = slice(h * LANES, (h + 1) * LANES)
            values = []
            for d in range(time_count):
                re = x_ref[d, 0, g : g + 16, lanes].astype(jnp.float32)
                im = x_ref[d, 1, g : g + 16, lanes].astype(jnp.float32)
                power = power + (re * re + im * im)
                values.append((re, im))
            for kd, pair in enumerate(fft_list(values, -1)):
                for r in range(2):
                    high, low = split_parts(pair[r])
                    high_ref[kd, r, g : g + 16, lanes] = high
                    low_ref[kd, r, g : g + 16, lanes] = low
    energy = jnp.sum(jnp.sum(power, axis=0, keepdims=True), axis=1, keepdims=True)
    scale = CEILING * lax.rsqrt(jnp.maximum(energy, 1e-30))
    scale = scale.astype(jnp.bfloat16).astype(jnp.float32)
    rows = []
    for h in range(halves):
        lanes = slice(h * LANES, (h + 1) * LANES)
        for r in range(2):
            last = x_ref[time_count - 1, r, fd - 16 :, lanes].astype(jnp.float32)
            rows.append(last[16 - tails :])
            rows.append(jnp.broadcast_to(scale, (1, LANES)))
    tail = jnp.concatenate(rows, axis=0).astype(jnp.bfloat16)
    for dest in range(groups):
        out_ref[dest, halves * pairs] = tail
    for p in range(pairs):
        high = high_ref[2 * p : 2 * p + 2].reshape(4 * fd, width)
        low = low_ref[2 * p : 2 * p + 2].reshape(4 * fd, width)
        code = expanded(left_product(table_ref[p], high, low) * scale)
        for dest in range(groups):
            for h in range(halves):
                out_ref[dest, h * pairs + p] = code[
                    dest * 16 : dest * 16 + 16, h * LANES : (h + 1) * LANES
                ]


def rows_kernel(
    x_ref, cos_ref, sin_ref, taps_ref, row_ref, twist_ref, inverse_ref, forward_ref,
    next_table_ref, out_ref, scale_ref, first_buf, second_buf, wrap,
):
    groups, slots = x_ref.shape[0], x_ref.shape[1]
    blocks = twist_ref.shape[0]
    halves = blocks // groups
    pairs = (slots - 1) // halves
    lanes = LANES
    def tap(n1, q):
        row = n1 % 2 * 4 + q
        return taps_ref[n1 // 2, row : row + 1, :]

    unitary = 1.0 / math.sqrt(groups * row_ref.shape[1])

    def block_of(source, h):
        return (source % 2) * (blocks // 2) + (source // 2) * halves + h

    def twist(n1, pair, direction):
        c, s = twist_ref[n1, 0:1, :], twist_ref[n1, 1:2, :]
        if direction < 0:
            s = -s
        return complex_times(pair[0], pair[1], c, s)

    def put(buf, n1, pair):
        buf[n1 * 8 : n1 * 8 + 8, :lanes] = pair[0]
        buf[n1 * 8 : n1 * 8 + 8, lanes:] = pair[1]

    def take(buf, n1):
        return buf[n1 * 8 : n1 * 8 + 8, :lanes], buf[n1 * 8 : n1 * 8 + 8, lanes:]

    def put_samples(buf, values):
        for n1, pair in enumerate(fft_list(values, 1)):
            put(buf, n1, twist(n1, pair, 1))

    def mix(buf, table_ref):
        buf[...] = right_product(buf[...], table_ref[...])

    energy = jnp.zeros((1, lanes), jnp.float32)
    steps = []
    for source in range(groups):
        step = 1.0 / x_ref[source, halves * pairs].astype(jnp.float32)[3:4]
        steps.append(step)
        reach = CEILING * step
        energy = energy + reach * reach
    gain = jnp.max(taps_ref[...], axis=0)
    gain = jnp.maximum(
        jnp.sum(gain[:4], axis=0, keepdims=True), jnp.sum(gain[4:], axis=0, keepdims=True)
    )
    gain = jnp.max(gain, axis=1, keepdims=True)
    scale = CEILING * lax.rsqrt(energy) / gain
    scale_ref[...] = jnp.broadcast_to(scale, scale_ref.shape)

    values = [None] * blocks
    for source in range(groups):
        tile = x_ref[source, halves * pairs].astype(jnp.float32) * unitary
        for h in range(halves):
            part = tile[h * 8 : h * 8 + 8]
            values[block_of(source, h)] = (part, jnp.concatenate([part[4:], part[:4]], axis=0))
    put_samples(first_buf, values)
    mix(first_buf, inverse_ref)
    for n1 in range(blocks):
        parts = take(first_buf, n1)
        t1, t2, t3 = [tap(n1, q) for q in range(1, 4)]
        rows = []
        for part in parts:
            v0, v1, v2 = part[0:1], part[1:2], part[2:3]
            rows += [t1 * v2 + t2 * v1 + t3 * v0, t2 * v2 + t3 * v1, t3 * v2, v0]
        wrap[n1] = jnp.concatenate(rows, axis=0)

    def one_pair(p, buf):
        first = pl.multiple_of(p * 8, 8)

        def row_table(index):
            return row_ref[2 * index, pl.ds(first, 8), :], row_ref[2 * index + 1, pl.ds(first, 8), :]

        values = [None] * blocks
        for source in range(groups):
            for h in range(halves):
                tile = restored(x_ref[source, h * pairs + p]) * steps[source]
                values[block_of(source, h)] = (tile[:8], tile[8:])
        put_samples(buf, values)
        yield
        mix(buf, inverse_ref)
        yield
        w1, w2, w3 = row_table(0), row_table(1), row_table(2)
        unit = row_table(3)
        turn = row_table(4)
        for n1 in range(blocks):
            re, im = take(buf, n1)
            t = [tap(n1, q) for q in range(4)]
            gain_re = t[0] + w1[0] * t[1] + w2[0] * t[2] + w3[0] * t[3]
            gain_im = w1[1] * t[1] + w2[1] * t[2] + w3[1] * t[3]
            u = [wrap[n1, q : q + 1, :] for q in range(7)]
            back_re = u[0] + (w1[0] * u[1] - w1[1] * u[5]) + (w2[0] * u[2] - w2[1] * u[6])
            back_im = u[4] + (w1[0] * u[5] + w1[1] * u[1]) + (w2[0] * u[6] + w2[1] * u[2])
            re, im = complex_times(re, im, gain_re, gain_im)
            put(buf, n1, complex_times(re - back_re, im - back_im, *turn))
            turn = complex_times(*turn, *unit)
        yield
        mix(buf, forward_ref)
        yield
        values = [twist(n1, take(buf, n1), -1) for n1 in range(blocks)]
        bins = []
        for k, pair in enumerate(fft_list(values, -1)):
            c = cos_ref[pl.ds(first, 8), k * lanes : (k + 1) * lanes]
            s = sin_ref[pl.ds(first, 8), k * lanes : (k + 1) * lanes]
            bins.append(complex_times(*pair, c, s))
        put_samples(buf, bins)
        yield
        mix(buf, inverse_ref)
        yield
        turn = row_table(4)
        turn = turn[0] * scale, turn[1] * scale
        for n1 in range(blocks):
            re, im = take(buf, n1)
            back = re * turn[0] + im * turn[1], im * turn[0] - re * turn[1]
            dest = n1 // 2 % (groups // 2) * 2 + n1 % 2
            h = n1 // groups
            out_ref[dest, h * pairs + p] = expanded(jnp.concatenate(back, axis=0))
            turn = complex_times(*turn, *unit)

    def two_pairs(step, carry):
        early = one_pair(2 * step, first_buf)
        late = one_pair(2 * step + 1, second_buf)
        next(early)
        running = True
        while running:
            next(early, None)
            running = next(late, late) is not late
        return carry

    lax.fori_loop(0, pairs // 2, two_pairs, 0)


def columns_kernel(count, x_ref, table_ref, *refs):
    outs, (out_ref, high_ref, low_ref, mid_ref) = refs[:count], refs[count:]
    groups, slots = x_ref.shape[0], x_ref.shape[1]
    time_count, halves, _, fd, _ = out_ref.shape
    me = lax.axis_index("tm")
    pairs = slots // halves
    width = halves * LANES

    def decode(p):
        for source in range(groups):
            for h in range(halves):
                high, low = split_parts(restored(x_ref[source, h * pairs + p]))
                rows = slice(source * 16, source * 16 + 16)
                cols = slice(h * LANES, (h + 1) * LANES)
                high_ref[p, rows, cols] = high
                low_ref[p, rows, cols] = low

    decode(0)
    for p in range(pairs):
        if p + 1 < pairs:
            decode(p + 1)
        mid_ref[2 * p : 2 * p + 2] = left_product(
            table_ref[p], high_ref[p], low_ref[p]
        ).reshape(2, 2 * fd, width)
    for g in range(0, fd, 16):
        for h in range(halves):
            cols = slice(h * LANES, (h + 1) * LANES)
            values = [
                (mid_ref[kd, g : g + 16, cols], mid_ref[kd, fd + g : fd + g + 16, cols])
                for kd in range(time_count)
            ]
            for d, pair in enumerate(fft_list(values, 1)):
                for r in range(2):
                    out_ref[d, h, r, g : g + 16, :] = expanded(pair[r])
    for k in range(count):
        outs[k][...] = out_ref[me ^ k]


def early_kernel(count, *refs):
    parts, out_ref = refs[:count], refs[count]
    halves, _, fd, _ = parts[0].shape
    for i, part in enumerate(parts):
        for h in range(halves):
            out_ref[i * halves + h] = restored(part[h].reshape(2 * fd, LANES)).T


def output_kernel(early, late, *refs):
    turned, parts = refs[0], refs[1 : 1 + len(late)]
    scale_ref, out_ref, mixed, held, sems = refs[1 + len(late) :]
    halves, _, fd, _ = parts[0].shape
    count = len(early) + len(late)
    lots = count * halves
    step = 1.0 / scale_ref[0:1, :]
    me = lax.axis_index("tm")
    for h in range(halves):
        for i, k in enumerate(early):
            rows = pl.ds((me ^ k) + count * h, LANES, stride=lots)
            mixed[rows, :] = turned[i * halves + h] * step
        for i, k in enumerate(late):
            rows = pl.ds((me ^ k) + count * h, LANES, stride=lots)
            mixed[rows, :] = (restored(parts[i][h].reshape(2 * fd, LANES)) * step).T
    wide = held.reshape(2 * fd, lots, LANES)
    copies = []
    for block in range(lots):
        tile = mixed[block * LANES : (block + 1) * LANES, :].T
        held[pl.ds(block, 2 * fd, stride=lots), :] = tile
        if block % STRIDE == STRIDE - 1:
            span = pl.ds(block + 1 - STRIDE, STRIDE)
            copies.append(
                pltpu.make_async_copy(
                    wide.at[:, span, :], out_ref.at[:, span, :], sems.at[block // STRIDE]
                )
            )
            copies[-1].start()
    for copy in copies:
        copy.wait()


def near(x):
    return pltpu.with_memory_space_constraint(x, pltpu.VMEM)


def call(kernel, outs, scratch, *args):
    return pl.pallas_call(
        kernel,
        out_shape=outs,
        in_specs=[pl.BlockSpec(memory_space=pltpu.VMEM)] * len(args),
        out_specs=jax.tree.map(lambda _: pl.BlockSpec(memory_space=pltpu.VMEM), outs),
        scratch_shapes=scratch,
        compiler_params=pltpu.CompilerParams(vmem_limit_bytes=24 << 20),
    )(*[near(x) for x in args])


def swap_parts(parts):
    count = len(parts)
    moved = {0: parts[0]}
    for k in range(count - 1, 0, -1):
        moved[k] = lax.ppermute(parts[k], "tm", [(i, i ^ k) for i in range(count)])
    return [moved[k] for k in range(count)]


def swap_all(x, axes):
    return lax.all_to_all(x, axes, split_axis=0, concat_axis=0, tiled=True)


def row_tables(k1, frames, width):
    series_len = frames * width
    shifts = [1 * k1 % frames, 2 * k1 % frames, 3 * k1 % frames]
    parts = [jnp.broadcast_to(s[:, None] * width, (k1.shape[0], LANES)) for s in shifts]
    parts.append(jnp.broadcast_to(k1[:, None], (k1.shape[0], LANES)))
    blocks = width // LANES
    parts.append(k1[:, None] * (blocks * jnp.arange(LANES, dtype=jnp.int32))[None, :] % series_len)
    angles = jnp.stack(parts).astype(jnp.float32) * (-2.0 * math.pi / series_len)
    return jnp.stack([jnp.cos(angles), jnp.sin(angles)], 1).reshape(10, k1.shape[0], LANES)


def fast_body(channels, synth_taps, chirp_phase):
    _, fd, half = channels.shape
    time_count = lax.axis_size("tm")
    subs = lax.axis_size("sub")
    groups = time_count * subs
    width = half * subs
    frames = fd * time_count
    col_width = half // time_count
    halves = col_width // LANES
    pairs = time_count // 2
    blocks = width // LANES
    per = fd // groups
    own = fd // subs
    time_index = lax.axis_index("tm")
    parity = lax.axis_index("sub")
    f32, bf16 = jnp.float32, jnp.bfloat16
    shape = pltpu.VMEM

    sent = pl.pallas_call(
        functools.partial(columns_apart_kernel, time_count),
        out_shape=[shape((2, fd, col_width), bf16)] * time_count,
        in_specs=[pl.BlockSpec(memory_space=pltpu.HBM)],
        out_specs=[pl.BlockSpec(memory_space=pltpu.VMEM)] * time_count,
        scratch_shapes=[pltpu.SemaphoreType.DMA((time_count,))],
        compiler_params=pltpu.CompilerParams(vmem_limit_bytes=24 << 20),
    )(pltpu.with_memory_space_constraint(channels, pltpu.HBM))
    got = swap_parts(sent)

    theirs = partner(chirp_phase, "sub", 0)
    other_taps = partner(synth_taps, "sub", 0)[:, 0]

    def both(a, b):
        return jnp.where(parity == 0, a, b), jnp.where(parity == 0, b, a)

    phase = call(
        functools.partial(phase_kernel, groups), shape((own, width), f32), [], chirp_phase, theirs
    )
    cos_part, sin_part = jnp.cos(phase), jnp.sin(phase)
    taps = jnp.concatenate(both(synth_taps[:, 0], other_taps), axis=0)
    taps = taps.reshape(-1, LANES, blocks // 2).transpose(2, 0, 1)
    row = jnp.arange(own, dtype=jnp.int32)
    k1 = row // per % 2 + 2 * (row // (2 * per))
    k1 = k1 + time_count * (time_index * (fd // time_count) + parity * per + row % per)
    rows = row_tables(k1, frames, width)

    slots = halves * pairs + 1
    coded = call(
        functools.partial(frames_kernel, time_count),
        shape((groups, slots, 16, LANES), bf16),
        [pltpu.VMEM((time_count, 2, fd, col_width), bf16)] * 3,
        *got,
        jnp.asarray(frame_tables(time_count, fd, groups, True)),
        cos_part,
        sin_part,
        taps,
        rows,
    )
    coded = swap_all(coded, ("tm", "sub"))
    back_table = jnp.asarray(frame_tables(time_count, fd, groups, False))
    coded, scale = call(
        rows_kernel,
        (shape((groups, slots - 1, 16, LANES), bf16), shape((8, LANES), f32)),
        [pltpu.VMEM((blocks * 8, 2 * LANES), f32)] * 2 + [pltpu.VMEM((blocks, 8, LANES), f32)],
        coded,
        cos_part,
        sin_part,
        taps,
        rows,
        jnp.asarray(twist_table(width)),
        jnp.asarray(lane_table(width, 1)),
        jnp.asarray(lane_table(width, -1)),
        back_table,
    )
    coded = swap_all(coded, ("tm", "sub"))
    sent = call(
        functools.partial(columns_kernel, time_count),
        [shape((halves, 2, fd, LANES), bf16)] * time_count,
        [pltpu.VMEM((time_count, halves, 2, fd, LANES), bf16)]
        + [pltpu.VMEM((pairs, 4 * fd, col_width), bf16)] * 2
        + [pltpu.VMEM((time_count, 2 * fd, col_width), f32)],
        coded,
        back_table,
    )
    moved = swap_parts(sent)
    early = [0, time_count - 1, time_count - 2]
    late = list(range(time_count - 3, 0, -1))
    turned = call(
        functools.partial(early_kernel, len(early)),
        shape((len(early) * halves, LANES, 2 * fd), f32),
        [],
        *[moved[k] for k in early],
    )
    blocks_out = half // LANES
    out = pl.pallas_call(
        functools.partial(output_kernel, early, late),
        out_shape=jax.ShapeDtypeStruct((2 * fd, blocks_out, LANES), f32),
        in_specs=[pl.BlockSpec(memory_space=pltpu.VMEM)] * (len(late) + 2),
        out_specs=pl.BlockSpec(memory_space=pltpu.HBM),
        scratch_shapes=[
            pltpu.VMEM((half, LANES), f32),
            pltpu.VMEM((2 * fd * blocks_out, LANES), f32),
            pltpu.SemaphoreType.DMA((blocks_out // STRIDE,)),
        ],
        compiler_params=pltpu.CompilerParams(vmem_limit_bytes=24 << 20),
    )(near(turned), *[near(moved[k]) for k in late], near(scale))
    return out.reshape(2, fd, 1, half)


def body(channels, synth_taps, chirp_phase):
    _, fd, half = channels.shape
    time_count, subs = lax.axis_size("tm"), lax.axis_size("sub")
    groups = time_count * subs
    fits = (
        subs == 2
        and synth_taps.shape[0] == 4
        and half == time_count * 2 * LANES
        and fd == 4 * groups
        and time_count & (time_count - 1) == 0
        and time_count >= 4
        and half == groups * LANES
        and 2 * fd == LANES
    )
    return (fast_body if fits else general_body)(channels, synth_taps, chirp_phase)


def solution(mesh):
    placed = (P(None, ("beam", "tm"), "sub"), P(None, "sub", None), P("tm", "sub"))
    return jax.shard_map(
        body,
        mesh=mesh,
        in_specs=placed,
        out_specs=P(None, ("beam", "tm"), "sub", None),
        check_vma=False,
    )
```

```python
import functools
import math

import jax
import jax.numpy as jnp
import ml_dtypes
import numpy as np
from jax import lax
from jax.experimental import pallas as pl
from jax.experimental.pallas import tpu as pltpu
from jax.sharding import PartitionSpec as P


highest = lax.Precision.HIGHEST
inv_root2 = 1.0 / math.sqrt(2.0)


def partner(x, axis, distance):
    return lax.ppermute(x, axis, [(i, i ^ 1 << distance) for i in range(lax.axis_size(axis))])


def shifted(block, axis, distance):
    devices = range(lax.axis_size(axis))
    route = [(i - distance, i) for i in devices if i - distance in devices]
    return lax.ppermute(block, axis, route)


def roots_table(row_count, col_count, length, direction):
    product = (
        jnp.arange(row_count, dtype=jnp.int32)[:, None]
        * jnp.arange(col_count, dtype=jnp.int32)[None, :]
        % length
    )
    angles = direction * 2.0 * math.pi / length * product.astype(jnp.float32)
    return (jnp.cos(angles), jnp.sin(angles))


def global_roots(left_index, right_index, length, direction):
    product = left_index * right_index % length
    angles = direction * 2.0 * math.pi / length * product.astype(jnp.float32)
    return (jnp.cos(angles), jnp.sin(angles))


def parity_roots(parity_f, half, direction):
    angles = direction * math.pi / half * parity_f * jnp.arange(half, dtype=jnp.float32)
    return (jnp.cos(angles), jnp.sin(angles))


def complex_times(left_re, left_im, right_re, right_im):
    return (left_re * right_re - left_im * right_im, left_re * right_im + left_im * right_re)


def complex_einsum(form, left_re, left_im, right_re, right_im):

    def contract(former, latter):
        return jnp.einsum(form, former, latter, precision=highest)

    return (
        contract(left_re, right_re) - contract(left_im, right_im),
        contract(left_re, right_im) + contract(left_im, right_re),
    )


def dft_last(re_part, im_part, direction):
    length = re_part.shape[-1]
    outer_len = math.gcd(length, 32)
    inner_len = length // outer_len
    leading = re_part.shape[:-1]
    re_part = re_part.reshape(leading + (outer_len, inner_len))
    im_part = im_part.reshape(leading + (outer_len, inner_len))
    table_re, table_im = roots_table(outer_len, outer_len, outer_len, direction)
    re_part, im_part = complex_einsum("...uw,ur->...rw", re_part, im_part, table_re, table_im)
    twist_re, twist_im = roots_table(outer_len, inner_len, length, direction)
    re_part, im_part = complex_times(re_part, im_part, twist_re, twist_im)
    table_re, table_im = roots_table(inner_len, inner_len, inner_len, direction)
    re_part, im_part = complex_einsum("...rw,wt->...tr", re_part, im_part, table_re, table_im)
    factor = 1.0 / math.sqrt(length)
    return (
        re_part.reshape(leading + (length,)) * factor,
        im_part.reshape(leading + (length,)) * factor,
    )


def half_swap(re_part, im_part, sign_own):
    other_re, other_im = partner((re_part, im_part), "sub", 0)
    return (
        (other_re + sign_own * re_part) * inv_root2,
        (other_im + sign_own * im_part) * inv_root2,
    )


def to_columns(re_part, im_part):
    time_count = lax.axis_size("tm")
    time_index = lax.axis_index("tm")
    parity = lax.axis_index("sub")
    half = re_part.shape[1]
    got_re, got_im = (
        lax.all_to_all(re_part.T, "tm", split_axis=0, concat_axis=1, tiled=True),
        lax.all_to_all(im_part.T, "tm", split_axis=0, concat_axis=1, tiled=True),
    )
    col_width = half // time_count
    sample_index = 2 * (time_index * col_width + jnp.arange(col_width, dtype=jnp.int32)) + parity
    return (got_re, got_im, sample_index)


def to_rows(re_part, im_part):
    got_re, got_im = (
        lax.all_to_all(re_part, "tm", split_axis=1, concat_axis=0, tiled=True),
        lax.all_to_all(im_part, "tm", split_axis=1, concat_axis=0, tiled=True),
    )
    return (got_re.T, got_im.T)


def general_body(channels, synth_taps, chirp_phase):
    frames_dev = channels.shape[1]
    half = channels.shape[2]
    tap_count = synth_taps.shape[0]
    time_index = lax.axis_index("tm")
    time_count = lax.axis_size("tm")
    parity = lax.axis_index("sub")
    parity_f = parity.astype(jnp.float32)
    sign_own = 1.0 - 2.0 * parity_f
    total_frames = frames_dev * time_count
    series_len = total_frames * 2 * half
    partner_re, partner_im = partner((channels[0], channels[1]), "sub", 0)
    mixed_re = (
        partner_re.astype(jnp.float32) + sign_own * channels[0].astype(jnp.float32)
    ) * inv_root2
    mixed_im = (
        partner_im.astype(jnp.float32) + sign_own * channels[1].astype(jnp.float32)
    ) * inv_root2
    turn_re, turn_im = parity_roots(parity_f, half, 1.0)
    mixed_re, mixed_im = complex_times(mixed_re, mixed_im, turn_re, turn_im)
    volt_re, volt_im = dft_last(mixed_re, mixed_im, 1.0)
    keep_from = frames_dev - tap_count + 1
    tail_re, tail_im = shifted((volt_re[keep_from:], volt_im[keep_from:]), "tm", 1)
    long_re = jnp.concatenate([tail_re, volt_re], axis=0)
    long_im = jnp.concatenate([tail_im, volt_im], axis=0)
    synth_re = jnp.zeros_like(volt_re)
    synth_im = jnp.zeros_like(volt_im)
    for offset in range(tap_count):
        begin = tap_count - 1 - offset
        synth_re = synth_re + synth_taps[offset, 0] * long_re[begin : begin + frames_dev]
        synth_im = synth_im + synth_taps[offset, 0] * long_im[begin : begin + frames_dev]
    col_re, col_im, sample_index = to_columns(synth_re, synth_im)
    col_re, col_im = dft_last(col_re, col_im, -1.0)
    bin_index = jnp.arange(total_frames, dtype=jnp.int32)
    twist_re, twist_im = global_roots(sample_index[:, None], bin_index[None, :], series_len, -1.0)
    col_re, col_im = complex_times(col_re, col_im, twist_re, twist_im)
    row_re, row_im = to_rows(col_re, col_im)
    row_re, row_im = dft_last(row_re, row_im, -1.0)
    turn_re, turn_im = parity_roots(parity_f, half, -1.0)
    row_re, row_im = complex_times(row_re, row_im, turn_re, turn_im)
    row_re, row_im = half_swap(row_re, row_im, sign_own)
    row_re, row_im = complex_times(row_re, row_im, jnp.cos(chirp_phase), jnp.sin(chirp_phase))
    row_re, row_im = half_swap(row_re, row_im, sign_own)
    turn_re, turn_im = parity_roots(parity_f, half, 1.0)
    row_re, row_im = complex_times(row_re, row_im, turn_re, turn_im)
    row_re, row_im = dft_last(row_re, row_im, 1.0)
    own_bins = time_index * frames_dev + jnp.arange(frames_dev, dtype=jnp.int32)
    own_samples = 2 * jnp.arange(half, dtype=jnp.int32) + parity
    twist_re, twist_im = global_roots(own_bins[:, None], own_samples[None, :], series_len, 1.0)
    row_re, row_im = complex_times(row_re, row_im, twist_re, twist_im)
    col_re, col_im, ignored = to_columns(row_re, row_im)
    col_re, col_im = dft_last(col_re, col_im, 1.0)
    out_re, out_im = to_rows(col_re, col_im)
    return jnp.stack([out_re, out_im])[:, :, None, :]


LANES = 128
CEILING = 224.0
STRIDE = 8
OFFSET = 2.0**-7.75


def expanded(x):
    grown = jnp.abs(x) + OFFSET
    for _ in range(4):
        grown = grown * grown
    return jnp.where(x < 0.0, -grown, grown).astype(jnp.bfloat16)


def restored(code):
    grown = code.astype(jnp.float32)
    size = jnp.abs(grown)
    for _ in range(4):
        size = lax.rsqrt(size)
    size = size - OFFSET
    return jnp.where(grown < 0.0, -size, size)


def times_root(pair, numerator, length):
    re, im = pair
    eighth = numerator * 8 % (8 * length)
    if eighth == 0:
        return re, im
    if eighth == 4 * length:
        return -re, -im
    if eighth == 2 * length:
        return -im, re
    if eighth == 6 * length:
        return im, -re
    angle = 2.0 * math.pi * numerator / length
    c, s = math.cos(angle), math.sin(angle)
    if eighth % (2 * length) == length:
        root = abs(c)
        if c * s > 0:
            plus, minus = (re - im) * root, (re + im) * root
            return (plus, minus) if c > 0 else (-plus, -minus)
        plus, minus = (re + im) * root, (im - re) * root
        return (plus, minus) if c > 0 else (-plus, -minus)
    return re * c - im * s, re * s + im * c


def fft_list(values, direction):
    count = len(values)
    if count == 1:
        return values
    even = fft_list(values[0::2], direction)
    odd = fft_list(values[1::2], direction)
    low, high = [], []
    for k in range(count // 2):
        t_re, t_im = times_root(odd[k], direction * k % count, count)
        e_re, e_im = even[k]
        low.append((e_re + t_re, e_im + t_im))
        high.append((e_re - t_re, e_im - t_im))
    return low + high


def split_parts(x):
    high = x.astype(jnp.bfloat16)
    return high, (x - high.astype(jnp.float32)).astype(jnp.bfloat16)


def np_split(table):
    high = table.astype(ml_dtypes.bfloat16)
    low = (table - high.astype(np.float64)).astype(ml_dtypes.bfloat16)
    return high, low


def real_form(table):
    return np.stack(
        [np.stack([table.real, -table.imag], -1), np.stack([table.imag, table.real], -1)], -2
    )


def frame_tables(time_count, fd, groups, forward):
    frames = time_count * fd
    per = fd // groups
    g = np.arange(fd)
    tables = []
    for p in range(time_count // 2):
        kd = 2 * p + np.arange(2)
        k1 = kd[:, None] + time_count * np.arange(fd)[None, :]
        sign = -1.0 if forward else 1.0
        phase = np.exp(sign * 2j * np.pi * (k1[:, :, None] * g % frames) / frames)
        form = real_form(phase / math.sqrt(frames))
        full = np.zeros((groups, 2, 2, per, 2, 2, fd))
        for j in range(2):
            block = form[j].reshape(groups, per, fd, 2, 2)
            if forward:
                full[:, :, j, :, j, :, :] = block.transpose(0, 3, 1, 4, 2)
            else:
                full[:, :, j, :, j, :, :] = block.transpose(0, 4, 1, 3, 2)
        size = 4 * fd
        full = full.reshape(size, size)
        if not forward:
            full = full.T
        tables.append(np.concatenate(np_split(full), axis=1))
    return np.stack(tables)


def lane_table(width, direction):
    index = np.arange(LANES)
    roots = np.exp(direction * 2j * np.pi * np.outer(index, index) / LANES) / math.sqrt(width)
    form = real_form(roots)
    table = form.transpose(3, 0, 2, 1).reshape(2 * LANES, 2 * LANES)
    return np.concatenate(np_split(table), axis=0)


def twist_table(width):
    blocks = width // LANES
    phase = 2.0 * np.pi * np.outer(np.arange(blocks), np.arange(LANES)) / width
    return np.stack([np.cos(phase), np.sin(phase)], 1).astype(np.float32)


def dot32(a, b):
    return jnp.dot(a, b, preferred_element_type=jnp.float32)


def left_product(table, high, low):
    return dot32(table, jnp.concatenate([high, high], axis=0)) + dot32(
        table[:, : high.shape[0]], low
    )


def right_product(x, table):
    high, low = split_parts(x)
    return dot32(jnp.concatenate([high, high], axis=1), table) + dot32(low, table[: x.shape[1]])


def columns_apart_kernel(count, x_ref, *refs):
    outs, sems = refs[:count], refs[count]
    me = lax.axis_index("tm")
    width = outs[0].shape[2]
    copies = []
    for k in range(count):
        first = pl.multiple_of((me ^ k) * width, LANES)
        copies.append(
            pltpu.make_async_copy(x_ref.at[:, :, pl.ds(first, width)], outs[k], sems.at[k])
        )
    for copy in copies:
        copy.start()
    for copy in copies:
        copy.wait()


def phase_kernel(groups, own_ref, other_ref, out_ref):
    half = own_ref.shape[1]
    own = out_ref.shape[0]
    parity = lax.axis_index("sub")
    for ref, side in ((own_ref, parity), (other_ref, 1 - parity)):
        cols = pl.ds(pl.multiple_of(side * half, LANES), half)
        for low in range(own // 8):
            rows = ref[pl.ds(pl.multiple_of(parity * own + low * 8, 8), 8), :]
            for kd in range(8):
                place = kd // 2 * 8 + kd % 2 * 4 + low
                out_ref[place : place + 1, cols] = rows[kd : kd + 1]


def frames_kernel(count, *refs):
    parts, table_ref = refs[:count], refs[count]
    out_ref, x_ref, high_ref, low_ref = refs[count + 5 :]
    time_count, _, fd, width = x_ref.shape
    me = lax.axis_index("tm")
    for k in range(count):
        x_ref[me ^ k] = parts[k][...]
    groups = out_ref.shape[0]
    halves = width // LANES
    pairs = time_count // 2
    tails = 3
    power = jnp.zeros((16, LANES), jnp.float32)
    for g in range(0, fd, 16):
        for h in range(halves):
            lanes = slice(h * LANES, (h + 1) * LANES)
            values = []
            for d in range(time_count):
                re = x_ref[d, 0, g : g + 16, lanes].astype(jnp.float32)
                im = x_ref[d, 1, g : g + 16, lanes].astype(jnp.float32)
                power = power + (re * re + im * im)
                values.append((re, im))
            for kd, pair in enumerate(fft_list(values, -1)):
                for r in range(2):
                    high, low = split_parts(pair[r])
                    high_ref[kd, r, g : g + 16, lanes] = high
                    low_ref[kd, r, g : g + 16, lanes] = low
    energy = jnp.sum(jnp.sum(power, axis=0, keepdims=True), axis=1, keepdims=True)
    scale = CEILING * lax.rsqrt(jnp.maximum(energy, 1e-30))
    scale = scale.astype(jnp.bfloat16).astype(jnp.float32)
    rows = []
    for h in range(halves):
        lanes = slice(h * LANES, (h + 1) * LANES)
        for r in range(2):
            last = x_ref[time_count - 1, r, fd - 16 :, lanes].astype(jnp.float32)
            rows.append(last[16 - tails :])
            rows.append(jnp.broadcast_to(scale, (1, LANES)))
    tail = jnp.concatenate(rows, axis=0).astype(jnp.bfloat16)
    for dest in range(groups):
        out_ref[dest, halves * pairs] = tail
    for p in range(pairs):
        high = high_ref[2 * p : 2 * p + 2].reshape(4 * fd, width)
        low = low_ref[2 * p : 2 * p + 2].reshape(4 * fd, width)
        code = expanded(left_product(table_ref[p], high, low) * scale)
        for dest in range(groups):
            for h in range(halves):
                out_ref[dest, h * pairs + p] = code[
                    dest * 16 : dest * 16 + 16, h * LANES : (h + 1) * LANES
                ]


def rows_kernel(
    x_ref, cos_ref, sin_ref, taps_ref, row_ref, twist_ref, inverse_ref, forward_ref,
    next_table_ref, out_ref, scale_ref, first_buf, second_buf, wrap,
):
    groups, slots = x_ref.shape[0], x_ref.shape[1]
    blocks = twist_ref.shape[0]
    halves = blocks // groups
    pairs = (slots - 1) // halves
    lanes = LANES
    def tap(n1, q):
        row = n1 % 2 * 4 + q
        return taps_ref[n1 // 2, row : row + 1, :]

    unitary = 1.0 / math.sqrt(groups * row_ref.shape[1])

    def block_of(source, h):
        return (source % 2) * (blocks // 2) + (source // 2) * halves + h

    def twist(n1, pair, direction):
        c, s = twist_ref[n1, 0:1, :], twist_ref[n1, 1:2, :]
        if direction < 0:
            return pair[0] * c + pair[1] * s, pair[1] * c - pair[0] * s
        return complex_times(pair[0], pair[1], c, s)

    def put(buf, n1, pair):
        buf[n1 * 8 : n1 * 8 + 8, :lanes] = pair[0]
        buf[n1 * 8 : n1 * 8 + 8, lanes:] = pair[1]

    def take(buf, n1):
        return buf[n1 * 8 : n1 * 8 + 8, :lanes], buf[n1 * 8 : n1 * 8 + 8, lanes:]

    def put_samples(buf, values):
        for n1, pair in enumerate(fft_list(values, 1)):
            put(buf, n1, twist(n1, pair, 1))

    def mix(buf, table_ref):
        buf[...] = right_product(buf[...], table_ref[...])

    energy = jnp.zeros((1, lanes), jnp.float32)
    steps = []
    for source in range(groups):
        step = 1.0 / x_ref[source, halves * pairs].astype(jnp.float32)[3:4]
        steps.append(step)
        reach = CEILING * step
        energy = energy + reach * reach
    gain = jnp.max(taps_ref[...], axis=0)
    gain = jnp.maximum(
        jnp.sum(gain[:4], axis=0, keepdims=True), jnp.sum(gain[4:], axis=0, keepdims=True)
    )
    gain = jnp.max(gain, axis=1, keepdims=True)
    scale = CEILING * lax.rsqrt(energy) / gain
    scale_ref[...] = jnp.broadcast_to(scale, scale_ref.shape)

    values = [None] * blocks
    for source in range(groups):
        tile = x_ref[source, halves * pairs].astype(jnp.float32) * unitary
        for h in range(halves):
            part = tile[h * 8 : h * 8 + 8]
            values[block_of(source, h)] = (part, jnp.concatenate([part[4:], part[:4]], axis=0))
    put_samples(first_buf, values)
    mix(first_buf, inverse_ref)
    for n1 in range(blocks):
        parts = take(first_buf, n1)
        t1, t2, t3 = [tap(n1, q) for q in range(1, 4)]
        rows = []
        for part in parts:
            v0, v1, v2 = part[0:1], part[1:2], part[2:3]
            rows += [t1 * v2 + t2 * v1 + t3 * v0, t2 * v2 + t3 * v1, t3 * v2, v0]
        wrap[n1] = jnp.concatenate(rows, axis=0)

    def one_pair(p, buf):
        first = pl.multiple_of(p * 8, 8)

        def row_table(index):
            return row_ref[2 * index, pl.ds(first, 8), :], row_ref[2 * index + 1, pl.ds(first, 8), :]

        values = [None] * blocks
        for source in range(groups):
            for h in range(halves):
                tile = restored(x_ref[source, h * pairs + p]) * steps[source]
                values[block_of(source, h)] = (tile[:8], tile[8:])
        put_samples(buf, values)
        yield
        mix(buf, inverse_ref)
        yield
        w1, w2, w3 = row_table(0), row_table(1), row_table(2)
        unit = row_table(3)
        turn = row_table(4)
        for n1 in range(blocks):
            re, im = take(buf, n1)
            t = [tap(n1, q) for q in range(4)]
            gain_re = t[0] + w1[0] * t[1] + w2[0] * t[2] + w3[0] * t[3]
            gain_im = w1[1] * t[1] + w2[1] * t[2] + w3[1] * t[3]
            u = [wrap[n1, q : q + 1, :] for q in range(7)]
            back_re = u[0] + (w1[0] * u[1] - w1[1] * u[5]) + (w2[0] * u[2] - w2[1] * u[6])
            back_im = u[4] + (w1[0] * u[5] + w1[1] * u[1]) + (w2[0] * u[6] + w2[1] * u[2])
            re, im = complex_times(re, im, gain_re, gain_im)
            put(buf, n1, complex_times(re - back_re, im - back_im, *turn))
            turn = complex_times(*turn, *unit)
        yield
        mix(buf, forward_ref)
        yield
        values = [twist(n1, take(buf, n1), -1) for n1 in range(blocks)]
        bins = []
        for k, pair in enumerate(fft_list(values, -1)):
            c = cos_ref[pl.ds(first, 8), k * lanes : (k + 1) * lanes]
            s = sin_ref[pl.ds(first, 8), k * lanes : (k + 1) * lanes]
            bins.append(complex_times(*pair, c, s))
        put_samples(buf, bins)
        yield
        mix(buf, inverse_ref)
        yield
        turn = row_table(4)
        turn = turn[0] * scale, turn[1] * scale
        for n1 in range(blocks):
            re, im = take(buf, n1)
            back = re * turn[0] + im * turn[1], im * turn[0] - re * turn[1]
            dest = n1 // 2 % (groups // 2) * 2 + n1 % 2
            h = n1 // groups
            out_ref[dest, h * pairs + p] = expanded(jnp.concatenate(back, axis=0))
            turn = complex_times(*turn, *unit)

    def two_pairs(step, carry):
        early = one_pair(2 * step, first_buf)
        late = one_pair(2 * step + 1, second_buf)
        next(early)
        running = True
        while running:
            next(early, None)
            running = next(late, late) is not late
        return carry

    lax.fori_loop(0, pairs // 2, two_pairs, 0)


def columns_kernel(count, x_ref, table_ref, *refs):
    outs, (out_ref, high_ref, low_ref, mid_ref) = refs[:count], refs[count:]
    groups, slots = x_ref.shape[0], x_ref.shape[1]
    time_count, halves, _, fd, _ = out_ref.shape
    me = lax.axis_index("tm")
    pairs = slots // halves
    width = halves * LANES

    def decode(p):
        for source in range(groups):
            for h in range(halves):
                high, low = split_parts(restored(x_ref[source, h * pairs + p]))
                rows = slice(source * 16, source * 16 + 16)
                cols = slice(h * LANES, (h + 1) * LANES)
                high_ref[p, rows, cols] = high
                low_ref[p, rows, cols] = low

    decode(0)
    for p in range(pairs):
        if p + 1 < pairs:
            decode(p + 1)
        mid_ref[2 * p : 2 * p + 2] = left_product(
            table_ref[p], high_ref[p], low_ref[p]
        ).reshape(2, 2 * fd, width)
    for g in range(0, fd, 16):
        for h in range(halves):
            cols = slice(h * LANES, (h + 1) * LANES)
            values = [
                (mid_ref[kd, g : g + 16, cols], mid_ref[kd, fd + g : fd + g + 16, cols])
                for kd in range(time_count)
            ]
            for d, pair in enumerate(fft_list(values, 1)):
                for r in range(2):
                    out_ref[d, h, r, g : g + 16, :] = expanded(pair[r])
    for k in range(count):
        outs[k][...] = out_ref[me ^ k]


def early_kernel(count, *refs):
    parts, out_ref = refs[:count], refs[count]
    halves, _, fd, _ = parts[0].shape
    for i, part in enumerate(parts):
        for h in range(halves):
            out_ref[i * halves + h] = restored(part[h].reshape(2 * fd, LANES)).T


def output_kernel(early, late, *refs):
    turned, parts = refs[0], refs[1 : 1 + len(late)]
    scale_ref, out_ref, mixed, held, sems = refs[1 + len(late) :]
    halves, _, fd, _ = parts[0].shape
    count = len(early) + len(late)
    lots = count * halves
    step = 1.0 / scale_ref[0:1, :]
    me = lax.axis_index("tm")
    for h in range(halves):
        for i, k in enumerate(early):
            rows = pl.ds((me ^ k) + count * h, LANES, stride=lots)
            mixed[rows, :] = turned[i * halves + h] * step
        for i, k in enumerate(late):
            rows = pl.ds((me ^ k) + count * h, LANES, stride=lots)
            mixed[rows, :] = (restored(parts[i][h].reshape(2 * fd, LANES)) * step).T
    wide = held.reshape(2 * fd, lots, LANES)
    copies = []
    for block in range(lots):
        tile = mixed[block * LANES : (block + 1) * LANES, :].T
        held[pl.ds(block, 2 * fd, stride=lots), :] = tile
        if block % STRIDE == STRIDE - 1:
            span = pl.ds(block + 1 - STRIDE, STRIDE)
            copies.append(
                pltpu.make_async_copy(
                    wide.at[:, span, :], out_ref.at[:, span, :], sems.at[block // STRIDE]
                )
            )
            copies[-1].start()
    for copy in copies:
        copy.wait()


def near(x):
    return pltpu.with_memory_space_constraint(x, pltpu.VMEM)


def call(kernel, outs, scratch, *args):
    return pl.pallas_call(
        kernel,
        out_shape=outs,
        in_specs=[pl.BlockSpec(memory_space=pltpu.VMEM)] * len(args),
        out_specs=jax.tree.map(lambda _: pl.BlockSpec(memory_space=pltpu.VMEM), outs),
        scratch_shapes=scratch,
        compiler_params=pltpu.CompilerParams(vmem_limit_bytes=24 << 20),
    )(*[near(x) for x in args])


def swap_parts(parts):
    count = len(parts)
    moved = {0: parts[0]}
    for k in range(count - 1, 0, -1):
        moved[k] = lax.ppermute(parts[k], "tm", [(i, i ^ k) for i in range(count)])
    return [moved[k] for k in range(count)]


def swap_all(x, axes):
    return lax.all_to_all(x, axes, split_axis=0, concat_axis=0, tiled=True)


def row_tables(k1, frames, width):
    series_len = frames * width
    shifts = [1 * k1 % frames, 2 * k1 % frames, 3 * k1 % frames]
    parts = [jnp.broadcast_to(s[:, None] * width, (k1.shape[0], LANES)) for s in shifts]
    parts.append(jnp.broadcast_to(k1[:, None], (k1.shape[0], LANES)))
    blocks = width // LANES
    parts.append(k1[:, None] * (blocks * jnp.arange(LANES, dtype=jnp.int32))[None, :] % series_len)
    angles = jnp.stack(parts).astype(jnp.float32) * (-2.0 * math.pi / series_len)
    return jnp.stack([jnp.cos(angles), jnp.sin(angles)], 1).reshape(10, k1.shape[0], LANES)


def fast_body(channels, synth_taps, chirp_phase):
    _, fd, half = channels.shape
    time_count = lax.axis_size("tm")
    subs = lax.axis_size("sub")
    groups = time_count * subs
    width = half * subs
    frames = fd * time_count
    col_width = half // time_count
    halves = col_width // LANES
    pairs = time_count // 2
    blocks = width // LANES
    per = fd // groups
    own = fd // subs
    time_index = lax.axis_index("tm")
    parity = lax.axis_index("sub")
    f32, bf16 = jnp.float32, jnp.bfloat16
    shape = pltpu.VMEM

    sent = pl.pallas_call(
        functools.partial(columns_apart_kernel, time_count),
        out_shape=[shape((2, fd, col_width), bf16)] * time_count,
        in_specs=[pl.BlockSpec(memory_space=pltpu.HBM)],
        out_specs=[pl.BlockSpec(memory_space=pltpu.VMEM)] * time_count,
        scratch_shapes=[pltpu.SemaphoreType.DMA((time_count,))],
        compiler_params=pltpu.CompilerParams(vmem_limit_bytes=24 << 20),
    )(pltpu.with_memory_space_constraint(channels, pltpu.HBM))
    got = swap_parts(sent)

    theirs = partner(chirp_phase, "sub", 0)
    other_taps = partner(synth_taps, "sub", 0)[:, 0]

    def both(a, b):
        return jnp.where(parity == 0, a, b), jnp.where(parity == 0, b, a)

    phase = call(
        functools.partial(phase_kernel, groups), shape((own, width), f32), [], chirp_phase, theirs
    )
    cos_part, sin_part = jnp.cos(phase), jnp.sin(phase)
    taps = jnp.concatenate(both(synth_taps[:, 0], other_taps), axis=0)
    taps = taps.reshape(-1, LANES, blocks // 2).transpose(2, 0, 1)
    row = jnp.arange(own, dtype=jnp.int32)
    k1 = row // per % 2 + 2 * (row // (2 * per))
    k1 = k1 + time_count * (time_index * (fd // time_count) + parity * per + row % per)
    rows = row_tables(k1, frames, width)

    slots = halves * pairs + 1
    coded = call(
        functools.partial(frames_kernel, time_count),
        shape((groups, slots, 16, LANES), bf16),
        [pltpu.VMEM((time_count, 2, fd, col_width), bf16)] * 3,
        *got,
        jnp.asarray(frame_tables(time_count, fd, groups, True)),
        cos_part,
        sin_part,
        taps,
        rows,
    )
    coded = swap_all(coded, ("tm", "sub"))
    back_table = jnp.asarray(frame_tables(time_count, fd, groups, False))
    coded, scale = call(
        rows_kernel,
        (shape((groups, slots - 1, 16, LANES), bf16), shape((8, LANES), f32)),
        [pltpu.VMEM((blocks * 8, 2 * LANES), f32)] * 2 + [pltpu.VMEM((blocks, 8, LANES), f32)],
        coded,
        cos_part,
        sin_part,
        taps,
        rows,
        jnp.asarray(twist_table(width)),
        jnp.asarray(lane_table(width, 1)),
        jnp.asarray(lane_table(width, -1)),
        back_table,
    )
    coded = swap_all(coded, ("tm", "sub"))
    sent = call(
        functools.partial(columns_kernel, time_count),
        [shape((halves, 2, fd, LANES), bf16)] * time_count,
        [pltpu.VMEM((time_count, halves, 2, fd, LANES), bf16)]
        + [pltpu.VMEM((pairs, 4 * fd, col_width), bf16)] * 2
        + [pltpu.VMEM((time_count, 2 * fd, col_width), f32)],
        coded,
        back_table,
    )
    moved = swap_parts(sent)
    early = [0, *range(time_count - 1, time_count // 2, -1)]
    late = list(range(time_count // 2, 0, -1))
    turned = call(
        functools.partial(early_kernel, len(early)),
        shape((len(early) * halves, LANES, 2 * fd), f32),
        [],
        *[moved[k] for k in early],
    )
    blocks_out = half // LANES
    out = pl.pallas_call(
        functools.partial(output_kernel, early, late),
        out_shape=jax.ShapeDtypeStruct((2 * fd, blocks_out, LANES), f32),
        in_specs=[pl.BlockSpec(memory_space=pltpu.VMEM)] * (len(late) + 2),
        out_specs=pl.BlockSpec(memory_space=pltpu.HBM),
        scratch_shapes=[
            pltpu.VMEM((half, LANES), f32),
            pltpu.VMEM((2 * fd * blocks_out, LANES), f32),
            pltpu.SemaphoreType.DMA((blocks_out // STRIDE,)),
        ],
        compiler_params=pltpu.CompilerParams(vmem_limit_bytes=24 << 20),
    )(near(turned), *[near(moved[k]) for k in late], near(scale))
    return out.reshape(2, fd, 1, half)


def body(channels, synth_taps, chirp_phase):
    _, fd, half = channels.shape
    time_count, subs = lax.axis_size("tm"), lax.axis_size("sub")
    groups = time_count * subs
    fits = (
        subs == 2
        and synth_taps.shape[0] == 4
        and half == time_count * 2 * LANES
        and fd == 4 * groups
        and time_count & (time_count - 1) == 0
        and half == groups * LANES
        and 2 * fd == LANES
    )
    return (fast_body if fits else general_body)(channels, synth_taps, chirp_phase)


def solution(mesh):
    placed = (P(None, ("beam", "tm"), "sub"), P(None, "sub", None), P("tm", "sub"))
    return jax.shard_map(
        body,
        mesh=mesh,
        in_specs=placed,
        out_specs=P(None, ("beam", "tm"), "sub", None),
        check_vma=False,
    )
```
